32 devices in a mesh: brick: 8 (over z, x), region: 4 (over y, core).
Axes of the slice: x: 2, y: 2, z: 4, core: 2. Of those that a mesh axis runs over, the one named last changes fastest.
Arguments:
- segments: float32 [1024, 8, 128], P(('brick', 'region'))
- ship_list: int32 [32, 8, 4], P(('brick', 'region')), may hold values from 0 to 31
- kept_tiles: int32 [32, 64, 2], P(('brick', 'region')), may hold values from 0 to 63
- kept_count: int32 [32], P(('brick', 'region')), may hold values from 1 to 64, as said below
- lent_tiles: int32 [32, 4, 8, 2], P(('brick', 'region')), may hold values from 0 to 63
- lent_count: int32 [8, 4, 4], P('brick'), may hold values from 0 to 8, as said below
Outputs:
- loads: float32 [1024, 6, 128], P(('brick', 'region'))
The draws below stay inside these ranges and needn't reach their ends.
Inputs may be any that keep to these rules, and one draw needn't show every extreme that they name: `kept_count`: in every brick one device has exactly 64 live kept slots. `lent_count`: zero where i equals j; in every brick some entry equals 8.
All inputs are finite; a program needn't handle non-finite values.
Results may differ from the reference program's by a relative error of at most 0.0001.
Values sent between devices are 32-bit elements; how exact they have to be, the bound alone decides.
No kernel may reach another device: no remote copies, remote signals or barrier semaphores. Data moves between devices by JAX's collectives and lax.ppermute only.
A program may use at most 64 MiB of HBM per device.

```python
import jax
import jax.numpy as jnp
from jax import lax

SEG = 128
LEAVES_DEV = 32
GSLOT = 4
KEEP = 64
LEND = 8
LEAVES = 1024
EXT = 64
N_BRICK = 8
N_REGION = 4
DEVICES = 32


def heavy_devices(key):
    return jax.random.randint(jax.random.fold_in(key, 11), (N_BRICK,), 0, N_REGION)


def draw_segments(key, part):
    keys = jax.random.split(key, 6)
    shape = (LEAVES, SEG)
    start = jax.random.uniform(keys[0], (LEAVES, 3, SEG), jnp.float32, 0.0, 1.2)
    modulus = jnp.exp(jax.random.uniform(keys[5], shape, jnp.float32, 0.0, jnp.log(10.0)))
    sign = jnp.where(jax.random.uniform(keys[1], shape, jnp.float32) < 0.5, 1.0, -1.0)
    along = sign * jax.random.uniform(keys[2], shape, jnp.float32, 0.25, 0.5)
    across = jax.random.uniform(keys[3], (LEAVES, 2, SEG), jnp.float32, -0.3, 0.3)
    radius = jax.random.uniform(keys[4], shape, jnp.float32, 0.06, 0.14)
    rows = [start, along[:, None, :], across, radius[:, None, :], modulus[:, None, :]]
    return jnp.concatenate(rows, axis=1).astype(jnp.float32)


def draw_kept_count(key, part):
    heavy = heavy_devices(key)
    counts = jax.random.randint(jax.random.fold_in(key, 12), (DEVICES,), 1, KEEP // 2 + 1)
    devices = jnp.arange(DEVICES)
    return jnp.where(devices % N_REGION == heavy[devices // N_REGION], KEEP, counts).astype(jnp.int32)


def draw_lent_count(key, part):
    heavy = heavy_devices(key)
    counts = jax.random.randint(jax.random.fold_in(key, 13), (N_BRICK, N_REGION, N_REGION), 0, LEND + 1)
    source = jnp.arange(N_REGION)[None, :, None]
    target = jnp.arange(N_REGION)[None, None, :]
    counts = jnp.where(source == target, 0, counts)
    chosen = (source == heavy[:, None, None]) & (target == (heavy[:, None, None] + 1) % N_REGION)
    return jnp.where(chosen, LEND, counts).astype(jnp.int32)


def plant(entries, stream_key, smallest, top_value):
    place = [jax.random.randint(jax.random.fold_in(stream_key, axis), (), 0, length) for axis, length in enumerate(entries.shape)]
    widest = entries.shape.index(max(entries.shape))
    next_to = place[:widest] + [(place[widest] + 1) % entries.shape[widest]] + place[widest + 1:]
    return entries.at[tuple(place)].set(smallest).at[tuple(next_to)].set(top_value)


def setup_inputs(seed: int = 0) -> dict:
    key_list = jax.random.split(jax.random.key(seed), 7)
    segments = draw_segments(jax.random.fold_in(key_list[6], 71), 0)
    ship_list = plant(jax.random.randint(key_list[1], (DEVICES, N_BRICK, GSLOT), 0, LEAVES_DEV), jax.random.fold_in(key_list[1], 1), 0, LEAVES_DEV - 1).astype(jnp.int32)
    kept_tiles = plant(jax.random.randint(key_list[2], (DEVICES, KEEP, 2), 0, EXT), jax.random.fold_in(key_list[2], 1), 0, EXT - 1).astype(jnp.int32)
    kept_count = draw_kept_count(jax.random.fold_in(key_list[6], 71), 0)
    lent_tiles = plant(jax.random.randint(key_list[4], (DEVICES, N_REGION, LEND, 2), 0, EXT), jax.random.fold_in(key_list[4], 1), 0, EXT - 1).astype(jnp.int32)
    lent_count = draw_lent_count(jax.random.fold_in(key_list[6], 71), 0)
    return dict(segments=segments, ship_list=ship_list, kept_tiles=kept_tiles, kept_count=kept_count, lent_tiles=lent_tiles, lent_count=lent_count)


DIST_FLOOR = 0.0025
PARALLEL_FLOOR = 0.05
REF_GROUP = 64

def cross_rows(lever, force):
    return jnp.stack([lever[:, 1] * force[:, 2] - lever[:, 2] * force[:, 1], lever[:, 2] * force[:, 0] - lever[:, 0] * force[:, 2], lever[:, 0] * force[:, 1] - lever[:, 1] * force[:, 0]], axis=1)

def pair_forces(left, right):
    start_a = left[:, 0:3, :, None]
    axis_a = left[:, 3:6, :, None]
    radius_a = left[:, 6, :, None]
    modulus_a = left[:, 7, :, None]
    start_b = right[:, 0:3, None, :]
    axis_b = right[:, 3:6, None, :]
    radius_b = right[:, 6, None, :]
    modulus_b = right[:, 7, None, :]
    offset = start_a - start_b
    len_a = lax.optimization_barrier(jnp.sum(axis_a * axis_a, axis=1))
    len_b = lax.optimization_barrier(jnp.sum(axis_b * axis_b, axis=1))
    cosine = lax.optimization_barrier(jnp.sum(axis_a * axis_b, axis=1))
    proj_a = lax.optimization_barrier(jnp.sum(axis_a * offset, axis=1))
    proj_b = lax.optimization_barrier(jnp.sum(axis_b * offset, axis=1))
    denom = jnp.maximum(len_a * len_b - cosine * cosine, PARALLEL_FLOOR * len_a * len_b)
    param_a = jnp.clip((cosine * proj_b - proj_a * len_b) / denom, 0.0, 1.0)
    param_b = jnp.clip((cosine * param_a + proj_b) / len_b, 0.0, 1.0)
    param_a = jnp.clip((cosine * param_b - proj_a) / len_a, 0.0, 1.0)
    gap = offset + param_a[:, None] * axis_a - param_b[:, None] * axis_b
    dist = jnp.sqrt(jnp.maximum(lax.optimization_barrier(jnp.sum(gap * gap, axis=1)), DIST_FLOOR))
    depth = jnp.maximum(radius_a + radius_b - dist, 0.0)
    stiff = 4.0 / 3.0 * modulus_a * modulus_b / (modulus_a + modulus_b) * jnp.sqrt(radius_a * radius_b / (radius_a + radius_b))
    scale = stiff * depth * jnp.sqrt(depth) / dist
    force = scale[:, None] * gap
    torque_a = cross_rows((param_a - 0.5)[:, None] * axis_a, force)
    torque_b = cross_rows((param_b - 0.5)[:, None] * axis_b, -force)
    on_a = jnp.concatenate([lax.optimization_barrier(jnp.sum(force, axis=3)), lax.optimization_barrier(jnp.sum(torque_a, axis=3))], axis=1)
    on_b = jnp.concatenate([-lax.optimization_barrier(jnp.sum(force, axis=2)), lax.optimization_barrier(jnp.sum(torque_b, axis=2))], axis=1)
    return (on_a, on_b)

def reference(segments, ship_list, kept_tiles, kept_count, lent_tiles, lent_count):
    devices = jnp.arange(DEVICES).astype(jnp.int32)

    def to_global(ext, owner):
        ghost = jnp.maximum(ext - LEAVES_DEV, 0)
        source = ghost // GSLOT * N_REGION + owner % N_REGION
        leaf = ship_list[source, owner // N_REGION, ghost % GSLOT]
        return jnp.where(ext < LEAVES_DEV, owner * LEAVES_DEV + ext, source * LEAVES_DEV + leaf).astype(jnp.int32)
    kept_owner = devices[:, None]
    kept_a = to_global(kept_tiles[:, :, 0], kept_owner)
    kept_b = to_global(kept_tiles[:, :, 1], kept_owner)
    kept_live = jnp.arange(KEEP).astype(jnp.int32)[None, :] < kept_count[:, None]
    lent_owner = devices[:, None, None]
    lent_a = to_global(lent_tiles[..., 0], lent_owner)
    lent_b = to_global(lent_tiles[..., 1], lent_owner)
    plan = lent_count[devices // N_REGION, devices % N_REGION]
    lent_live = jnp.arange(LEND).astype(jnp.int32)[None, None, :] < plan[:, :, None]
    first = jnp.concatenate([kept_a.reshape(-1), lent_a.reshape(-1)])
    second = jnp.concatenate([kept_b.reshape(-1), lent_b.reshape(-1)])
    live = jnp.concatenate([kept_live.reshape(-1), lent_live.reshape(-1)])
    extra = -first.shape[0] % REF_GROUP
    first = jnp.pad(first, (0, extra)).reshape(-1, REF_GROUP)
    second = jnp.pad(second, (0, extra)).reshape(-1, REF_GROUP)
    live = jnp.pad(live, (0, extra)).reshape(-1, REF_GROUP)

    def group_step(acc, item):
        group_a, group_b, group_live = item
        on_a, on_b = pair_forces(segments[group_a], segments[group_b])
        keep = group_live[:, None, None]
        acc = acc.at[group_a].add(jnp.where(keep, on_a, 0.0))
        acc = acc.at[group_b].add(jnp.where(keep, on_b, 0.0))
        return (acc, None)
    zeros = jnp.zeros((LEAVES, 6, SEG), jnp.float32)
    loads, _ = lax.scan(group_step, zeros, (first, second, live))
    return loads
```

```python
import jax
import jax.numpy as jnp
from jax import lax
from jax.experimental import pallas as pl
from jax.experimental.pallas import tpu as pltpu
from jax.sharding import PartitionSpec as P

DIST_FLOOR = 0.0025
PARALLEL_FLOOR = 0.05
TINY = 1e-20
FEATS = 16
UNROLL = 2
SHIFT = 10


def gather_kernel(ship_ref, seg_ref, out_ref):
    slots, bricks = ship_ref.shape[1:]
    for q in range(bricks):
        for k in range(slots):
            out_ref[q, k] = seg_ref[ship_ref[0, k, q]]


def write_features(src, feat, first, blocks):
    for c in range(0, blocks, 8):
        rows = [src[c : c + 8, q, :] for q in range(8)]
        squared = rows[3] * rows[3] + rows[4] * rows[4] + rows[5] * rows[5]
        inverse = lax.rsqrt(squared)
        values = rows[0:3] + [rows[q] * inverse for q in (3, 4, 5)]
        values += [squared * inverse, rows[6], 0.75 / rows[7], 1.0 / rows[6]]
        for q, value in enumerate(values):
            feat[first + c : first + c + 8, q, :] = value


def pair_tile(feat, part, ia, ib, slot):
    column = jnp.transpose(feat[ia])
    px2, py2, pz2, ux2, uy2, uz2, len2, rad2, eps2, kap2 = (
        jnp.broadcast_to(feat[ib, q : q + 1, :], (8, 128)) for q in range(10)
    )
    sums = None
    for g in range(16):
        piece = column[8 * g : 8 * g + 8, :]
        px1, py1, pz1, ux1, uy1, uz1, len1, rad1, eps1, kap1 = (
            jnp.broadcast_to(piece[:, q : q + 1], (8, 128)) for q in range(10)
        )
        ox, oy, oz = px1 - px2, py1 - py2, pz1 - pz2
        c = ux1 * ox + uy1 * oy + uz1 * oz
        f = ux2 * ox + uy2 * oy + uz2 * oz
        w = ux1 * ux2 + uy1 * uy2 + uz1 * uz2
        inverse = pl.reciprocal(jnp.maximum(1.0 - w * w, PARALLEL_FLOOR))
        s = jnp.minimum(jnp.maximum((w * f - c) * inverse, 0.0), len1)
        t = jnp.minimum(jnp.maximum(w * s + f, 0.0), len2)
        s = jnp.minimum(jnp.maximum(w * t - c, 0.0), len1)
        gx = ox + s * ux1 - t * ux2
        gy = oy + s * uy1 - t * uy2
        gz = oz + s * uz1 - t * uz2
        square = jnp.maximum(gx * gx + gy * gy + gz * gz, DIST_FLOOR)
        nearness = lax.rsqrt(square)
        depth = jnp.maximum(rad1 + rad2 - square * nearness, TINY)
        root = lax.rsqrt(depth * (kap1 + kap2))
        stiff = pl.reciprocal(eps1 + eps2)
        scale = (depth * root) * (depth * nearness) * stiff
        force = [scale * gx, scale * gy, scale * gz]
        on_a = force + [s * v for v in force]
        on_b = force + [t * v for v in force]
        for q in range(6):
            part[slot, 8 * g : 8 * g + 8, q : q + 1] = jnp.sum(on_a[q], axis=1, keepdims=True)
        sums = on_b if sums is None else [x + y for x, y in zip(sums, on_b)]
    rows_b = jnp.concatenate([jnp.sum(x, axis=0, keepdims=True) for x in sums] + [jnp.zeros((2, 128), jnp.float32)], axis=0)
    return rows_b


def run_tiles(feat, part, acc, tiles, first, count):
    def step(n, carry):
        pairs = []
        for u in range(UNROLL):
            code = tiles[first + n * UNROLL + u]
            pairs.append((lax.shift_right_logical(code, SHIFT), code & ((1 << SHIFT) - 1)))
        rows = [pair_tile(feat, part, ia, ib, u) for u, (ia, ib) in enumerate(pairs)]
        for u, (ia, ib) in enumerate(pairs):
            acc[ia] += jnp.transpose(part[u])[0:8, :]
            acc[ib] -= rows[u]
        return carry

    lax.fori_loop(0, (count + UNROLL - 1) // UNROLL, step, 0)


def local_kernel(ship_ref, kept_ref, count_ref, lent_ref, plan_ref, seg_ref, acc_ref, list_ref, total_ref, feat, part, tiles):
    leaves = seg_ref.shape[0]
    slots, bricks = ship_ref.shape[1:]
    ext = leaves + slots * bricks
    peers, _, lend = lent_ref.shape[1:]
    brick = lax.axis_index("brick")
    region = lax.axis_index("region")
    write_features(seg_ref, feat, 0, leaves)
    acc_ref[...] = jnp.zeros_like(acc_ref)
    part[...] = jnp.zeros_like(part)
    mine = leaves + brick * slots

    def local_id(e):
        ghost = e - mine
        is_mine = (ghost >= 0) & (ghost < slots)
        return jnp.where(is_mine, ship_ref[0, jnp.where(is_mine, ghost, 0), brick], e)

    def file_tile(a, b, carry):
        near, far = carry
        a, b = local_id(a), local_id(b)
        code = lax.shift_left(a, SHIFT) | b
        is_near = (a < leaves) & (b < leaves)

        @pl.when(is_near)
        def _():
            tiles[near] = code

        @pl.when(jnp.logical_not(is_near))
        def _():
            list_ref[far] = code

        step = is_near.astype(jnp.int32)
        return near + step, far + 1 - step

    carry = lax.fori_loop(0, count_ref[0], lambda k, c: file_tile(kept_ref[0, 0, k], kept_ref[0, 1, k], c), (0, 0))
    for j in range(peers):
        carry = lax.fori_loop(
            0, plan_ref[0, region, j], lambda k, c: file_tile(lent_ref[0, j, 0, k], lent_ref[0, j, 1, k], c), carry
        )
    near, far = carry
    for u in range(UNROLL - 1):
        tiles[near + u] = (leaves << SHIFT) | leaves
        list_ref[far + u] = (ext << SHIFT) | ext
    total_ref[0] = far
    run_tiles(feat, part, acc_ref, tiles, 0, near)


def far_kernel(list_ref, total_ref, seg_ref, ghost_ref, near_ref, own_ref, back_ref, feat, part, acc):
    leaves = seg_ref.shape[0]
    ghosts = ghost_ref.shape[0]
    write_features(seg_ref, feat, 0, leaves)
    write_features(ghost_ref, feat, leaves, ghosts)
    acc[0:leaves] = near_ref[0:leaves]
    acc[leaves:] = jnp.zeros_like(acc[leaves:])
    part[...] = jnp.zeros_like(part)
    run_tiles(feat, part, acc, list_ref, 0, total_ref[0])
    own_ref[...] = acc[0:leaves]
    back_ref[...] = acc[leaves : leaves + ghosts, 0:6, :]


def finish_kernel(ship_ref, seg_ref, own_ref, back_ref, out_ref, acc):
    leaves = seg_ref.shape[0]
    slots, bricks = ship_ref.shape[1:]
    acc[...] = own_ref[...]
    for q in range(bricks):
        for k in range(slots):
            acc[ship_ref[0, k, q], 0:6, :] += back_ref[q, k]
    for c in range(0, leaves, 8):
        d = [seg_ref[c : c + 8, 3 + q, :] for q in range(3)]
        force = [acc[c : c + 8, q, :] for q in range(3)]
        lever = [acc[c : c + 8, 3 + q, :] for q in range(3)]
        squared = d[0] * d[0] + d[1] * d[1] + d[2] * d[2]
        inverse = lax.rsqrt(squared)
        half = 0.5 * squared * inverse
        u = [x * inverse for x in d]
        m = [x - half * y for x, y in zip(lever, force)]
        for q in range(3):
            out_ref[c : c + 8, q, :] = force[q]
            out_ref[c : c + 8, 3 + q, :] = u[(q + 1) % 3] * m[(q + 2) % 3] - u[(q + 2) % 3] * m[(q + 1) % 3]


def body(segments, ship_list, kept_tiles, kept_count, lent_tiles, lent_count):
    leaves = segments.shape[0]
    bricks, slots = ship_list.shape[1:]
    keep = kept_tiles.shape[1]
    peers, lend = lent_tiles.shape[1:3]
    ghosts = bricks * slots
    ext = leaves + ghosts
    cap = keep + peers * lend + 8
    ship = jnp.transpose(ship_list, (0, 2, 1))
    kept = jnp.transpose(kept_tiles, (0, 2, 1))
    lent = jnp.transpose(lent_tiles, (0, 1, 3, 2))
    smem = pl.BlockSpec(memory_space=pltpu.SMEM)
    vmem = pl.BlockSpec(memory_space=pltpu.VMEM)
    f32 = jnp.float32
    outgoing = pl.pallas_call(
        gather_kernel,
        out_shape=jax.ShapeDtypeStruct((bricks, slots, 8, 128), f32),
        in_specs=[smem, vmem],
        out_specs=vmem,
        name="ship_gather",
    )(ship, segments)
    incoming = lax.all_to_all(outgoing, "brick", split_axis=0, concat_axis=0, tiled=True)
    near_acc, far_list, far_total = pl.pallas_call(
        local_kernel,
        out_shape=[
            jax.ShapeDtypeStruct((leaves + 1, 8, 128), f32),
            jax.ShapeDtypeStruct((cap,), jnp.int32),
            jax.ShapeDtypeStruct((1,), jnp.int32),
        ],
        in_specs=[smem, smem, smem, smem, smem, vmem],
        out_specs=[vmem, smem, smem],
        scratch_shapes=[
            pltpu.VMEM((leaves + 1, FEATS, 128), f32),
            pltpu.VMEM((UNROLL, 128, 128), f32),
            pltpu.SMEM((cap,), jnp.int32),
        ],
        name="near_tiles",
    )(ship, kept, kept_count, lent, lent_count, segments)
    own, back = pl.pallas_call(
        far_kernel,
        out_shape=[jax.ShapeDtypeStruct((leaves, 8, 128), f32), jax.ShapeDtypeStruct((ghosts, 6, 128), f32)],
        in_specs=[smem, smem, vmem, vmem, vmem],
        out_specs=[vmem, vmem],
        scratch_shapes=[
            pltpu.VMEM((ext + 1, FEATS, 128), f32),
            pltpu.VMEM((UNROLL, 128, 128), f32),
            pltpu.VMEM((ext + 1, 8, 128), f32),
        ],
        name="far_tiles",
    )(far_list, far_total, segments, incoming.reshape(ghosts, 8, 128), near_acc)
    returned = lax.all_to_all(back.reshape(bricks, slots, 6, 128), "brick", split_axis=0, concat_axis=0, tiled=True)
    return pl.pallas_call(
        finish_kernel,
        out_shape=jax.ShapeDtypeStruct((leaves, 6, 128), f32),
        in_specs=[smem, vmem, vmem, vmem],
        out_specs=vmem,
        scratch_shapes=[pltpu.VMEM((leaves, 8, 128), f32)],
        name="finish",
    )(ship, segments, own, returned)


def solution(mesh):
    placed = (
        P(("brick", "region"), None, None),
        P(("brick", "region"), None, None),
        P(("brick", "region"), None, None),
        P(("brick", "region")),
        P(("brick", "region"), None, None, None),
        P("brick", None, None),
    )
    return jax.shard_map(
        body,
        mesh=mesh,
        in_specs=placed,
        out_specs=P(("brick", "region"), None, None),
        check_vma=False,
    )
```

```python
import jax
import jax.numpy as jnp
from jax import lax
from jax.experimental import pallas as pl
from jax.experimental.pallas import tpu as pltpu
from jax.sharding import PartitionSpec as P

DIST_FLOOR = 0.0025
PARALLEL_FLOOR = 0.05
TINY = 1e-20
STAND_IN = 1e-30
SHIFT = 10
F32 = jnp.float32

XPART = (0, 0, 0, 1, 1, 2)
YPART = (0, 1, 2, 0, 1, 0)
WHOLE = (0, 3, 5)

DIR_ROW, START_ROW, SINGLE_ROW, ONE_ROW, LEFT_ROWS = 0, 24, 48, 64, 72
RIGHT_ROWS = 80
FEAT_ROWS = 8
OUTS = 13


def parts(x):
    first = x.astype(jnp.bfloat16).astype(F32)
    rest = x - first
    second = rest.astype(jnp.bfloat16).astype(F32)
    return first, second, rest - second


def stride_rows(first, count, row, stride):
    return pl.ds(first * stride + row, count, stride=stride)


def write_blocks(src, feat, left, right, first, blocks):
    one = jnp.ones((8, 128), F32)
    zero = jnp.zeros((8, 128), F32)
    for c in range(0, blocks, 8):

        def put(ref, row, stride, value):
            ref[stride_rows(first + c, 8, row, stride), :] = value

        rows = [src[stride_rows(c, 8, q, 8), :] for q in range(8)]
        squared = rows[3] * rows[3] + rows[4] * rows[4] + rows[5] * rows[5]
        inverse = lax.rsqrt(squared)
        start = rows[0:3]
        unit = [x * inverse for x in rows[3:6]]
        length = squared * inverse
        along = unit[0] * start[0] + unit[1] * start[1] + unit[2] * start[2]
        compliance = 0.75 / jnp.where(rows[7] == 0.0, STAND_IN, rows[7])
        curvature = 1.0 / jnp.where(rows[6] == 0.0, STAND_IN, rows[6])
        for k in range(3):
            put(feat, k, FEAT_ROWS, unit[k])
        put(feat, 3, FEAT_ROWS, length)
        unit_parts = [parts(x) for x in unit]
        start_parts = [parts(x) for x in start]
        for k in range(3):
            for m in range(6):
                put(left, DIR_ROW + 6 * k + m, LEFT_ROWS, unit_parts[k][XPART[m]])
                put(left, START_ROW + 6 * k + m, LEFT_ROWS, start_parts[k][XPART[m]])
                put(right, 6 * k + m, RIGHT_ROWS, unit_parts[k][YPART[m]])
                put(right, 24 + 6 * k + m, RIGHT_ROWS, -start_parts[k][YPART[m]])
        for r in (*range(18, 24), *range(42, 48), 63):
            put(left, r, LEFT_ROWS, zero)
        for r in range(8):
            put(left, ONE_ROW + r, LEFT_ROWS, one)
        singles = [parts(x) for x in (along, rows[6], compliance, curvature, length)]
        for n, single in enumerate(singles):
            for m in range(3):
                put(left, SINGLE_ROW + 3 * n + m, LEFT_ROWS, single[m])
        for m in range(3):
            put(right, 48 + m, RIGHT_ROWS, -singles[0][m])
            put(right, 51 + m, RIGHT_ROWS, -start_parts[0][m])
            put(right, 56 + m, RIGHT_ROWS, -start_parts[1][m])
            put(right, 59 + m, RIGHT_ROWS, -start_parts[2][m])
            put(right, 64 + m, RIGHT_ROWS, singles[1][m])
            put(right, 67 + m, RIGHT_ROWS, singles[2][m])
            put(right, 72 + m, RIGHT_ROWS, singles[3][m])


def write_template(rhs):
    row = lax.broadcasted_iota(jnp.int32, (LEFT_ROWS, 128), 0)
    picks = [[], range(SINGLE_ROW, SINGLE_ROW + 3), []]
    picks += [[START_ROW + 6 * k + m for m in WHOLE] for k in range(3)]
    picks += [range(SINGLE_ROW + 3 * n, SINGLE_ROW + 3 * n + 3) for n in (1, 2, 3)]
    picks += [[DIR_ROW + 6 * k + m for m in WHOLE] for k in range(3)]
    picks += [range(SINGLE_ROW + 12, SINGLE_ROW + 15)]
    for n, chosen in enumerate(picks):
        hit = jnp.zeros((LEFT_ROWS, 128), jnp.bool_)
        for r in chosen:
            hit = hit | (row == r)
        rhs[:, 128 * n : 128 * (n + 1)] = jnp.where(hit, 1.0, 0.0).astype(F32)


def products(left, right, rhs, prod, ia, ib):
    base = pl.multiple_of(ib * RIGHT_ROWS, 8)

    def put(row, out, source, count):
        rhs[row : row + count, 128 * out : 128 * (out + 1)] = right[pl.ds(base + source, count), :]

    put(DIR_ROW, 0, 0, 18)
    put(DIR_ROW, 1, 24, 18)
    put(START_ROW, 2, 0, 18)
    for out, source in ((2, 48), (3, 51), (4, 56), (5, 59), (6, 64), (7, 67), (8, 72)):
        put(ONE_ROW + source % 8, out, source, 3)
    a = left[pl.ds(pl.multiple_of(ia * LEFT_ROWS, 8), LEFT_ROWS), :]
    prod[...] = lax.dot_general(
        a.astype(jnp.bfloat16),
        rhs[...].astype(jnp.bfloat16),
        (((0,), (0,)), ((), ())),
        preferred_element_type=F32,
    )


def pair_sums(feat, prod, part, ib):
    ux2, uy2, uz2, len2 = (jnp.broadcast_to(feat[pl.ds(ib * FEAT_ROWS + q, 1), :], (8, 128)) for q in range(4))
    sums = None
    for g in range(16):
        rows = slice(8 * g, 8 * g + 8)
        w, c, f, ox, oy, oz, reach, compliance, curvature, ux1, uy1, uz1, len1 = (
            prod[rows, 128 * n : 128 * (n + 1)] for n in range(OUTS)
        )
        inverse = pl.reciprocal(jnp.maximum(1.0 - w * w, PARALLEL_FLOOR))
        s = jnp.minimum(jnp.maximum((w * f - c) * inverse, 0.0), len1)
        t = jnp.minimum(jnp.maximum(w * s + f, 0.0), len2)
        s = jnp.minimum(jnp.maximum(w * t - c, 0.0), len1)
        gx = ox + s * ux1 - t * ux2
        gy = oy + s * uy1 - t * uy2
        gz = oz + s * uz1 - t * uz2
        square = jnp.maximum(gx * gx + gy * gy + gz * gz, DIST_FLOOR)
        near = lax.rsqrt(square)
        depth = jnp.maximum(reach - square * near, TINY)
        root = lax.rsqrt(depth * curvature)
        scale = (depth * root) * (depth * near) * pl.reciprocal(compliance)
        force = [scale * gx, scale * gy, scale * gz]
        on_a = force + [s * x for x in force]
        on_b = force + [t * x for x in force]
        for q in range(6):
            part[rows, q : q + 1] = jnp.sum(on_a[q], axis=1, keepdims=True)
        sums = on_b if sums is None else [x + y for x, y in zip(sums, on_b)]
    return jnp.concatenate([jnp.sum(x, axis=0, keepdims=True) for x in sums] + [jnp.zeros((2, 128), F32)], axis=0)


def tile_scratch(blocks):
    return [
        pltpu.VMEM((blocks * FEAT_ROWS, 128), F32),
        pltpu.VMEM((blocks * LEFT_ROWS, 128), F32),
        pltpu.VMEM((blocks * RIGHT_ROWS, 128), F32),
        *[pltpu.VMEM((LEFT_ROWS, OUTS * 128), F32)] * 2,
        *[pltpu.VMEM((128, OUTS * 128), F32)] * 2,
        *[pltpu.VMEM((128, 128), F32)] * 2,
    ]


def run_tiles(scratch, acc, tiles, count):
    feat, left, right, rhs0, rhs1, prod0, prod1, part0, part1 = scratch
    for rhs in (rhs0, rhs1):
        write_template(rhs)
    for part in (part0, part1):
        part[...] = jnp.zeros_like(part)

    def ids(n):
        code = tiles[n]
        return lax.shift_right_logical(code, SHIFT), code & ((1 << SHIFT) - 1)

    def finish(pair, part, on_b):
        ia, ib = pair
        acc[pl.ds(pl.multiple_of(ia * 8, 8), 8), :] += jnp.transpose(part[...])[0:8, :]
        acc[pl.ds(pl.multiple_of(ib * 8, 8), 8), :] -= on_b

    products(left, right, rhs0, prod0, *ids(0))

    def step(n, carry):
        even, odd, following = ids(2 * n), ids(2 * n + 1), ids(2 * n + 2)
        products(left, right, rhs1, prod1, *odd)
        finish(even, part0, pair_sums(feat, prod0, part0, even[1]))
        products(left, right, rhs0, prod0, *following)
        finish(odd, part1, pair_sums(feat, prod1, part1, odd[1]))
        return carry

    lax.fori_loop(0, (count + 1) // 2, step, 0)


def gather_kernel(ship_ref, seg_ref, out_ref):
    slots, bricks = ship_ref.shape[1:]
    for q in range(bricks):
        for k in range(slots):
            out_ref[q, 8 * k : 8 * k + 8, :] = seg_ref[pl.ds(pl.multiple_of(ship_ref[0, k, q] * 8, 8), 8), :]


def near_kernel(ship_ref, kept_ref, count_ref, lent_ref, plan_ref, seg_ref, acc_ref, list_ref, total_ref, tiles, *scratch):
    leaves = seg_ref.shape[0] // 8
    slots, bricks = ship_ref.shape[1:]
    ext = leaves + slots * bricks
    peers = lent_ref.shape[1]
    brick = lax.axis_index("brick")
    region = lax.axis_index("region")
    write_blocks(seg_ref, *scratch[0:3], 0, leaves)
    acc_ref[...] = jnp.zeros_like(acc_ref)
    mine = leaves + brick * slots

    def local_id(e):
        ghost = e - mine
        is_mine = (ghost >= 0) & (ghost < slots)
        return jnp.where(is_mine, ship_ref[0, jnp.where(is_mine, ghost, 0), brick], e)

    def file_tile(a, b, carry):
        near, far = carry
        a, b = local_id(a), local_id(b)
        code = lax.shift_left(a, SHIFT) | b
        is_near = (a < leaves) & (b < leaves)

        @pl.when(is_near)
        def _():
            tiles[near] = code

        @pl.when(jnp.logical_not(is_near))
        def _():
            list_ref[far] = code

        step = is_near.astype(jnp.int32)
        return near + step, far + 1 - step

    carry = lax.fori_loop(0, count_ref[0], lambda k, c: file_tile(kept_ref[0, 0, k], kept_ref[0, 1, k], c), (0, 0))
    for j in range(peers):
        carry = lax.fori_loop(
            0, plan_ref[0, region, j], lambda k, c: file_tile(lent_ref[0, j, 0, k], lent_ref[0, j, 1, k], c), carry
        )
    near, far = carry
    for u in range(2):
        tiles[near + u] = (leaves << SHIFT) | leaves
        list_ref[far + u] = (ext << SHIFT) | ext
    total_ref[0] = far
    run_tiles(scratch, acc_ref, tiles, near)


def far_kernel(list_ref, total_ref, seg_ref, ghost_ref, near_ref, own_ref, back_ref, acc, *scratch):
    own_rows = seg_ref.shape[0]
    leaves = own_rows // 8
    ghosts = ghost_ref.shape[0] // 8
    bricks = back_ref.shape[0]
    slots = ghosts // bricks
    write_blocks(seg_ref, *scratch[0:3], 0, leaves)
    write_blocks(ghost_ref, *scratch[0:3], leaves, ghosts)
    acc[0:own_rows, :] = near_ref[0:own_rows, :]
    acc[own_rows:, :] = jnp.zeros_like(acc[own_rows:, :])
    run_tiles(scratch, acc, list_ref, total_ref[0])
    own_ref[...] = acc[0:own_rows, :]
    for q in range(bricks):
        for k in range(slots):
            row = own_rows + 8 * (q * slots + k)
            back_ref[q, 6 * k : 6 * k + 6, :] = acc[row : row + 6, :]


def finish_kernel(ship_ref, seg_ref, own_ref, back_ref, out_ref, acc):
    leaves = seg_ref.shape[0] // 8
    slots, bricks = ship_ref.shape[1:]
    acc[...] = own_ref[...]
    for q in range(bricks):
        for k in range(slots):
            row = pl.multiple_of(ship_ref[0, k, q] * 8, 8)
            acc[pl.ds(row, 6), :] += back_ref[q, 6 * k : 6 * k + 6, :]
    for c in range(0, leaves, 8):
        d = [seg_ref[stride_rows(c, 8, 3 + q, 8), :] for q in range(3)]
        force = [acc[stride_rows(c, 8, q, 8), :] for q in range(3)]
        lever = [acc[stride_rows(c, 8, 3 + q, 8), :] for q in range(3)]
        squared = d[0] * d[0] + d[1] * d[1] + d[2] * d[2]
        inverse = lax.rsqrt(squared)
        half = 0.5 * squared * inverse
        unit = [x * inverse for x in d]
        m = [x - half * y for x, y in zip(lever, force)]
        for q in range(3):
            i, j = (q + 1) % 3, (q + 2) % 3
            out_ref[q, c : c + 8, :] = force[q]
            out_ref[3 + q, c : c + 8, :] = unit[i] * m[j] - unit[j] * m[i]


def body(segments, ship_list, kept_tiles, kept_count, lent_tiles, lent_count):
    leaves = segments.shape[0]
    bricks, slots = ship_list.shape[1:]
    keep = kept_tiles.shape[1]
    peers, lend = lent_tiles.shape[1:3]
    ghosts = bricks * slots
    ext = leaves + ghosts
    cap = keep + peers * lend + 8
    ship = jnp.transpose(ship_list, (0, 2, 1))
    kept = jnp.transpose(kept_tiles, (0, 2, 1))
    lent = jnp.transpose(lent_tiles, (0, 1, 3, 2))
    flat = segments.reshape(leaves * 8, 128)
    smem = pl.BlockSpec(memory_space=pltpu.SMEM)
    vmem = pl.BlockSpec(memory_space=pltpu.VMEM)
    outgoing = pl.pallas_call(
        gather_kernel,
        out_shape=jax.ShapeDtypeStruct((bricks, slots * 8, 128), F32),
        in_specs=[smem, vmem],
        out_specs=vmem,
        name="ship_gather",
    )(ship, flat)
    incoming = lax.all_to_all(outgoing, "brick", split_axis=0, concat_axis=0, tiled=True)
    near_acc, far_list, far_total = pl.pallas_call(
        near_kernel,
        out_shape=[
            jax.ShapeDtypeStruct(((leaves + 1) * 8, 128), F32),
            jax.ShapeDtypeStruct((cap,), jnp.int32),
            jax.ShapeDtypeStruct((1,), jnp.int32),
        ],
        in_specs=[smem, smem, smem, smem, smem, vmem],
        out_specs=[vmem, smem, smem],
        scratch_shapes=[pltpu.SMEM((cap,), jnp.int32), *tile_scratch(leaves + 1)],
        name="near_tiles",
    )(ship, kept, kept_count, lent, lent_count, flat)
    own, back = pl.pallas_call(
        far_kernel,
        out_shape=[jax.ShapeDtypeStruct((leaves * 8, 128), F32), jax.ShapeDtypeStruct((bricks, slots * 6, 128), F32)],
        in_specs=[smem, smem, vmem, vmem, vmem],
        out_specs=[vmem, vmem],
        scratch_shapes=[pltpu.VMEM(((ext + 1) * 8, 128), F32), *tile_scratch(ext + 1)],
        name="far_tiles",
    )(far_list, far_total, flat, incoming.reshape(ghosts * 8, 128), near_acc)
    returned = lax.all_to_all(back, "brick", split_axis=0, concat_axis=0, tiled=True)
    loads = pl.pallas_call(
        finish_kernel,
        out_shape=jax.ShapeDtypeStruct((6, leaves, 128), F32),
        in_specs=[smem, vmem, vmem, vmem],
        out_specs=vmem,
        scratch_shapes=[pltpu.VMEM((leaves * 8, 128), F32)],
        name="finish",
    )(ship, flat, own, returned)
    return jnp.transpose(loads, (1, 0, 2))


def solution(mesh):
    placed = (
        P(("brick", "region"), None, None),
        P(("brick", "region"), None, None),
        P(("brick", "region"), None, None),
        P(("brick", "region")),
        P(("brick", "region"), None, None, None),
        P("brick", None, None),
    )
    return jax.shard_map(
        body,
        mesh=mesh,
        in_specs=placed,
        out_specs=P(("brick", "region"), None, None),
        check_vma=False,
    )
```

```python
import jax
import jax.numpy as jnp
from jax import lax
from jax.experimental import pallas as pl
from jax.experimental.pallas import tpu as pltpu
from jax.sharding import PartitionSpec as P

DIST_FLOOR = 0.0025
PARALLEL_FLOOR = 0.05
TINY = 1e-20
STAND_IN = 1e-30
SHIFT = 10
F32 = jnp.float32
BF16 = jnp.bfloat16

GROUPS = 12
DEPTH = 8 * GROUPS
RIGHT_ROWS = 8 * (3 * 6 + 7 * 4)
OUTS = 13
PLACES = [{0: 3 * n, 1: 3 * n + 1, 2: 3 * n + 2} for n in range(3)] + [{}, {}, {}, {}, {}, {}]
for _n in range(7):
    PLACES[2 + _n].update({4: 9 + 2 * _n, 5: 10 + 2 * _n})
PLACES += [{}] * 4
BATCH = 4
PREP = 8
EARLY = 8
LATE = 16


def parts(x):
    first = x.astype(BF16).astype(F32)
    rest = x - first
    second = rest.astype(BF16).astype(F32)
    return first, second, rest - second


def write_blocks(src, feat, left, right, first, blocks):
    row = lax.broadcasted_iota(jnp.int32, (8, 128), 0)
    is_dir = (row >= 3) & (row < 6)
    one = jnp.ones((8, 128), F32)
    zero = jnp.zeros((8, 128), F32)

    def pick(mask, x):
        return jnp.where(mask, x, 0.0)

    def total(x):
        return jnp.broadcast_to(jnp.sum(x, axis=0, keepdims=True), (8, 128))

    def spread(x, r):
        return jnp.broadcast_to(x[r : r + 1, :], (8, 128))

    def one_block(n):
        x = src[pl.ds(pl.multiple_of(n * 8, 8), 8), :]
        squared = total(pick(is_dir, x * x))
        inverse = lax.rsqrt(squared)
        pose = jnp.where(is_dir, x * inverse, pick(row < 3, x))
        along = total(pick(is_dir, pose * pltpu.roll(pose, 3, 0)))
        length = squared * inverse
        flipped = 1.0 / jnp.where(x == 0.0, STAND_IN, x)
        single = pick(row == 4, length)
        for r, value in ((3, spread(flipped, 6)), (2, 0.75 * spread(flipped, 7)), (1, spread(x, 6)), (0, along)):
            single = jnp.where(row == r, value, single)
        at = first + n
        feat[pl.ds(pl.multiple_of(at * 8, 8), 8), :] = jnp.where(row == 3, length, pltpu.roll(pose, 5, 0))
        p, q = parts(pose), parts(single)
        stack = jnp.concatenate([p[0], p[0], p[0], p[1], p[1], p[2], *q, one, one, one], axis=0)
        left[pl.ds(pl.multiple_of(at * 128, 128), 128), 0:DEPTH] = jnp.transpose(stack.astype(BF16))
        halves = []
        for three in (
            [pick(is_dir, y) for y in p],
            [pick(is_dir, -pltpu.roll(y, 3, 0)) for y in p],
            [pick(row < 3, pltpu.roll(y, 5, 0)) for y in p],
        ):
            halves += [three[m] for m in (0, 1, 2, 0, 1, 0)]
        for source, r in ((q, 0), (p, 0), (p, 1), (p, 2)):
            halves += [zero] + [pick(row == r, -y) for y in source]
        for r in (1, 2, 3):
            halves += [jnp.where(row == r, 1.0, 0.0)] + [pick(row == r, y) for y in q]
        right[pl.ds(pl.multiple_of(at * RIGHT_ROWS, 16), RIGHT_ROWS), :] = jnp.concatenate(halves, axis=0).astype(BF16)

    def step(n, carry):
        for u in range(PREP):
            one_block(n * PREP + u)
        return carry

    lax.fori_loop(0, blocks // PREP, step, 0)


def write_template(fixed):
    row = lax.broadcasted_iota(jnp.int32, (DEPTH, 128), 0)
    picks = [[], [48, 56, 64], []]
    picks += [[k, 24 + k, 40 + k] for k in range(3)]
    picks += [[48 + n, 56 + n, 64 + n] for n in (1, 2, 3)]
    picks += [[3 + k, 27 + k, 43 + k] for k in range(3)]
    picks += [[52, 60, 68]]
    for n, chosen in enumerate(picks):
        hit = jnp.zeros((DEPTH, 128), jnp.bool_)
        for r in chosen:
            hit = hit | (row == r)
        fixed[:, 128 * n : 128 * (n + 1)] = jnp.where(hit, 1.0, 0.0).astype(BF16)


def products(left, right, fixed, prod, pair):
    ia, ib = pair
    a = left[pl.ds(pl.multiple_of(ia * 128, 128), 128), 0:DEPTH]
    mine = right[pl.ds(pl.multiple_of(ib * RIGHT_ROWS, 16), RIGHT_ROWS), :]

    def column(n):
        places = PLACES[n]
        rows = []
        for k in range(GROUPS // 2):
            if k in places:
                rows.append(mine[16 * places[k] : 16 * places[k] + 16, :])
            else:
                rows.append(fixed[16 * k : 16 * k + 16, 128 * n : 128 * (n + 1)])
        return jnp.concatenate(rows, axis=0)

    for low in range(0, OUTS, 2):
        high = min(low + 2, OUTS)
        b = jnp.concatenate([column(n) for n in range(low, high)], axis=1)
        prod[:, 128 * low : 128 * high] = lax.dot_general(
            a, b, (((1,), (0,)), ((), ())), preferred_element_type=F32
        )


def pair_sums(feat, prod, part, ib):
    ux2, uy2, uz2, len2 = (jnp.broadcast_to(feat[pl.ds(ib * 8 + q, 1), :], (8, 128)) for q in range(4))
    sums = None
    for g in range(16):
        rows = slice(8 * g, 8 * g + 8)
        w, c, f, ox, oy, oz, reach, compliance, curvature, ux1, uy1, uz1, len1 = (
            prod[rows, 128 * n : 128 * (n + 1)] for n in range(OUTS)
        )
        inverse = pl.reciprocal(jnp.maximum(1.0 - w * w, PARALLEL_FLOOR))
        s = jnp.minimum(jnp.maximum((w * f - c) * inverse, 0.0), len1)
        t = jnp.minimum(jnp.maximum(w * s + f, 0.0), len2)
        s = jnp.minimum(jnp.maximum(w * t - c, 0.0), len1)
        gx = ox + s * ux1 - t * ux2
        gy = oy + s * uy1 - t * uy2
        gz = oz + s * uz1 - t * uz2
        square = jnp.maximum(gx * gx + gy * gy + gz * gz, DIST_FLOOR)
        near = lax.rsqrt(square)
        depth = jnp.maximum(reach - square * near, TINY)
        root = lax.rsqrt(depth * curvature)
        scale = (depth * root) * (depth * near) * pl.reciprocal(compliance)
        force = [scale * gx, scale * gy, scale * gz]
        on_a = force + [s * x for x in force]
        on_b = force + [t * x for x in force]
        for q in range(6):
            part[rows, q : q + 1] = jnp.sum(on_a[q], axis=1, keepdims=True)
        sums = on_b if sums is None else [x + y for x, y in zip(sums, on_b)]
    return jnp.concatenate([jnp.sum(x, axis=0, keepdims=True) for x in sums] + [jnp.zeros((2, 128), F32)], axis=0)


def tile_scratch(blocks):
    return [
        pltpu.VMEM((blocks * 8, 128), F32),
        pltpu.VMEM((blocks * 128, 128), BF16),
        pltpu.VMEM((blocks * RIGHT_ROWS, 128), BF16),
        pltpu.VMEM((DEPTH, OUTS * 128), BF16),
        *[pltpu.VMEM((128, OUTS * 128), F32)] * (2 * BATCH),
        *[pltpu.VMEM((128, 128), F32)] * (2 * BATCH),
        *[pltpu.VMEM((8, 128), F32)] * (2 * BATCH),
    ]


def pad_list(tiles, count, dummy):
    for u in range(2 * BATCH):
        tiles[count + u] = (dummy << SHIFT) | dummy


def run_tiles(scratch, acc, tiles, count):
    feat, left, right, fixed = scratch[0:4]
    prods, sums_a, sums_b = (scratch[4 + 2 * BATCH * k : 4 + 2 * BATCH * (k + 1)] for k in range(3))
    write_template(fixed)
    for ref in (*sums_a, *sums_b):
        ref[...] = jnp.zeros_like(ref)

    def ids(n):
        code = tiles[n]
        return lax.shift_right_logical(code, SHIFT), code & ((1 << SHIFT) - 1)

    def collect(first, side):
        for u in range(BATCH):
            ia, ib = ids(jnp.maximum(first + u, 0))
            slot = side * BATCH + u
            acc[pl.ds(pl.multiple_of(ia * 8, 8), 8), :] += jnp.transpose(sums_a[slot][...])[0:8, :]
            acc[pl.ds(pl.multiple_of(ib * 8, 8), 8), :] -= sums_b[slot][...]

    def prepare(first, side):
        for u in range(BATCH):
            products(left, right, fixed, prods[side * BATCH + u], ids(first + u))

    def batch(first, side):
        collect(first - BATCH, 1 - side)
        prepare(first + BATCH, 1 - side)
        for u in range(BATCH):
            slot = side * BATCH + u
            sums_b[slot][...] = pair_sums(feat, prods[slot], sums_a[slot], ids(first + u)[1])

    prepare(0, 0)

    def step(n, carry):
        first = 2 * BATCH * n
        batch(first, 0)

        @pl.when(first + BATCH < count)
        def _():
            batch(first + BATCH, 1)

        return carry

    lax.fori_loop(0, (count + 2 * BATCH - 1) // (2 * BATCH), step, 0)
    batches = (count + BATCH - 1) // BATCH

    @pl.when((batches & 1) == 1)
    def _():
        collect((batches - 1) * BATCH, 0)

    @pl.when((batches > 0) & ((batches & 1) == 0))
    def _():
        collect((batches - 1) * BATCH, 1)


def gather_kernel(ship_ref, seg_ref, out_ref):
    slots, bricks = ship_ref.shape[1:]
    for q in range(bricks):
        for k in range(slots):
            out_ref[q, 8 * k : 8 * k + 8, :] = seg_ref[pl.ds(pl.multiple_of(ship_ref[0, k, q] * 8, 8), 8), :]


def near_kernel(
    ship_ref, kept_ref, count_ref, lent_ref, plan_ref, seg_ref, acc_ref, far_ref, late_ref, total_ref, tiles, *scratch
):
    leaves = seg_ref.shape[0] // 8
    slots, bricks = ship_ref.shape[1:]
    ext = leaves + slots * bricks
    peers = lent_ref.shape[1]
    brick = lax.axis_index("brick")
    region = lax.axis_index("region")
    write_blocks(seg_ref, *scratch[0:3], 0, leaves)
    acc_ref[...] = jnp.zeros_like(acc_ref)
    mine = leaves + brick * slots

    def local_id(e):
        ghost = e - mine
        is_mine = (ghost >= 0) & (ghost < slots)
        return jnp.where(is_mine, ship_ref[0, jnp.where(is_mine, ghost, 0), brick], e)

    def file_tile(a, b, carry):
        near, far = carry
        a, b = local_id(a), local_id(b)
        code = lax.shift_left(a, SHIFT) | b
        is_near = (a < leaves) & (b < leaves)

        @pl.when(is_near)
        def _():
            tiles[near] = code

        @pl.when(jnp.logical_not(is_near))
        def _():
            far_ref[far] = code

        step = is_near.astype(jnp.int32)
        return near + step, far + 1 - step

    carry = lax.fori_loop(
        0, count_ref[0, 0], lambda k, c: file_tile(kept_ref[0, 0, k], kept_ref[0, 1, k], c), (0, 0)
    )
    for j in range(peers):
        carry = lax.fori_loop(
            0, plan_ref[0, region, j], lambda k, c: file_tile(lent_ref[0, j, 0, k], lent_ref[0, j, 1, k], c), carry
        )
    near, far = carry
    early = jnp.minimum(near, EARLY)
    late = jnp.minimum(near - early, LATE)

    def move(target, base):
        def step(k, carry):
            target[base[0] + k] = tiles[base[1] + k]
            return carry

        return step

    lax.fori_loop(0, late, move(late_ref, (0, early)), 0)
    rest = near - early - late
    lax.fori_loop(0, rest, move(far_ref, (far, early + late)), 0)
    pad_list(tiles, early, leaves)
    pad_list(late_ref, late, leaves)
    pad_list(far_ref, far + rest, ext)
    total_ref[0] = far + rest
    total_ref[1] = late
    run_tiles(scratch, acc_ref, tiles, early)


def far_kernel(list_ref, total_ref, seg_ref, ghost_ref, near_ref, own_ref, back_ref, acc, *scratch):
    own_rows = seg_ref.shape[0]
    leaves = own_rows // 8
    ghosts = ghost_ref.shape[0] // 8
    bricks = back_ref.shape[0]
    slots = ghosts // bricks
    write_blocks(seg_ref, *scratch[0:3], 0, leaves)
    write_blocks(ghost_ref, *scratch[0:3], leaves, ghosts)
    acc[0:own_rows, :] = near_ref[0:own_rows, :]
    acc[own_rows:, :] = jnp.zeros_like(acc[own_rows:, :])
    run_tiles(scratch, acc, list_ref, total_ref[0])
    own_ref[...] = acc[0:own_rows, :]
    for q in range(bricks):
        for k in range(slots):
            row = own_rows + 8 * (q * slots + k)
            back_ref[q, 6 * k : 6 * k + 6, :] = acc[row : row + 6, :]


def late_kernel(list_ref, total_ref, seg_ref, far_ref, own_ref, acc, *scratch):
    own_rows = seg_ref.shape[0]
    write_blocks(seg_ref, *scratch[0:3], 0, own_rows // 8)
    acc[0:own_rows, :] = far_ref[...]
    run_tiles(scratch, acc, list_ref, total_ref[1])
    own_ref[...] = acc[0:own_rows, :]


def stride_rows(first, count, row, stride):
    return pl.ds(first * stride + row, count, stride=stride)


def finish_kernel(ship_ref, seg_ref, own_ref, back_ref, out_ref, acc):
    leaves = seg_ref.shape[0] // 8
    slots, bricks = ship_ref.shape[1:]
    acc[...] = own_ref[...]
    for q in range(bricks):
        for k in range(slots):
            row = pl.multiple_of(ship_ref[0, k, q] * 8, 8)
            acc[pl.ds(row, 6), :] += back_ref[q, 6 * k : 6 * k + 6, :]
    for c in range(0, leaves, 8):
        d = [seg_ref[stride_rows(c, 8, 3 + q, 8), :] for q in range(3)]
        force = [acc[stride_rows(c, 8, q, 8), :] for q in range(3)]
        lever = [acc[stride_rows(c, 8, 3 + q, 8), :] for q in range(3)]
        squared = d[0] * d[0] + d[1] * d[1] + d[2] * d[2]
        inverse = lax.rsqrt(squared)
        half = 0.5 * squared * inverse
        unit = [x * inverse for x in d]
        m = [x - half * y for x, y in zip(lever, force)]
        for q in range(3):
            i, j = (q + 1) % 3, (q + 2) % 3
            out_ref[q, c : c + 8, :] = force[q]
            out_ref[3 + q, c : c + 8, :] = unit[i] * m[j] - unit[j] * m[i]


def body(segments, ship_list, kept_tiles, kept_count, lent_tiles, lent_count):
    leaves = segments.shape[0]
    bricks, slots = ship_list.shape[1:]
    keep = kept_tiles.shape[1]
    peers, lend = lent_tiles.shape[1:3]
    ghosts = bricks * slots
    ext = leaves + ghosts
    cap = keep + peers * lend + 2 * BATCH
    ship = jnp.transpose(ship_list, (0, 2, 1))
    kept = jnp.transpose(kept_tiles, (0, 2, 1))
    lent = jnp.transpose(lent_tiles, (0, 1, 3, 2))
    flat = segments.reshape(leaves * 8, 128)
    smem = pl.BlockSpec(memory_space=pltpu.SMEM)
    vmem = pl.BlockSpec(memory_space=pltpu.VMEM)
    tile_list = jax.ShapeDtypeStruct((cap,), jnp.int32)
    own_sums = jax.ShapeDtypeStruct((leaves * 8, 128), F32)
    outgoing = pl.pallas_call(
        gather_kernel,
        out_shape=jax.ShapeDtypeStruct((bricks, slots * 8, 128), F32),
        in_specs=[smem, vmem],
        out_specs=vmem,
        name="ship_gather",
    )(ship, flat)
    incoming = lax.all_to_all(outgoing, "brick", split_axis=0, concat_axis=0, tiled=True)
    near_sums, far_list, late_list, totals = pl.pallas_call(
        near_kernel,
        out_shape=[
            jax.ShapeDtypeStruct(((leaves + 1) * 8, 128), F32),
            tile_list,
            tile_list,
            jax.ShapeDtypeStruct((2,), jnp.int32),
        ],
        in_specs=[smem, smem, smem, smem, smem, vmem],
        out_specs=[vmem, smem, smem, smem],
        scratch_shapes=[pltpu.SMEM((cap,), jnp.int32), *tile_scratch(leaves + 1)],
        name="near_tiles",
    )(ship, kept, kept_count.reshape(1, 1), lent, lent_count, flat)
    far_sums, back = pl.pallas_call(
        far_kernel,
        out_shape=[own_sums, jax.ShapeDtypeStruct((bricks, slots * 6, 128), F32)],
        in_specs=[smem, smem, vmem, vmem, vmem],
        out_specs=[vmem, vmem],
        scratch_shapes=[pltpu.VMEM(((ext + 1) * 8, 128), F32), *tile_scratch(ext + 1)],
        name="far_tiles",
    )(far_list, totals, flat, incoming.reshape(ghosts * 8, 128), near_sums)
    returned = lax.all_to_all(back, "brick", split_axis=0, concat_axis=0, tiled=True)
    own = pl.pallas_call(
        late_kernel,
        out_shape=own_sums,
        in_specs=[smem, smem, vmem, vmem],
        out_specs=vmem,
        scratch_shapes=[pltpu.VMEM(((leaves + 1) * 8, 128), F32), *tile_scratch(leaves + 1)],
        name="late_tiles",
    )(late_list, totals, flat, far_sums)
    loads = pl.pallas_call(
        finish_kernel,
        out_shape=jax.ShapeDtypeStruct((6, leaves, 128), F32),
        in_specs=[smem, vmem, vmem, vmem],
        out_specs=vmem,
        scratch_shapes=[pltpu.VMEM((leaves * 8, 128), F32)],
        name="finish",
    )(ship, flat, own, returned)
    return jnp.transpose(loads, (1, 0, 2))


def solution(mesh):
    placed = (
        P(("brick", "region"), None, None),
        P(("brick", "region"), None, None),
        P(("brick", "region"), None, None),
        P(("brick", "region")),
        P(("brick", "region"), None, None, None),
        P("brick", None, None),
    )
    return jax.shard_map(
        body,
        mesh=mesh,
        in_specs=placed,
        out_specs=P(("brick", "region"), None, None),
        check_vma=False,
    )
```

```python
import jax
import jax.numpy as jnp
from jax import lax
from jax.experimental import pallas as pl
from jax.experimental.pallas import tpu as pltpu
from jax.sharding import PartitionSpec as P

DIST_FLOOR = 0.0025
PARALLEL_FLOOR = 0.05
TINY = 1e-20
STAND_IN = 1e-30
SHIFT = 10
F32 = jnp.float32
BF16 = jnp.bfloat16

GROUPS = 12
DEPTH = 8 * GROUPS
RIGHT_ROWS = 8 * (3 * 6 + 7 * 4)
OUTS = 13
PLACES = [{0: 3 * n, 1: 3 * n + 1, 2: 3 * n + 2} for n in range(3)] + [{}, {}, {}, {}, {}, {}]
for _n in range(7):
    PLACES[2 + _n].update({4: 9 + 2 * _n, 5: 10 + 2 * _n})
PLACES += [{}] * 4
BATCH = 4
PREP = 8
LATE = 12


def parts(x):
    first = x.astype(BF16).astype(F32)
    rest = x - first
    second = rest.astype(BF16).astype(F32)
    return first, second, rest - second


def write_blocks(src, feat, left, right, first, blocks, skip=0):
    row = lax.broadcasted_iota(jnp.int32, (8, 128), 0)
    is_dir = (row >= 3) & (row < 6)
    one = jnp.ones((8, 128), F32)
    zero = jnp.zeros((8, 128), F32)

    def pick(mask, x):
        return jnp.where(mask, x, 0.0)

    def total(x):
        return jnp.broadcast_to(jnp.sum(x, axis=0, keepdims=True), (8, 128))

    def spread(x, r):
        return jnp.broadcast_to(x[r : r + 1, :], (8, 128))

    def one_block(n):
        x = src[pl.ds(pl.multiple_of((skip + n) * 8, 8), 8), :]
        squared = total(pick(is_dir, x * x))
        inverse = lax.rsqrt(squared)
        pose = jnp.where(is_dir, x * inverse, pick(row < 3, x))
        along = total(pick(is_dir, pose * pltpu.roll(pose, 3, 0)))
        length = squared * inverse
        flipped = 1.0 / jnp.where(x == 0.0, STAND_IN, x)
        single = pick(row == 4, length)
        for r, value in ((3, spread(flipped, 6)), (2, 0.75 * spread(flipped, 7)), (1, spread(x, 6)), (0, along)):
            single = jnp.where(row == r, value, single)
        at = first + n
        feat[pl.ds(pl.multiple_of(at * 8, 8), 8), :] = jnp.where(row == 3, length, pltpu.roll(pose, 5, 0))
        p, q = parts(pose), parts(single)
        stack = jnp.concatenate([p[0], p[0], p[0], p[1], p[1], p[2], *q, one, one, one], axis=0)
        left[pl.ds(pl.multiple_of(at * 128, 128), 128), 0:DEPTH] = jnp.transpose(stack.astype(BF16))
        halves = []
        for three in (
            [pick(is_dir, y) for y in p],
            [pick(is_dir, -pltpu.roll(y, 3, 0)) for y in p],
            [pick(row < 3, pltpu.roll(y, 5, 0)) for y in p],
        ):
            halves += [three[m] for m in (0, 1, 2, 0, 1, 0)]
        for source, r in ((q, 0), (p, 0), (p, 1), (p, 2)):
            halves += [zero] + [pick(row == r, -y) for y in source]
        for r in (1, 2, 3):
            halves += [jnp.where(row == r, 1.0, 0.0)] + [pick(row == r, y) for y in q]
        right[pl.ds(pl.multiple_of(at * RIGHT_ROWS, 16), RIGHT_ROWS), :] = jnp.concatenate(halves, axis=0).astype(BF16)

    def step(n, carry):
        for u in range(PREP):
            one_block(n * PREP + u)
        return carry

    lax.fori_loop(0, blocks // PREP, step, 0)


def write_template(fixed):
    row = lax.broadcasted_iota(jnp.int32, (DEPTH, 128), 0)
    picks = [[], [48, 56, 64], []]
    picks += [[k, 24 + k, 40 + k] for k in range(3)]
    picks += [[48 + n, 56 + n, 64 + n] for n in (1, 2, 3)]
    picks += [[3 + k, 27 + k, 43 + k] for k in range(3)]
    picks += [[52, 60, 68]]
    for n, chosen in enumerate(picks):
        hit = jnp.zeros((DEPTH, 128), jnp.bool_)
        for r in chosen:
            hit = hit | (row == r)
        fixed[:, 128 * n : 128 * (n + 1)] = jnp.where(hit, 1.0, 0.0).astype(BF16)


def products(left, right, fixed, prod, pair):
    ia, ib = pair
    a = left[pl.ds(pl.multiple_of(ia * 128, 128), 128), 0:DEPTH]
    mine = right[pl.ds(pl.multiple_of(ib * RIGHT_ROWS, 16), RIGHT_ROWS), :]

    def column(n):
        places = PLACES[n]
        rows = []
        for k in range(GROUPS // 2):
            if k in places:
                rows.append(mine[16 * places[k] : 16 * places[k] + 16, :])
            else:
                rows.append(fixed[16 * k : 16 * k + 16, 128 * n : 128 * (n + 1)])
        return jnp.concatenate(rows, axis=0)

    for low in range(0, OUTS, 2):
        high = min(low + 2, OUTS)
        b = jnp.concatenate([column(n) for n in range(low, high)], axis=1)
        prod[:, 128 * low : 128 * high] = lax.dot_general(
            a, b, (((1,), (0,)), ((), ())), preferred_element_type=F32
        )


def pair_sums(feat, prod, part, ib):
    ux2, uy2, uz2, len2 = (jnp.broadcast_to(feat[pl.ds(ib * 8 + q, 1), :], (8, 128)) for q in range(4))
    sums = None
    for g in range(16):
        rows = slice(8 * g, 8 * g + 8)
        w, c, f, ox, oy, oz, reach, compliance, curvature, ux1, uy1, uz1, len1 = (
            prod[rows, 128 * n : 128 * (n + 1)] for n in range(OUTS)
        )
        inverse = pl.reciprocal(jnp.maximum(1.0 - w * w, PARALLEL_FLOOR))
        s = jnp.minimum(jnp.maximum((w * f - c) * inverse, 0.0), len1)
        t = jnp.minimum(jnp.maximum(w * s + f, 0.0), len2)
        s = jnp.minimum(jnp.maximum(w * t - c, 0.0), len1)
        gx = ox + s * ux1 - t * ux2
        gy = oy + s * uy1 - t * uy2
        gz = oz + s * uz1 - t * uz2
        square = jnp.maximum(gx * gx + gy * gy + gz * gz, DIST_FLOOR)
        near = lax.rsqrt(square)
        depth = jnp.maximum(reach - square * near, TINY)
        root = lax.rsqrt(depth * curvature)
        scale = (depth * root) * (depth * near) * pl.reciprocal(compliance)
        force = [scale * gx, scale * gy, scale * gz]
        on_a = force + [s * x for x in force]
        on_b = force + [t * x for x in force]
        for q in range(6):
            part[rows, q : q + 1] = jnp.sum(on_a[q], axis=1, keepdims=True)
        sums = on_b if sums is None else [x + y for x, y in zip(sums, on_b)]
    return jnp.concatenate([jnp.sum(x, axis=0, keepdims=True) for x in sums] + [jnp.zeros((2, 128), F32)], axis=0)


def block_arrays(blocks):
    return [
        pltpu.VMEM((blocks * 8, 128), F32),
        pltpu.VMEM((blocks * 128, 128), BF16),
        pltpu.VMEM((blocks * RIGHT_ROWS, 128), BF16),
    ]


def tile_scratch():
    return [
        pltpu.VMEM((DEPTH, OUTS * 128), BF16),
        *[pltpu.VMEM((128, OUTS * 128), F32)] * (2 * BATCH),
        *[pltpu.VMEM((128, 128), F32)] * (2 * BATCH),
        *[pltpu.VMEM((8, 128), F32)] * (2 * BATCH),
    ]


def pad_list(tiles, count, dummy):
    for u in range(2 * BATCH):
        tiles[count + u] = (dummy << SHIFT) | dummy


def run_tiles(blocks, scratch, acc, tiles, count):
    feat, left, right = blocks
    fixed = scratch[0]
    prods, sums_a, sums_b = (scratch[1 + 2 * BATCH * k : 1 + 2 * BATCH * (k + 1)] for k in range(3))
    write_template(fixed)
    for ref in (*sums_a, *sums_b):
        ref[...] = jnp.zeros_like(ref)

    def ids(n):
        code = tiles[n]
        return lax.shift_right_logical(code, SHIFT), code & ((1 << SHIFT) - 1)

    def collect(first, side):
        for u in range(BATCH):
            ia, ib = ids(jnp.maximum(first + u, 0))
            slot = side * BATCH + u
            acc[pl.ds(pl.multiple_of(ia * 8, 8), 8), :] += jnp.transpose(sums_a[slot][...])[0:8, :]
            acc[pl.ds(pl.multiple_of(ib * 8, 8), 8), :] -= sums_b[slot][...]

    def prepare(first, side):
        for u in range(BATCH):
            products(left, right, fixed, prods[side * BATCH + u], ids(first + u))

    def batch(first, side):
        collect(first - BATCH, 1 - side)
        prepare(first + BATCH, 1 - side)
        for u in range(BATCH):
            slot = side * BATCH + u
            sums_b[slot][...] = pair_sums(feat, prods[slot], sums_a[slot], ids(first + u)[1])

    prepare(0, 0)

    def step(n, carry):
        first = 2 * BATCH * n
        batch(first, 0)

        @pl.when(first + BATCH < count)
        def _():
            batch(first + BATCH, 1)

        return carry

    lax.fori_loop(0, (count + 2 * BATCH - 1) // (2 * BATCH), step, 0)
    batches = (count + BATCH - 1) // BATCH

    @pl.when((batches & 1) == 1)
    def _():
        collect((batches - 1) * BATCH, 0)

    @pl.when((batches > 0) & ((batches & 1) == 0))
    def _():
        collect((batches - 1) * BATCH, 1)


def gather_kernel(ship_ref, seg_ref, out_ref):
    slots, bricks = ship_ref.shape[1:]
    for q in range(bricks):
        for k in range(slots):
            out_ref[q, 8 * k : 8 * k + 8, :] = seg_ref[pl.ds(pl.multiple_of(ship_ref[0, k, q] * 8, 8), 8), :]


def plan_kernel(
    ship_ref, kept_ref, count_ref, lent_ref, plan_ref, seg_ref, far_ref, late_ref, total_ref, *refs
):
    held, (feat, left, right, tiles, sems) = refs[0:3], refs[3:]
    leaves = seg_ref.shape[0] // 8
    slots, bricks = ship_ref.shape[1:]
    ext = leaves + slots * bricks
    peers = lent_ref.shape[1]
    brick = lax.axis_index("brick")
    region = lax.axis_index("region")
    copies = []
    for c in range(leaves // PREP):
        write_blocks(seg_ref, feat, left, right, PREP * c, PREP, PREP * c)
        for m, (ref, target) in enumerate(zip((feat, left, right), held)):
            size = ref.shape[0] // leaves * PREP
            rows = pl.ds(c * size, size)
            copies.append(pltpu.make_async_copy(ref.at[rows, :], target.at[rows, :], sems.at[c, m]))
            copies[-1].start()
    mine = leaves + brick * slots

    def local_id(e):
        ghost = e - mine
        is_mine = (ghost >= 0) & (ghost < slots)
        return jnp.where(is_mine, ship_ref[0, jnp.where(is_mine, ghost, 0), brick], e)

    def file_tile(a, b, carry):
        near, far = carry
        a, b = local_id(a), local_id(b)
        code = lax.shift_left(a, SHIFT) | b
        is_near = (a < leaves) & (b < leaves)

        @pl.when(is_near)
        def _():
            tiles[near] = code

        @pl.when(jnp.logical_not(is_near))
        def _():
            far_ref[far] = code

        step = is_near.astype(jnp.int32)
        return near + step, far + 1 - step

    carry = lax.fori_loop(
        0, count_ref[0], lambda k, c: file_tile(kept_ref[0, 0, k], kept_ref[0, 1, k], c), (0, 0)
    )
    for j in range(peers):
        carry = lax.fori_loop(
            0, plan_ref[0, region, j], lambda k, c: file_tile(lent_ref[0, j, 0, k], lent_ref[0, j, 1, k], c), carry
        )
    near, far = carry
    late = jnp.minimum(near, LATE)

    def move(target, base):
        def step(k, carry):
            target[base[0] + k] = tiles[base[1] + k]
            return carry

        return step

    lax.fori_loop(0, late, move(late_ref, (0, 0)), 0)
    rest = near - late
    lax.fori_loop(0, rest, move(far_ref, (far, late)), 0)
    pad_list(late_ref, late, leaves)
    pad_list(far_ref, far + rest, ext)
    total_ref[0] = far + rest
    total_ref[1] = late
    for copy in copies:
        copy.wait()


def far_kernel(list_ref, total_ref, ghost_ref, *refs):
    held, own_ref, back_ref, (acc, feat, left, right, sems, *scratch) = refs[0:3], refs[3], refs[4], refs[5:]
    ghosts = ghost_ref.shape[0] // 8
    leaves = own_ref.shape[0] // 8
    bricks = back_ref.shape[0]
    slots = ghosts // bricks
    blocks = (feat, left, right)
    copies = [
        pltpu.make_async_copy(source, ref.at[0 : source.shape[0], :], sems.at[m])
        for m, (source, ref) in enumerate(zip(held, blocks))
    ]
    for copy in copies:
        copy.start()
    acc[...] = jnp.zeros_like(acc)
    write_blocks(ghost_ref, feat, left, right, leaves, ghosts)
    for copy in copies:
        copy.wait()
    run_tiles(blocks, scratch, acc, list_ref, total_ref[0])
    own_ref[...] = acc[0 : leaves * 8, :]
    for q in range(bricks):
        for k in range(slots):
            row = 8 * (leaves + q * slots + k)
            back_ref[q, 6 * k : 6 * k + 6, :] = acc[row : row + 6, :]


def late_kernel(list_ref, total_ref, seg_ref, far_ref, own_ref, acc, feat, left, right, *scratch):
    own_rows = seg_ref.shape[0]
    write_blocks(seg_ref, feat, left, right, 0, own_rows // 8)
    acc[0:own_rows, :] = far_ref[...]
    run_tiles((feat, left, right), scratch, acc, list_ref, total_ref[1])
    own_ref[...] = acc[0:own_rows, :]


def stride_rows(first, count, row, stride):
    return pl.ds(first * stride + row, count, stride=stride)


def finish_kernel(ship_ref, seg_ref, own_ref, back_ref, out_ref, acc):
    leaves = seg_ref.shape[0] // 8
    slots, bricks = ship_ref.shape[1:]
    acc[...] = own_ref[...]
    for q in range(bricks):
        for k in range(slots):
            row = pl.multiple_of(ship_ref[0, k, q] * 8, 8)
            acc[pl.ds(row, 6), :] += back_ref[q, 6 * k : 6 * k + 6, :]
    for c in range(0, leaves, 8):
        d = [seg_ref[stride_rows(c, 8, 3 + q, 8), :] for q in range(3)]
        force = [acc[stride_rows(c, 8, q, 8), :] for q in range(3)]
        lever = [acc[stride_rows(c, 8, 3 + q, 8), :] for q in range(3)]
        squared = d[0] * d[0] + d[1] * d[1] + d[2] * d[2]
        inverse = lax.rsqrt(squared)
        half = 0.5 * squared * inverse
        unit = [x * inverse for x in d]
        m = [x - half * y for x, y in zip(lever, force)]
        for q in range(3):
            i, j = (q + 1) % 3, (q + 2) % 3
            out_ref[q, c : c + 8, :] = force[q]
            out_ref[3 + q, c : c + 8, :] = unit[i] * m[j] - unit[j] * m[i]


def body(segments, ship_list, kept_tiles, kept_count, lent_tiles, lent_count):
    leaves = segments.shape[0]
    bricks, slots = ship_list.shape[1:]
    keep = kept_tiles.shape[1]
    peers, lend = lent_tiles.shape[1:3]
    ghosts = bricks * slots
    ext = leaves + ghosts
    cap = keep + peers * lend + 2 * BATCH
    ship = jnp.transpose(ship_list, (0, 2, 1))
    kept = jnp.transpose(kept_tiles, (0, 2, 1))
    lent = jnp.transpose(lent_tiles, (0, 1, 3, 2))
    flat = segments.reshape(leaves * 8, 128)
    smem = pl.BlockSpec(memory_space=pltpu.SMEM)
    vmem = pl.BlockSpec(memory_space=pltpu.VMEM)
    tile_list = jax.ShapeDtypeStruct((cap,), jnp.int32)
    own_sums = jax.ShapeDtypeStruct((leaves * 8, 128), F32)
    hbm = pl.BlockSpec(memory_space=pl.ANY)

    def on_chip(x):
        return pltpu.with_memory_space_constraint(x, pltpu.VMEM)

    outgoing = pl.pallas_call(
        gather_kernel,
        out_shape=jax.ShapeDtypeStruct((bricks, slots * 8, 128), F32),
        in_specs=[smem, vmem],
        out_specs=vmem,
        name="ship_gather",
    )(ship, flat)
    incoming = lax.all_to_all(outgoing, "brick", split_axis=0, concat_axis=0, tiled=True)
    far_list, late_list, totals, *blocks = pl.pallas_call(
        plan_kernel,
        out_shape=[
            tile_list,
            tile_list,
            jax.ShapeDtypeStruct((2,), jnp.int32),
            *(jax.ShapeDtypeStruct(x.shape, x.dtype) for x in block_arrays(leaves)),
        ],
        in_specs=[smem, smem, smem, smem, smem, vmem],
        out_specs=[smem, smem, smem, hbm, hbm, hbm],
        scratch_shapes=[
            *block_arrays(leaves),
            pltpu.SMEM((cap,), jnp.int32),
            pltpu.SemaphoreType.DMA((leaves // PREP, 3)),
        ],
        name="plan_tiles",
    )(ship, kept, kept_count, lent, lent_count, flat)
    far_sums, back = pl.pallas_call(
        far_kernel,
        out_shape=[own_sums, jax.ShapeDtypeStruct((bricks, slots * 6, 128), F32)],
        in_specs=[smem, smem, vmem, hbm, hbm, hbm],
        out_specs=[vmem, vmem],
        scratch_shapes=[
            pltpu.VMEM(((ext + 1) * 8, 128), F32),
            *block_arrays(ext + 1),
            pltpu.SemaphoreType.DMA((3,)),
            *tile_scratch(),
        ],
        name="far_tiles",
    )(far_list, totals, on_chip(incoming.reshape(ghosts * 8, 128)), *blocks)
    returned = lax.all_to_all(back, "brick", split_axis=0, concat_axis=0, tiled=True)
    own = pl.pallas_call(
        late_kernel,
        out_shape=own_sums,
        in_specs=[smem, smem, vmem, vmem],
        out_specs=vmem,
        scratch_shapes=[pltpu.VMEM(((leaves + 1) * 8, 128), F32), *block_arrays(leaves + 1), *tile_scratch()],
        name="late_tiles",
    )(late_list, totals, flat, far_sums)
    loads = pl.pallas_call(
        finish_kernel,
        out_shape=jax.ShapeDtypeStruct((6, leaves, 128), F32),
        in_specs=[smem, vmem, vmem, vmem],
        out_specs=vmem,
        scratch_shapes=[pltpu.VMEM((leaves * 8, 128), F32)],
        name="finish",
    )(ship, flat, own, on_chip(returned))
    return jnp.transpose(loads, (1, 0, 2))


def solution(mesh):
    placed = (
        P(("brick", "region"), None, None),
        P(("brick", "region"), None, None),
        P(("brick", "region"), None, None),
        P(("brick", "region")),
        P(("brick", "region"), None, None, None),
        P("brick", None, None),
    )
    return jax.shard_map(
        body,
        mesh=mesh,
        in_specs=placed,
        out_specs=P(("brick", "region"), None, None),
        check_vma=False,
    )
```

```python
import jax
import jax.numpy as jnp
from jax import lax
from jax.experimental import pallas as pl
from jax.experimental.pallas import tpu as pltpu
from jax.sharding import PartitionSpec as P

DIST_FLOOR = 0.0025
PARALLEL_FLOOR = 0.05
TINY = 1e-20
STAND_IN = 1e-30
SHIFT = 10
F32 = jnp.float32
BF16 = jnp.bfloat16

GROUPS = 12
DEPTH = 8 * GROUPS
RIGHT_ROWS = 8 * (3 * 6 + 7 * 4)
OUTS = 13
PLACES = [{0: 3 * n, 1: 3 * n + 1, 2: 3 * n + 2} for n in range(3)] + [{}, {}, {}, {}, {}, {}]
for _n in range(7):
    PLACES[2 + _n].update({4: 9 + 2 * _n, 5: 10 + 2 * _n})
PLACES += [{}] * 4
BATCH = 4
PREP = 8


def parts(x):
    first = x.astype(BF16).astype(F32)
    rest = x - first
    second = rest.astype(BF16).astype(F32)
    return first, second, rest - second


def write_blocks(src, feat, left, right, first, blocks):
    row = lax.broadcasted_iota(jnp.int32, (8, 128), 0)
    is_dir = (row >= 3) & (row < 6)
    one = jnp.ones((8, 128), F32)
    zero = jnp.zeros((8, 128), F32)

    def pick(mask, x):
        return jnp.where(mask, x, 0.0)

    def total(x):
        return jnp.broadcast_to(jnp.sum(x, axis=0, keepdims=True), (8, 128))

    def spread(x, r):
        return jnp.broadcast_to(x[r : r + 1, :], (8, 128))

    def one_block(n):
        x = src[pl.ds(pl.multiple_of(n * 8, 8), 8), :]
        squared = total(pick(is_dir, x * x))
        inverse = lax.rsqrt(squared)
        pose = jnp.where(is_dir, x * inverse, pick(row < 3, x))
        along = total(pick(is_dir, pose * pltpu.roll(pose, 3, 0)))
        length = squared * inverse
        flipped = 1.0 / jnp.where(x == 0.0, STAND_IN, x)
        single = pick(row == 4, length)
        for r, value in ((3, spread(flipped, 6)), (2, 0.75 * spread(flipped, 7)), (1, spread(x, 6)), (0, along)):
            single = jnp.where(row == r, value, single)
        at = first + n
        feat[pl.ds(pl.multiple_of(at * 8, 8), 8), :] = jnp.where(row == 3, length, pltpu.roll(pose, 5, 0))
        p, q = parts(pose), parts(single)
        stack = jnp.concatenate([p[0], p[0], p[0], p[1], p[1], p[2], *q, one, one, one], axis=0)
        left[pl.ds(pl.multiple_of(at * 128, 128), 128), 0:DEPTH] = jnp.transpose(stack.astype(BF16))
        halves = []
        for three in (
            [pick(is_dir, y) for y in p],
            [pick(is_dir, -pltpu.roll(y, 3, 0)) for y in p],
            [pick(row < 3, pltpu.roll(y, 5, 0)) for y in p],
        ):
            halves += [three[m] for m in (0, 1, 2, 0, 1, 0)]
        for source, r in ((q, 0), (p, 0), (p, 1), (p, 2)):
            halves += [zero] + [pick(row == r, -y) for y in source]
        for r in (1, 2, 3):
            halves += [jnp.where(row == r, 1.0, 0.0)] + [pick(row == r, y) for y in q]
        right[pl.ds(pl.multiple_of(at * RIGHT_ROWS, 16), RIGHT_ROWS), :] = jnp.concatenate(halves, axis=0).astype(BF16)

    def step(n, carry):
        for u in range(PREP):
            one_block(n * PREP + u)
        return carry

    lax.fori_loop(0, blocks // PREP, step, 0)


def write_template(fixed):
    row = lax.broadcasted_iota(jnp.int32, (DEPTH, 128), 0)
    picks = [[], [48, 56, 64], []]
    picks += [[k, 24 + k, 40 + k] for k in range(3)]
    picks += [[48 + n, 56 + n, 64 + n] for n in (1, 2, 3)]
    picks += [[3 + k, 27 + k, 43 + k] for k in range(3)]
    picks += [[52, 60, 68]]
    for n, chosen in enumerate(picks):
        hit = jnp.zeros((DEPTH, 128), jnp.bool_)
        for r in chosen:
            hit = hit | (row == r)
        fixed[:, 128 * n : 128 * (n + 1)] = jnp.where(hit, 1.0, 0.0).astype(BF16)


def products(left, right, fixed, prod, pair):
    ia, ib = pair
    a = left[pl.ds(pl.multiple_of(ia * 128, 128), 128), 0:DEPTH]
    mine = right[pl.ds(pl.multiple_of(ib * RIGHT_ROWS, 16), RIGHT_ROWS), :]

    def column(n):
        places = PLACES[n]
        rows = []
        for k in range(GROUPS // 2):
            if k in places:
                rows.append(mine[16 * places[k] : 16 * places[k] + 16, :])
            else:
                rows.append(fixed[16 * k : 16 * k + 16, 128 * n : 128 * (n + 1)])
        return jnp.concatenate(rows, axis=0)

    for low in range(0, OUTS, 2):
        high = min(low + 2, OUTS)
        b = jnp.concatenate([column(n) for n in range(low, high)], axis=1)
        prod[:, 128 * low : 128 * high] = lax.dot_general(
            a, b, (((1,), (0,)), ((), ())), preferred_element_type=F32
        )


def pair_sums(feat, prod, part, ib):
    ux2, uy2, uz2, len2 = (jnp.broadcast_to(feat[pl.ds(ib * 8 + q, 1), :], (8, 128)) for q in range(4))
    sums = None
    for g in range(16):
        rows = slice(8 * g, 8 * g + 8)
        w, c, f, ox, oy, oz, reach, compliance, curvature, ux1, uy1, uz1, len1 = (
            prod[rows, 128 * n : 128 * (n + 1)] for n in range(OUTS)
        )
        inverse = pl.reciprocal(jnp.maximum(1.0 - w * w, PARALLEL_FLOOR))
        s = jnp.minimum(jnp.maximum((w * f - c) * inverse, 0.0), len1)
        t = jnp.minimum(jnp.maximum(w * s + f, 0.0), len2)
        s = jnp.minimum(jnp.maximum(w * t - c, 0.0), len1)
        gx = ox + s * ux1 - t * ux2
        gy = oy + s * uy1 - t * uy2
        gz = oz + s * uz1 - t * uz2
        square = jnp.maximum(gx * gx + gy * gy + gz * gz, DIST_FLOOR)
        near = lax.rsqrt(square)
        depth = jnp.maximum(reach - square * near, TINY)
        root = lax.rsqrt(depth * curvature)
        scale = (depth * root) * (depth * near) * pl.reciprocal(compliance)
        force = [scale * gx, scale * gy, scale * gz]
        on_a = force + [s * x for x in force]
        on_b = force + [t * x for x in force]
        for q in range(6):
            part[rows, q : q + 1] = jnp.sum(on_a[q], axis=1, keepdims=True)
        sums = on_b if sums is None else [x + y for x, y in zip(sums, on_b)]
    return jnp.concatenate([jnp.sum(x, axis=0, keepdims=True) for x in sums] + [jnp.zeros((2, 128), F32)], axis=0)


def block_arrays(blocks):
    return [
        pltpu.VMEM((blocks * 8, 128), F32),
        pltpu.VMEM((blocks * 128, 128), BF16),
        pltpu.VMEM((blocks * RIGHT_ROWS, 128), BF16),
    ]


def tile_scratch():
    return [
        pltpu.VMEM((DEPTH, OUTS * 128), BF16),
        *[pltpu.VMEM((128, OUTS * 128), F32)] * (2 * BATCH),
        *[pltpu.VMEM((128, 128), F32)] * (2 * BATCH),
        *[pltpu.VMEM((8, 128), F32)] * (2 * BATCH),
    ]


def pad_list(tiles, count, dummy):
    for u in range(2 * BATCH):
        tiles[count + u] = (dummy << SHIFT) | dummy


def run_tiles(blocks, scratch, acc, tiles, count):
    feat, left, right = blocks
    fixed = scratch[0]
    prods, sums_a, sums_b = (scratch[1 + 2 * BATCH * k : 1 + 2 * BATCH * (k + 1)] for k in range(3))
    write_template(fixed)
    for ref in (*sums_a, *sums_b):
        ref[...] = jnp.zeros_like(ref)

    def ids(n):
        code = tiles[n]
        return lax.shift_right_logical(code, SHIFT), code & ((1 << SHIFT) - 1)

    def collect(first, side):
        for u in range(BATCH):
            ia, ib = ids(jnp.maximum(first + u, 0))
            slot = side * BATCH + u
            acc[pl.ds(pl.multiple_of(ia * 8, 8), 8), :] += jnp.transpose(sums_a[slot][...])[0:8, :]
            acc[pl.ds(pl.multiple_of(ib * 8, 8), 8), :] -= sums_b[slot][...]

    def prepare(first, side):
        for u in range(BATCH):
            products(left, right, fixed, prods[side * BATCH + u], ids(first + u))

    def batch(first, side):
        collect(first - BATCH, 1 - side)
        prepare(first + BATCH, 1 - side)
        for u in range(BATCH):
            slot = side * BATCH + u
            sums_b[slot][...] = pair_sums(feat, prods[slot], sums_a[slot], ids(first + u)[1])

    prepare(0, 0)

    def step(n, carry):
        first = 2 * BATCH * n
        batch(first, 0)

        @pl.when(first + BATCH < count)
        def _():
            batch(first + BATCH, 1)

        return carry

    lax.fori_loop(0, (count + 2 * BATCH - 1) // (2 * BATCH), step, 0)
    batches = (count + BATCH - 1) // BATCH

    @pl.when((batches & 1) == 1)
    def _():
        collect((batches - 1) * BATCH, 0)

    @pl.when((batches > 0) & ((batches & 1) == 0))
    def _():
        collect((batches - 1) * BATCH, 1)


def gather_kernel(ship_ref, seg_ref, out_ref):
    slots, bricks = ship_ref.shape[1:]
    for q in range(bricks):
        for k in range(slots):
            out_ref[q, 8 * k : 8 * k + 8, :] = seg_ref[pl.ds(pl.multiple_of(ship_ref[0, k, q] * 8, 8), 8), :]


def plan_kernel(ship_ref, kept_ref, count_ref, lent_ref, plan_ref, list_ref, total_ref):
    slots, bricks = ship_ref.shape[1:]
    peers = lent_ref.shape[1]
    leaves = total_ref.shape[0]
    brick = lax.axis_index("brick")
    region = lax.axis_index("region")
    mine = leaves + brick * slots

    def local_id(e):
        ghost = e - mine
        is_mine = (ghost >= 0) & (ghost < slots)
        return jnp.where(is_mine, ship_ref[0, jnp.where(is_mine, ghost, 0), brick], e)

    def file_tile(a, b, n):
        list_ref[n] = lax.shift_left(local_id(a), SHIFT) | local_id(b)
        return n + 1

    n = lax.fori_loop(0, count_ref[0], lambda k, c: file_tile(kept_ref[0, 0, k], kept_ref[0, 1, k], c), 0)
    for j in range(peers):
        n = lax.fori_loop(
            0, plan_ref[0, region, j], lambda k, c: file_tile(lent_ref[0, j, 0, k], lent_ref[0, j, 1, k], c), n
        )
    pad_list(list_ref, n, leaves + slots * bricks)
    total_ref[0] = n


def tile_kernel(list_ref, total_ref, seg_ref, ghost_ref, own_ref, back_ref, acc, feat, left, right, *scratch):
    own_rows = seg_ref.shape[0]
    leaves = own_rows // 8
    ghosts = ghost_ref.shape[0] // 8
    bricks = back_ref.shape[0]
    slots = ghosts // bricks
    acc[...] = jnp.zeros_like(acc)
    write_blocks(seg_ref, feat, left, right, 0, leaves)
    write_blocks(ghost_ref, feat, left, right, leaves, ghosts)
    run_tiles((feat, left, right), scratch, acc, list_ref, total_ref[0])
    own_ref[...] = acc[0:own_rows, :]
    for q in range(bricks):
        for k in range(slots):
            row = own_rows + 8 * (q * slots + k)
            back_ref[q, 6 * k : 6 * k + 6, :] = acc[row : row + 6, :]


def stride_rows(first, count, row, stride):
    return pl.ds(first * stride + row, count, stride=stride)


def finish_kernel(ship_ref, seg_ref, own_ref, back_ref, out_ref, acc):
    leaves = seg_ref.shape[0] // 8
    slots, bricks = ship_ref.shape[1:]
    acc[...] = own_ref[...]
    for q in range(bricks):
        for k in range(slots):
            row = pl.multiple_of(ship_ref[0, k, q] * 8, 8)
            acc[pl.ds(row, 6), :] += back_ref[q, 6 * k : 6 * k + 6, :]
    for c in range(0, leaves, 8):
        d = [seg_ref[stride_rows(c, 8, 3 + q, 8), :] for q in range(3)]
        force = [acc[stride_rows(c, 8, q, 8), :] for q in range(3)]
        lever = [acc[stride_rows(c, 8, 3 + q, 8), :] for q in range(3)]
        squared = d[0] * d[0] + d[1] * d[1] + d[2] * d[2]
        inverse = lax.rsqrt(squared)
        half = 0.5 * squared * inverse
        unit = [x * inverse for x in d]
        m = [x - half * y for x, y in zip(lever, force)]
        for q in range(3):
            i, j = (q + 1) % 3, (q + 2) % 3
            out_ref[q, c : c + 8, :] = force[q]
            out_ref[3 + q, c : c + 8, :] = unit[i] * m[j] - unit[j] * m[i]


def body(segments, ship_list, kept_tiles, kept_count, lent_tiles, lent_count):
    leaves = segments.shape[0]
    bricks, slots = ship_list.shape[1:]
    keep = kept_tiles.shape[1]
    peers, lend = lent_tiles.shape[1:3]
    ghosts = bricks * slots
    ext = leaves + ghosts
    cap = keep + peers * lend + 2 * BATCH
    ship = jnp.transpose(ship_list, (0, 2, 1))
    kept = jnp.transpose(kept_tiles, (0, 2, 1))
    lent = jnp.transpose(lent_tiles, (0, 1, 3, 2))
    flat = segments.reshape(leaves * 8, 128)
    smem = pl.BlockSpec(memory_space=pltpu.SMEM)
    vmem = pl.BlockSpec(memory_space=pltpu.VMEM)
    tile_list = jax.ShapeDtypeStruct((cap,), jnp.int32)
    own_sums = jax.ShapeDtypeStruct((leaves * 8, 128), F32)

    def on_chip(x):
        return pltpu.with_memory_space_constraint(x, pltpu.VMEM)

    outgoing = pl.pallas_call(
        gather_kernel,
        out_shape=jax.ShapeDtypeStruct((bricks, slots * 8, 128), F32),
        in_specs=[smem, vmem],
        out_specs=vmem,
        name="ship_gather",
    )(ship, flat)
    incoming = lax.all_to_all(outgoing, "brick", split_axis=0, concat_axis=0, tiled=True)
    tiles, total = pl.pallas_call(
        plan_kernel,
        out_shape=[tile_list, jax.ShapeDtypeStruct((leaves,), jnp.int32)],
        in_specs=[smem] * 5,
        out_specs=[smem, smem],
        name="plan_tiles",
    )(ship, kept, kept_count, lent, lent_count)
    own, back = pl.pallas_call(
        tile_kernel,
        out_shape=[own_sums, jax.ShapeDtypeStruct((bricks, slots * 6, 128), F32)],
        in_specs=[smem, smem, vmem, vmem],
        out_specs=[vmem, vmem],
        scratch_shapes=[pltpu.VMEM(((ext + 1) * 8, 128), F32), *block_arrays(ext + 1), *tile_scratch()],
        name="all_tiles",
    )(tiles, total, flat, on_chip(incoming.reshape(ghosts * 8, 128)))
    returned = lax.all_to_all(back, "brick", split_axis=0, concat_axis=0, tiled=True)
    loads = pl.pallas_call(
        finish_kernel,
        out_shape=jax.ShapeDtypeStruct((6, leaves, 128), F32),
        in_specs=[smem, vmem, vmem, vmem],
        out_specs=vmem,
        scratch_shapes=[pltpu.VMEM((leaves * 8, 128), F32)],
        name="finish",
    )(ship, flat, own, returned)
    return jnp.transpose(loads, (1, 0, 2))


def solution(mesh):
    placed = (
        P(("brick", "region"), None, None),
        P(("brick", "region"), None, None),
        P(("brick", "region"), None, None),
        P(("brick", "region")),
        P(("brick", "region"), None, None, None),
        P("brick", None, None),
    )
    return jax.shard_map(
        body,
        mesh=mesh,
        in_specs=placed,
        out_specs=P(("brick", "region"), None, None),
        check_vma=False,
    )
```

```python
import jax
import jax.numpy as jnp
from jax import lax
from jax.experimental import pallas as pl
from jax.experimental.pallas import tpu as pltpu
from jax.sharding import PartitionSpec as P

DIST_FLOOR = 0.0025
PARALLEL_FLOOR = 0.05
TINY = 1e-20
STAND_IN = 1e-30
SHIFT = 10
F32 = jnp.float32
BF16 = jnp.bfloat16

GROUPS = 12
DEPTH = 8 * GROUPS
RIGHT_ROWS = 8 * (3 * 6 + 7 * 4)
OUTS = 13
PLACES = [{0: 3 * n, 1: 3 * n + 1, 2: 3 * n + 2} for n in range(3)] + [{}, {}, {}, {}, {}, {}]
for _n in range(7):
    PLACES[2 + _n].update({4: 9 + 2 * _n, 5: 10 + 2 * _n})
PLACES += [{}] * 4
HEAD = 8
BATCH = 4
PREP = 8


def parts(x):
    first = x.astype(BF16).astype(F32)
    rest = x - first
    second = rest.astype(BF16).astype(F32)
    return first, second, rest - second


def write_blocks(src, feat, left, right, first, blocks):
    row = lax.broadcasted_iota(jnp.int32, (8, 128), 0)
    is_dir = (row >= 3) & (row < 6)
    one = jnp.ones((8, 128), F32)
    zero = jnp.zeros((8, 128), F32)

    def pick(mask, x):
        return jnp.where(mask, x, 0.0)

    def total(x):
        return jnp.broadcast_to(jnp.sum(x, axis=0, keepdims=True), (8, 128))

    def spread(x, r):
        return jnp.broadcast_to(x[r : r + 1, :], (8, 128))

    def one_block(n):
        x = src[pl.ds(pl.multiple_of(n * 8, 8), 8), :]
        squared = total(pick(is_dir, x * x))
        inverse = lax.rsqrt(squared)
        pose = jnp.where(is_dir, x * inverse, pick(row < 3, x))
        along = total(pick(is_dir, pose * pltpu.roll(pose, 3, 0)))
        length = squared * inverse
        flipped = 1.0 / jnp.where(x == 0.0, STAND_IN, x)
        single = pick(row == 4, length)
        for r, value in ((3, spread(flipped, 6)), (2, 0.75 * spread(flipped, 7)), (1, spread(x, 6)), (0, along)):
            single = jnp.where(row == r, value, single)
        at = first + n
        feat[pl.ds(pl.multiple_of(at * 8, 8), 8), :] = jnp.where(row == 3, length, pltpu.roll(pose, 5, 0))
        p, q = parts(pose), parts(single)
        stack = jnp.concatenate([p[0], p[0], p[0], p[1], p[1], p[2], *q, one, one, one], axis=0)
        left[pl.ds(pl.multiple_of(at * 128, 128), 128), 0:DEPTH] = jnp.transpose(stack.astype(BF16))
        halves = []
        for three in (
            [pick(is_dir, y) for y in p],
            [pick(is_dir, -pltpu.roll(y, 3, 0)) for y in p],
            [pick(row < 3, pltpu.roll(y, 5, 0)) for y in p],
        ):
            halves += [three[m] for m in (0, 1, 2, 0, 1, 0)]
        for source, r in ((q, 0), (p, 0), (p, 1), (p, 2)):
            halves += [zero] + [pick(row == r, -y) for y in source]
        for r in (1, 2, 3):
            halves += [jnp.where(row == r, 1.0, 0.0)] + [pick(row == r, y) for y in q]
        right[pl.ds(pl.multiple_of(at * RIGHT_ROWS, 16), RIGHT_ROWS), :] = jnp.concatenate(halves, axis=0).astype(BF16)

    def step(n, carry):
        for u in range(PREP):
            one_block(n * PREP + u)
        return carry

    lax.fori_loop(0, blocks // PREP, step, 0)


def write_template(fixed):
    row = lax.broadcasted_iota(jnp.int32, (DEPTH, 128), 0)
    picks = [[], [48, 56, 64], []]
    picks += [[k, 24 + k, 40 + k] for k in range(3)]
    picks += [[48 + n, 56 + n, 64 + n] for n in (1, 2, 3)]
    picks += [[3 + k, 27 + k, 43 + k] for k in range(3)]
    picks += [[52, 60, 68]]
    for n, chosen in enumerate(picks):
        hit = jnp.zeros((DEPTH, 128), jnp.bool_)
        for r in chosen:
            hit = hit | (row == r)
        fixed[:, 128 * n : 128 * (n + 1)] = jnp.where(hit, 1.0, 0.0).astype(BF16)


def products(left, right, fixed, prod, pair):
    ia, ib = pair
    a = left[pl.ds(pl.multiple_of(ia * 128, 128), 128), 0:DEPTH]
    mine = right[pl.ds(pl.multiple_of(ib * RIGHT_ROWS, 16), RIGHT_ROWS), :]

    def column(n):
        places = PLACES[n]
        rows = []
        for k in range(GROUPS // 2):
            if k in places:
                rows.append(mine[16 * places[k] : 16 * places[k] + 16, :])
            else:
                rows.append(fixed[16 * k : 16 * k + 16, 128 * n : 128 * (n + 1)])
        return jnp.concatenate(rows, axis=0)

    for low in range(0, OUTS, 2):
        high = min(low + 2, OUTS)
        b = jnp.concatenate([column(n) for n in range(low, high)], axis=1)
        prod[:, 128 * low : 128 * high] = lax.dot_general(
            a, b, (((1,), (0,)), ((), ())), preferred_element_type=F32
        )


def pair_sums(feat, prod, part, ib):
    ux2, uy2, uz2, len2 = (jnp.broadcast_to(feat[pl.ds(ib * 8 + q, 1), :], (8, 128)) for q in range(4))
    sums = None
    for g in range(16):
        rows = slice(8 * g, 8 * g + 8)
        w, c, f, ox, oy, oz, reach, compliance, curvature, ux1, uy1, uz1, len1 = (
            prod[rows, 128 * n : 128 * (n + 1)] for n in range(OUTS)
        )
        inverse = pl.reciprocal(jnp.maximum(1.0 - w * w, PARALLEL_FLOOR))
        s = jnp.minimum(jnp.maximum((w * f - c) * inverse, 0.0), len1)
        t = jnp.minimum(jnp.maximum(w * s + f, 0.0), len2)
        s = jnp.minimum(jnp.maximum(w * t - c, 0.0), len1)
        gx = ox + s * ux1 - t * ux2
        gy = oy + s * uy1 - t * uy2
        gz = oz + s * uz1 - t * uz2
        square = jnp.maximum(gx * gx + gy * gy + gz * gz, DIST_FLOOR)
        near = lax.rsqrt(square)
        depth = jnp.maximum(reach - square * near, TINY)
        root = lax.rsqrt(depth * curvature)
        scale = (depth * root) * (depth * near) * pl.reciprocal(compliance)
        force = [scale * gx, scale * gy, scale * gz]
        on_a = force + [s * x for x in force]
        on_b = force + [t * x for x in force]
        for q in range(6):
            part[rows, q : q + 1] = jnp.sum(on_a[q], axis=1, keepdims=True)
        sums = on_b if sums is None else [x + y for x, y in zip(sums, on_b)]
    return jnp.concatenate([jnp.sum(x, axis=0, keepdims=True) for x in sums] + [jnp.zeros((2, 128), F32)], axis=0)


def block_arrays(blocks):
    return [
        pltpu.VMEM((blocks * 8, 128), F32),
        pltpu.VMEM((blocks * 128, 128), BF16),
        pltpu.VMEM((blocks * RIGHT_ROWS, 128), BF16),
    ]


def tile_scratch():
    return [
        pltpu.VMEM((DEPTH, OUTS * 128), BF16),
        *[pltpu.VMEM((128, OUTS * 128), F32)] * (2 * BATCH),
        *[pltpu.VMEM((128, 128), F32)] * (2 * BATCH),
        *[pltpu.VMEM((8, 128), F32)] * (2 * BATCH),
    ]


def run_tiles(blocks, scratch, acc, code_at, count):
    feat, left, right = blocks
    fixed = scratch[0]
    prods, sums_a, sums_b = (scratch[1 + 2 * BATCH * k : 1 + 2 * BATCH * (k + 1)] for k in range(3))
    write_template(fixed)
    for ref in (*sums_a, *sums_b):
        ref[...] = jnp.zeros_like(ref)

    def ids(n):
        code = code_at(n)
        return lax.shift_right_logical(code, SHIFT), code & ((1 << SHIFT) - 1)

    def collect(first, side):
        for u in range(BATCH):
            ia, ib = ids(jnp.maximum(first + u, 0))
            slot = side * BATCH + u
            acc[pl.ds(pl.multiple_of(ia * 8, 8), 8), :] += jnp.transpose(sums_a[slot][...])[0:8, :]
            acc[pl.ds(pl.multiple_of(ib * 8, 8), 8), :] -= sums_b[slot][...]

    def prepare(first, side):
        for u in range(BATCH):
            products(left, right, fixed, prods[side * BATCH + u], ids(first + u))

    def batch(first, side):
        collect(first - BATCH, 1 - side)
        prepare(first + BATCH, 1 - side)
        for u in range(BATCH):
            slot = side * BATCH + u
            sums_b[slot][...] = pair_sums(feat, prods[slot], sums_a[slot], ids(first + u)[1])

    prepare(0, 0)

    def step(n, carry):
        first = 2 * BATCH * n
        batch(first, 0)

        @pl.when(first + BATCH < count)
        def _():
            batch(first + BATCH, 1)

        return carry

    lax.fori_loop(0, (count + 2 * BATCH - 1) // (2 * BATCH), step, 0)
    batches = (count + BATCH - 1) // BATCH

    @pl.when((batches & 1) == 1)
    def _():
        collect((batches - 1) * BATCH, 0)

    @pl.when((batches > 0) & ((batches & 1) == 0))
    def _():
        collect((batches - 1) * BATCH, 1)


def gather_kernel(ship_ref, seg_ref, out_ref):
    slots, bricks = ship_ref.shape[1:]
    for q in range(bricks):
        for k in range(slots):
            out_ref[q, 8 * k : 8 * k + 8, :] = seg_ref[pl.ds(pl.multiple_of(ship_ref[0, k, q] * 8, 8), 8), :]


def plan_kernel(ship_ref, kept_ref, count_ref, lent_ref, plan_ref, seg_ref, list_ref, near_ref):
    slots, bricks = ship_ref.shape[1:]
    peers = lent_ref.shape[1]
    leaves = seg_ref.shape[0] // 8
    brick = lax.axis_index("brick")
    region = lax.axis_index("region")
    mine = leaves + brick * slots

    def local_id(e):
        ghost = e - mine
        is_mine = (ghost >= 0) & (ghost < slots)
        return jnp.where(is_mine, ship_ref[0, jnp.where(is_mine, ghost, 0), brick], e)

    def file_tile(a, b, carry):
        near, far = carry
        a, b = local_id(a), local_id(b)
        code = lax.shift_left(a, SHIFT) | b
        is_near = (a < leaves) & (b < leaves)
        near_ref[near] = code
        list_ref[HEAD + far] = code
        step = is_near.astype(jnp.int32)
        return near + step, far + 1 - step

    carry = lax.fori_loop(
        0, count_ref[0], lambda k, c: file_tile(kept_ref[0, 0, k], kept_ref[0, 1, k], c), (0, 0)
    )
    for j in range(peers):
        carry = lax.fori_loop(
            0, plan_ref[0, region, j], lambda k, c: file_tile(lent_ref[0, j, 0, k], lent_ref[0, j, 1, k], c), carry
        )
    near, far = carry

    def append(k, carry):
        list_ref[HEAD + far + k] = near_ref[k]
        return carry

    lax.fori_loop(0, near, append, 0)
    list_ref[0] = near + far
    list_ref[1] = near


def tile_kernel(list_ref, other_ref, seg_ref, ghost_ref, guest_ref, own_ref, back_ref, loan_ref, acc, feat, left, right, *scratch):
    own_rows = seg_ref.shape[0]
    leaves = own_rows // 8
    ghosts = ghost_ref.shape[0] // 8
    ext = leaves + ghosts
    bricks = back_ref.shape[0]
    slots = ghosts // bricks
    last = list_ref.shape[0] - 1
    excess = list_ref[0] - other_ref[0]
    give = jnp.minimum(lax.shift_right_arithmetic(jnp.maximum(excess, 0), 1), list_ref[1])
    take = jnp.minimum(lax.shift_right_arithmetic(jnp.maximum(-excess, 0), 1), other_ref[1])
    keep = list_ref[0] - give
    borrowed = HEAD + other_ref[0] - take - keep
    guest_code = (ext << SHIFT) | ext
    dummy_code = ((ext + leaves) << SHIFT) | (ext + leaves)

    def code_at(n):
        kept = list_ref[jnp.minimum(HEAD + n, last)]
        lent = other_ref[jnp.clip(borrowed + n, 0, last)] + guest_code
        return jnp.where(n < keep, kept, jnp.where(n < keep + take, lent, dummy_code))

    acc[...] = jnp.zeros_like(acc)
    write_blocks(seg_ref, feat, left, right, 0, leaves)
    write_blocks(ghost_ref, feat, left, right, leaves, ghosts)

    @pl.when(take > 0)
    def _():
        write_blocks(guest_ref, feat, left, right, ext, leaves)

    run_tiles((feat, left, right), scratch, acc, code_at, keep + take)
    own_ref[...] = acc[0:own_rows, :]
    loan_ref[...] = acc[8 * ext : 8 * ext + own_rows, :]
    for q in range(bricks):
        for k in range(slots):
            row = own_rows + 8 * (q * slots + k)
            back_ref[q, 6 * k : 6 * k + 6, :] = acc[row : row + 6, :]


def stride_rows(first, count, row, stride):
    return pl.ds(first * stride + row, count, stride=stride)


def finish_kernel(ship_ref, seg_ref, own_ref, loan_ref, back_ref, out_ref, acc):
    leaves = seg_ref.shape[0] // 8
    slots, bricks = ship_ref.shape[1:]
    acc[...] = own_ref[...] + loan_ref[...]
    for q in range(bricks):
        for k in range(slots):
            row = pl.multiple_of(ship_ref[0, k, q] * 8, 8)
            acc[pl.ds(row, 6), :] += back_ref[q, 6 * k : 6 * k + 6, :]
    for c in range(0, leaves, 8):
        d = [seg_ref[stride_rows(c, 8, 3 + q, 8), :] for q in range(3)]
        force = [acc[stride_rows(c, 8, q, 8), :] for q in range(3)]
        lever = [acc[stride_rows(c, 8, 3 + q, 8), :] for q in range(3)]
        squared = d[0] * d[0] + d[1] * d[1] + d[2] * d[2]
        inverse = lax.rsqrt(squared)
        half = 0.5 * squared * inverse
        unit = [x * inverse for x in d]
        m = [x - half * y for x, y in zip(lever, force)]
        for q in range(3):
            i, j = (q + 1) % 3, (q + 2) % 3
            out_ref[q, c : c + 8, :] = force[q]
            out_ref[3 + q, c : c + 8, :] = unit[i] * m[j] - unit[j] * m[i]


def body(segments, ship_list, kept_tiles, kept_count, lent_tiles, lent_count):
    leaves = segments.shape[0]
    bricks, slots = ship_list.shape[1:]
    keep = kept_tiles.shape[1]
    peers, lend = lent_tiles.shape[1:3]
    ghosts = bricks * slots
    ext = leaves + ghosts
    cap = -(-(HEAD + keep + peers * lend + 1) // 128) * 128
    ship = jnp.transpose(ship_list, (0, 2, 1))
    kept = jnp.transpose(kept_tiles, (0, 2, 1))
    lent = jnp.transpose(lent_tiles, (0, 1, 3, 2))
    flat = segments.reshape(leaves * 8, 128)
    smem = pl.BlockSpec(memory_space=pltpu.SMEM)
    vmem = pl.BlockSpec(memory_space=pltpu.VMEM)
    tile_list = jax.ShapeDtypeStruct((cap,), jnp.int32)
    own_sums = jax.ShapeDtypeStruct((leaves * 8, 128), F32)

    def on_chip(x):
        return pltpu.with_memory_space_constraint(x, pltpu.VMEM)

    outgoing = pl.pallas_call(
        gather_kernel,
        out_shape=jax.ShapeDtypeStruct((bricks, slots * 8, 128), F32),
        in_specs=[smem, vmem],
        out_specs=vmem,
        name="ship_gather",
    )(ship, flat)
    incoming = lax.all_to_all(outgoing, "brick", split_axis=0, concat_axis=0, tiled=True)
    partner = [(r, r ^ 1) for r in range(lax.axis_size("region"))]
    guests = lax.ppermute(flat, "region", partner)
    tiles = pl.pallas_call(
        plan_kernel,
        out_shape=tile_list,
        in_specs=[smem] * 5 + [pl.BlockSpec(memory_space=pl.ANY)],
        out_specs=smem,
        scratch_shapes=[pltpu.SMEM((cap,), jnp.int32)],
        name="plan_tiles",
    )(ship, kept, kept_count, lent, lent_count, flat)
    other_tiles = lax.ppermute(tiles, "region", partner)
    own, back, loan = pl.pallas_call(
        tile_kernel,
        out_shape=[own_sums, jax.ShapeDtypeStruct((bricks, slots * 6, 128), F32), own_sums],
        in_specs=[smem, smem, vmem, vmem, vmem],
        out_specs=[vmem, vmem, vmem],
        scratch_shapes=[
            pltpu.VMEM(((ext + leaves + 1) * 8, 128), F32),
            *block_arrays(ext + leaves + 1),
            *tile_scratch(),
        ],
        name="all_tiles",
    )(tiles, other_tiles, flat, on_chip(incoming.reshape(ghosts * 8, 128)), on_chip(guests))
    repaid = lax.ppermute(loan, "region", partner)
    returned = lax.all_to_all(back, "brick", split_axis=0, concat_axis=0, tiled=True)
    loads = pl.pallas_call(
        finish_kernel,
        out_shape=jax.ShapeDtypeStruct((6, leaves, 128), F32),
        in_specs=[smem, vmem, vmem, vmem, vmem],
        out_specs=vmem,
        scratch_shapes=[pltpu.VMEM((leaves * 8, 128), F32)],
        name="finish",
    )(ship, flat, own, on_chip(repaid), on_chip(returned))
    return jnp.transpose(loads, (1, 0, 2))


def solution(mesh):
    placed = (
        P(("brick", "region"), None, None),
        P(("brick", "region"), None, None),
        P(("brick", "region"), None, None),
        P(("brick", "region")),
        P(("brick", "region"), None, None, None),
        P("brick", None, None),
    )
    return jax.shard_map(
        body,
        mesh=mesh,
        in_specs=placed,
        out_specs=P(("brick", "region"), None, None),
        check_vma=False,
    )
```

```python
import jax
import jax.numpy as jnp
from jax import lax
from jax.experimental import pallas as pl
from jax.experimental.pallas import tpu as pltpu
from jax.sharding import PartitionSpec as P

DIST_FLOOR = 0.0025
PARALLEL_FLOOR = 0.05
TINY = 1e-20
STAND_IN = 1e-30
SHIFT = 10
F32 = jnp.float32
BF16 = jnp.bfloat16

GROUPS = 12
DEPTH = 8 * GROUPS
RIGHT_ROWS = 8 * (3 * 6 + 7 * 4)
OUTS = 13
PLACES = [{0: 3 * n, 1: 3 * n + 1, 2: 3 * n + 2} for n in range(3)] + [{}, {}, {}, {}, {}, {}]
for _n in range(7):
    PLACES[2 + _n].update({4: 9 + 2 * _n, 5: 10 + 2 * _n})
PLACES += [{}] * 4
HEAD = 8
BATCH = 4
PREP = 8


def parts(x):
    first = x.astype(BF16).astype(F32)
    rest = x - first
    second = rest.astype(BF16).astype(F32)
    return first, second, rest - second


def write_blocks(src, feat, left, right, first, blocks):
    row = lax.broadcasted_iota(jnp.int32, (8, 128), 0)
    is_dir = (row >= 3) & (row < 6)
    one = jnp.ones((8, 128), F32)
    zero = jnp.zeros((8, 128), F32)

    def pick(mask, x):
        return jnp.where(mask, x, 0.0)

    def total(x):
        return jnp.broadcast_to(jnp.sum(x, axis=0, keepdims=True), (8, 128))

    def spread(x, r):
        return jnp.broadcast_to(x[r : r + 1, :], (8, 128))

    def one_block(n):
        x = src[pl.ds(pl.multiple_of(n * 8, 8), 8), :]
        squared = total(pick(is_dir, x * x))
        inverse = lax.rsqrt(squared)
        pose = jnp.where(is_dir, x * inverse, pick(row < 3, x))
        along = total(pick(is_dir, pose * pltpu.roll(pose, 3, 0)))
        length = squared * inverse
        flipped = 1.0 / jnp.where(x == 0.0, STAND_IN, x)
        single = pick(row == 4, length)
        for r, value in ((3, spread(flipped, 6)), (2, 0.75 * spread(flipped, 7)), (1, spread(x, 6)), (0, along)):
            single = jnp.where(row == r, value, single)
        at = first + n
        feat[pl.ds(pl.multiple_of(at * 8, 8), 8), :] = jnp.where(row == 3, length, pltpu.roll(pose, 5, 0))
        p, q = parts(pose), parts(single)
        stack = jnp.concatenate([p[0], p[0], p[0], p[1], p[1], p[2], *q, one, one, one], axis=0)
        left[pl.ds(pl.multiple_of(at * 128, 128), 128), 0:DEPTH] = jnp.transpose(stack.astype(BF16))
        halves = []
        for three in (
            [pick(is_dir, y) for y in p],
            [pick(is_dir, -pltpu.roll(y, 3, 0)) for y in p],
            [pick(row < 3, pltpu.roll(y, 5, 0)) for y in p],
        ):
            halves += [three[m] for m in (0, 1, 2, 0, 1, 0)]
        for source, r in ((q, 0), (p, 0), (p, 1), (p, 2)):
            halves += [zero] + [pick(row == r, -y) for y in source]
        for r in (1, 2, 3):
            halves += [jnp.where(row == r, 1.0, 0.0)] + [pick(row == r, y) for y in q]
        right[pl.ds(pl.multiple_of(at * RIGHT_ROWS, 16), RIGHT_ROWS), :] = jnp.concatenate(halves, axis=0).astype(BF16)

    def step(n, carry):
        for u in range(PREP):
            one_block(n * PREP + u)
        return carry

    lax.fori_loop(0, blocks // PREP, step, 0)


def write_template(fixed):
    row = lax.broadcasted_iota(jnp.int32, (DEPTH, 128), 0)
    picks = [[], [48, 56, 64], []]
    picks += [[k, 24 + k, 40 + k] for k in range(3)]
    picks += [[48 + n, 56 + n, 64 + n] for n in (1, 2, 3)]
    picks += [[3 + k, 27 + k, 43 + k] for k in range(3)]
    picks += [[52, 60, 68]]
    for n, chosen in enumerate(picks):
        hit = jnp.zeros((DEPTH, 128), jnp.bool_)
        for r in chosen:
            hit = hit | (row == r)
        fixed[:, 128 * n : 128 * (n + 1)] = jnp.where(hit, 1.0, 0.0).astype(BF16)


def products(left, right, fixed, prod, pair):
    ia, ib = pair
    a = left[pl.ds(pl.multiple_of(ia * 128, 128), 128), 0:DEPTH]
    mine = right[pl.ds(pl.multiple_of(ib * RIGHT_ROWS, 16), RIGHT_ROWS), :]

    def column(n):
        places = PLACES[n]
        rows = []
        for k in range(GROUPS // 2):
            if k in places:
                rows.append(mine[16 * places[k] : 16 * places[k] + 16, :])
            else:
                rows.append(fixed[16 * k : 16 * k + 16, 128 * n : 128 * (n + 1)])
        return jnp.concatenate(rows, axis=0)

    for low in range(0, OUTS, 2):
        high = min(low + 2, OUTS)
        b = jnp.concatenate([column(n) for n in range(low, high)], axis=1)
        prod[:, 128 * low : 128 * high] = lax.dot_general(
            a, b, (((1,), (0,)), ((), ())), preferred_element_type=F32
        )


def pair_sums(feat, prod, part, ib):
    ux2, uy2, uz2, len2 = (jnp.broadcast_to(feat[pl.ds(ib * 8 + q, 1), :], (8, 128)) for q in range(4))
    sums = None
    for g in range(16):
        rows = slice(8 * g, 8 * g + 8)
        w, c, f, ox, oy, oz, reach, compliance, curvature, ux1, uy1, uz1, len1 = (
            prod[rows, 128 * n : 128 * (n + 1)] for n in range(OUTS)
        )
        inverse = pl.reciprocal(jnp.maximum(1.0 - w * w, PARALLEL_FLOOR))
        s = jnp.minimum(jnp.maximum((w * f - c) * inverse, 0.0), len1)
        t = jnp.minimum(jnp.maximum(w * s + f, 0.0), len2)
        s = jnp.minimum(jnp.maximum(w * t - c, 0.0), len1)
        gx = ox + s * ux1 - t * ux2
        gy = oy + s * uy1 - t * uy2
        gz = oz + s * uz1 - t * uz2
        square = jnp.maximum(gx * gx + gy * gy + gz * gz, DIST_FLOOR)
        near = lax.rsqrt(square)
        depth = jnp.maximum(reach - square * near, TINY)
        root = lax.rsqrt(depth * curvature)
        scale = (depth * root) * (depth * near) * pl.reciprocal(compliance)
        force = [scale * gx, scale * gy, scale * gz]
        on_a = force + [s * x for x in force]
        on_b = force + [t * x for x in force]
        for q in range(6):
            part[rows, q : q + 1] = jnp.sum(on_a[q], axis=1, keepdims=True)
        sums = on_b if sums is None else [x + y for x, y in zip(sums, on_b)]
    return jnp.concatenate([jnp.sum(x, axis=0, keepdims=True) for x in sums] + [jnp.zeros((2, 128), F32)], axis=0)


def block_arrays(blocks):
    return [
        pltpu.VMEM((blocks * 8, 128), F32),
        pltpu.VMEM((blocks * 128, 128), BF16),
        pltpu.VMEM((blocks * RIGHT_ROWS, 128), BF16),
    ]


def tile_scratch():
    return [
        pltpu.VMEM((DEPTH, OUTS * 128), BF16),
        *[pltpu.VMEM((128, OUTS * 128), F32)] * (2 * BATCH),
        *[pltpu.VMEM((128, 128), F32)] * (2 * BATCH),
        *[pltpu.VMEM((8, 128), F32)] * (2 * BATCH),
    ]


def run_tiles(blocks, scratch, acc, code_at, count):
    feat, left, right = blocks
    fixed = scratch[0]
    prods, sums_a, sums_b = (scratch[1 + 2 * BATCH * k : 1 + 2 * BATCH * (k + 1)] for k in range(3))
    write_template(fixed)
    for ref in (*sums_a, *sums_b):
        ref[...] = jnp.zeros_like(ref)

    def ids(n):
        code = code_at(n)
        return lax.shift_right_logical(code, SHIFT), code & ((1 << SHIFT) - 1)

    def collect(first, side):
        for u in range(BATCH):
            ia, ib = ids(jnp.maximum(first + u, 0))
            slot = side * BATCH + u
            acc[pl.ds(pl.multiple_of(ia * 8, 8), 8), :] += jnp.transpose(sums_a[slot][...])[0:8, :]
            acc[pl.ds(pl.multiple_of(ib * 8, 8), 8), :] -= sums_b[slot][...]

    def prepare(first, side):
        for u in range(BATCH):
            products(left, right, fixed, prods[side * BATCH + u], ids(first + u))

    def batch(first, side):
        collect(first - BATCH, 1 - side)
        prepare(first + BATCH, 1 - side)
        for u in range(BATCH):
            slot = side * BATCH + u
            sums_b[slot][...] = pair_sums(feat, prods[slot], sums_a[slot], ids(first + u)[1])

    prepare(0, 0)

    def step(n, carry):
        first = 2 * BATCH * n
        batch(first, 0)

        @pl.when(first + BATCH < count)
        def _():
            batch(first + BATCH, 1)

        return carry

    lax.fori_loop(0, (count + 2 * BATCH - 1) // (2 * BATCH), step, 0)
    batches = (count + BATCH - 1) // BATCH

    @pl.when((batches & 1) == 1)
    def _():
        collect((batches - 1) * BATCH, 0)

    @pl.when((batches > 0) & ((batches & 1) == 0))
    def _():
        collect((batches - 1) * BATCH, 1)


def plan_kernel(ship_ref, kept_ref, count_ref, lent_ref, plan_ref, seg_ref, out_ref, list_ref, near_ref, sems):
    slots, bricks = ship_ref.shape[1:]
    peers = lent_ref.shape[1]
    leaves = seg_ref.shape[0] // 8
    copies = []
    for q in range(bricks):
        for k in range(slots):
            rows = pl.ds(pl.multiple_of(ship_ref[0, k, q] * 8, 8), 8)
            copies.append(
                pltpu.make_async_copy(seg_ref.at[rows, :], out_ref.at[q, 8 * k : 8 * k + 8, :], sems.at[q, k])
            )
            copies[-1].start()
    brick = lax.axis_index("brick")
    region = lax.axis_index("region")
    mine = leaves + brick * slots

    def local_id(e):
        ghost = e - mine
        is_mine = (ghost >= 0) & (ghost < slots)
        return jnp.where(is_mine, ship_ref[0, jnp.where(is_mine, ghost, 0), brick], e)

    def file_tile(a, b, carry):
        near, far = carry
        a, b = local_id(a), local_id(b)
        code = lax.shift_left(a, SHIFT) | b
        is_near = (a < leaves) & (b < leaves)
        near_ref[near] = code
        list_ref[HEAD + far] = code
        step = is_near.astype(jnp.int32)
        return near + step, far + 1 - step

    carry = lax.fori_loop(
        0, count_ref[0, 0], lambda k, c: file_tile(kept_ref[0, 0, k], kept_ref[0, 1, k], c), (0, 0)
    )
    for j in range(peers):
        carry = lax.fori_loop(
            0, plan_ref[0, region, j], lambda k, c: file_tile(lent_ref[0, j, 0, k], lent_ref[0, j, 1, k], c), carry
        )
    near, far = carry

    def append(k, carry):
        list_ref[HEAD + far + k] = near_ref[k]
        return carry

    lax.fori_loop(0, near, append, 0)
    list_ref[0] = near + far
    list_ref[1] = near
    for copy in copies:
        copy.wait()


def tile_kernel(
    list_ref, other_in, seg_ref, ghost_ref, guest_ref, own_ref, back_ref, loan_ref, other_ref, sem, acc, feat, left, right, *scratch
):
    own_rows = seg_ref.shape[0]
    leaves = own_rows // 8
    ghosts = ghost_ref.shape[0] // 8
    ext = leaves + ghosts
    bricks = back_ref.shape[0]
    slots = ghosts // bricks
    last = list_ref.shape[0] - 1
    fetch = pltpu.make_async_copy(other_in, other_ref, sem)
    fetch.start()
    acc[...] = jnp.zeros_like(acc)
    write_blocks(seg_ref, feat, left, right, 0, leaves)
    write_blocks(ghost_ref, feat, left, right, leaves, ghosts)
    fetch.wait()
    excess = list_ref[0] - other_ref[0]
    give = jnp.minimum(lax.shift_right_arithmetic(jnp.maximum(excess, 0), 1), list_ref[1])
    take = jnp.minimum(lax.shift_right_arithmetic(jnp.maximum(-excess, 0), 1), other_ref[1])
    keep = list_ref[0] - give
    borrowed = HEAD + other_ref[0] - take - keep
    guest_code = (ext << SHIFT) | ext
    dummy_code = ((ext + leaves) << SHIFT) | (ext + leaves)

    def code_at(n):
        kept = list_ref[jnp.minimum(HEAD + n, last)]
        lent = other_ref[jnp.clip(borrowed + n, 0, last)] + guest_code
        return jnp.where(n < keep, kept, jnp.where(n < keep + take, lent, dummy_code))

    @pl.when(take > 0)
    def _():
        write_blocks(guest_ref, feat, left, right, ext, leaves)

    run_tiles((feat, left, right), scratch, acc, code_at, keep + take)
    own_ref[...] = acc[0:own_rows, :]
    loan_ref[...] = acc[8 * ext : 8 * ext + own_rows, :]
    for q in range(bricks):
        for k in range(slots):
            row = own_rows + 8 * (q * slots + k)
            back_ref[q, 6 * k : 6 * k + 6, :] = acc[row : row + 6, :]


def stride_rows(first, count, row, stride):
    return pl.ds(first * stride + row, count, stride=stride)


def finish_kernel(ship_ref, seg_ref, own_ref, loan_ref, back_ref, out_ref, acc):
    leaves = seg_ref.shape[0] // 8
    slots, bricks = ship_ref.shape[1:]
    acc[...] = own_ref[...] + loan_ref[...]
    for q in range(bricks):
        for k in range(slots):
            row = pl.multiple_of(ship_ref[0, k, q] * 8, 8)
            acc[pl.ds(row, 6), :] += back_ref[q, 6 * k : 6 * k + 6, :]
    for c in range(0, leaves, 8):
        d = [seg_ref[stride_rows(c, 8, 3 + q, 8), :] for q in range(3)]
        force = [acc[stride_rows(c, 8, q, 8), :] for q in range(3)]
        lever = [acc[stride_rows(c, 8, 3 + q, 8), :] for q in range(3)]
        squared = d[0] * d[0] + d[1] * d[1] + d[2] * d[2]
        inverse = lax.rsqrt(squared)
        half = 0.5 * squared * inverse
        unit = [x * inverse for x in d]
        m = [x - half * y for x, y in zip(lever, force)]
        for q in range(3):
            i, j = (q + 1) % 3, (q + 2) % 3
            out_ref[q, c : c + 8, :] = force[q]
            out_ref[3 + q, c : c + 8, :] = unit[i] * m[j] - unit[j] * m[i]


def body(segments, ship_list, kept_tiles, kept_count, lent_tiles, lent_count):
    leaves = segments.shape[0]
    bricks, slots = ship_list.shape[1:]
    keep = kept_tiles.shape[1]
    peers, lend = lent_tiles.shape[1:3]
    ghosts = bricks * slots
    ext = leaves + ghosts
    cap = -(-(HEAD + keep + peers * lend + 1) // 128) * 128
    ship = jnp.transpose(ship_list, (0, 2, 1))
    kept = jnp.transpose(kept_tiles, (0, 2, 1))
    lent = jnp.transpose(lent_tiles, (0, 1, 3, 2))
    flat = segments.reshape(leaves * 8, 128)
    smem = pl.BlockSpec(memory_space=pltpu.SMEM)
    vmem = pl.BlockSpec(memory_space=pltpu.VMEM)
    tile_list = jax.ShapeDtypeStruct((cap,), jnp.int32)
    own_sums = jax.ShapeDtypeStruct((leaves * 8, 128), F32)

    def on_chip(x):
        return pltpu.with_memory_space_constraint(x, pltpu.VMEM)

    hbm = pl.BlockSpec(memory_space=pl.ANY)
    outgoing, tiles = pl.pallas_call(
        plan_kernel,
        out_shape=[jax.ShapeDtypeStruct((bricks, slots * 8, 128), F32), tile_list],
        in_specs=[smem, smem, vmem, smem, smem, hbm],
        out_specs=[hbm, smem],
        scratch_shapes=[pltpu.SMEM((cap,), jnp.int32), pltpu.SemaphoreType.DMA((bricks, slots))],
        name="ship_and_plan",
    )(ship, kept, kept_count.reshape(1, 1), lent, lent_count, flat)
    incoming = lax.all_to_all(outgoing, "brick", split_axis=0, concat_axis=0, tiled=True)
    partner = [(r, r ^ 1) for r in range(lax.axis_size("region"))]
    guests = lax.ppermute(flat, "region", partner)
    other_tiles = lax.ppermute(tiles, "region", partner)
    own, back, loan = pl.pallas_call(
        tile_kernel,
        out_shape=[
            pltpu.VMEM(own_sums.shape, F32),
            jax.ShapeDtypeStruct((bricks, slots * 6, 128), F32),
            pltpu.VMEM(own_sums.shape, F32),
        ],
        in_specs=[smem, vmem, vmem, vmem, vmem],
        out_specs=[vmem, vmem, vmem],
        scratch_shapes=[
            pltpu.SMEM((cap,), jnp.int32),
            pltpu.SemaphoreType.DMA(()),
            pltpu.VMEM(((ext + leaves + 1) * 8, 128), F32),
            *block_arrays(ext + leaves + 1),
            *tile_scratch(),
        ],
        name="all_tiles",
    )(tiles, on_chip(other_tiles), on_chip(flat), on_chip(incoming.reshape(ghosts * 8, 128)), on_chip(guests))
    repaid = lax.ppermute(loan, "region", partner)
    returned = lax.all_to_all(back, "brick", split_axis=0, concat_axis=0, tiled=True)
    loads = pl.pallas_call(
        finish_kernel,
        out_shape=jax.ShapeDtypeStruct((6, leaves, 128), F32),
        in_specs=[smem, vmem, vmem, vmem, vmem],
        out_specs=vmem,
        scratch_shapes=[pltpu.VMEM((leaves * 8, 128), F32)],
        name="finish",
    )(ship, on_chip(flat), on_chip(own), on_chip(repaid), on_chip(returned))
    return jnp.transpose(loads, (1, 0, 2))


def solution(mesh):
    placed = (
        P(("brick", "region"), None, None),
        P(("brick", "region"), None, None),
        P(("brick", "region"), None, None),
        P(("brick", "region")),
        P(("brick", "region"), None, None, None),
        P("brick", None, None),
    )
    return jax.shard_map(
        body,
        mesh=mesh,
        in_specs=placed,
        out_specs=P(("brick", "region"), None, None),
        check_vma=False,
    )
```

```python
import functools

import jax
import jax.numpy as jnp
from jax import lax
from jax.experimental import pallas as pl
from jax.experimental.pallas import tpu as pltpu
from jax.sharding import PartitionSpec as P

DIST_FLOOR = 0.0025
PARALLEL_FLOOR = 0.05
TINY = 1e-20
STAND_IN = 1e-30
SHIFT = 10
F32 = jnp.float32
BF16 = jnp.bfloat16

GROUPS = 12
DEPTH = 8 * GROUPS
RIGHT_ROWS = 8 * (3 * 6 + 7 * 4)
OUTS = 13
PLACES = [{0: 3 * n, 1: 3 * n + 1, 2: 3 * n + 2} for n in range(3)] + [{}, {}, {}, {}, {}, {}]
for _n in range(7):
    PLACES[2 + _n].update({4: 9 + 2 * _n, 5: 10 + 2 * _n})
PLACES += [{}] * 4
HEAD = 8
BATCH = 4
PREP = 8


def parts(x):
    first = x.astype(BF16).astype(F32)
    rest = x - first
    second = rest.astype(BF16).astype(F32)
    return first, second, rest - second


def write_blocks(src, feat, left, right, first, blocks):
    row = lax.broadcasted_iota(jnp.int32, (8, 128), 0)
    is_dir = (row >= 3) & (row < 6)
    one = jnp.ones((8, 128), F32)
    zero = jnp.zeros((8, 128), F32)

    def pick(mask, x):
        return jnp.where(mask, x, 0.0)

    def total(x):
        return jnp.broadcast_to(jnp.sum(x, axis=0, keepdims=True), (8, 128))

    def spread(x, r):
        return jnp.broadcast_to(x[r : r + 1, :], (8, 128))

    def one_block(n):
        x = src[pl.ds(pl.multiple_of(n * 8, 8), 8), :]
        squared = total(pick(is_dir, x * x))
        inverse = lax.rsqrt(squared)
        pose = jnp.where(is_dir, x * inverse, pick(row < 3, x))
        along = total(pick(is_dir, pose * pltpu.roll(pose, 3, 0)))
        length = squared * inverse
        flipped = 1.0 / jnp.where(x == 0.0, STAND_IN, x)
        single = pick(row == 4, length)
        for r, value in ((3, spread(flipped, 6)), (2, 0.75 * spread(flipped, 7)), (1, spread(x, 6)), (0, along)):
            single = jnp.where(row == r, value, single)
        at = first + n
        feat[pl.ds(pl.multiple_of(at * 8, 8), 8), :] = jnp.where(row == 3, length, pltpu.roll(pose, 5, 0))
        p, q = parts(pose), parts(single)
        stack = jnp.concatenate([p[0], p[0], p[0], p[1], p[1], p[2], *q, one, one, one], axis=0)
        left[pl.ds(pl.multiple_of(at * 128, 128), 128), 0:DEPTH] = jnp.transpose(stack.astype(BF16))
        halves = []
        for three in (
            [pick(is_dir, y) for y in p],
            [pick(is_dir, -pltpu.roll(y, 3, 0)) for y in p],
            [pick(row < 3, pltpu.roll(y, 5, 0)) for y in p],
        ):
            halves += [three[m] for m in (0, 1, 2, 0, 1, 0)]
        for source, r in ((q, 0), (p, 0), (p, 1), (p, 2)):
            halves += [zero] + [pick(row == r, -y) for y in source]
        for r in (1, 2, 3):
            halves += [jnp.where(row == r, 1.0, 0.0)] + [pick(row == r, y) for y in q]
        right[pl.ds(pl.multiple_of(at * RIGHT_ROWS, 16), RIGHT_ROWS), :] = jnp.concatenate(halves, axis=0).astype(BF16)

    def step(n, carry):
        for u in range(PREP):
            one_block(n * PREP + u)
        return carry

    lax.fori_loop(0, blocks // PREP, step, 0)


def write_template(fixed):
    row = lax.broadcasted_iota(jnp.int32, (DEPTH, 128), 0)
    picks = [[], [48, 56, 64], []]
    picks += [[k, 24 + k, 40 + k] for k in range(3)]
    picks += [[48 + n, 56 + n, 64 + n] for n in (1, 2, 3)]
    picks += [[3 + k, 27 + k, 43 + k] for k in range(3)]
    picks += [[52, 60, 68]]
    for n, chosen in enumerate(picks):
        hit = jnp.zeros((DEPTH, 128), jnp.bool_)
        for r in chosen:
            hit = hit | (row == r)
        fixed[:, 128 * n : 128 * (n + 1)] = jnp.where(hit, 1.0, 0.0).astype(BF16)


def products(left, right, fixed, prod, pair):
    ia, ib = pair
    a = left[pl.ds(pl.multiple_of(ia * 128, 128), 128), 0:DEPTH]
    mine = right[pl.ds(pl.multiple_of(ib * RIGHT_ROWS, 16), RIGHT_ROWS), :]

    def column(n):
        places = PLACES[n]
        rows = []
        for k in range(GROUPS // 2):
            if k in places:
                rows.append(mine[16 * places[k] : 16 * places[k] + 16, :])
            else:
                rows.append(fixed[16 * k : 16 * k + 16, 128 * n : 128 * (n + 1)])
        return jnp.concatenate(rows, axis=0)

    for low in range(0, OUTS, 2):
        high = min(low + 2, OUTS)
        b = jnp.concatenate([column(n) for n in range(low, high)], axis=1)
        prod[:, 128 * low : 128 * high] = lax.dot_general(
            a, b, (((1,), (0,)), ((), ())), preferred_element_type=F32
        )


def pair_sums(feat, prod, part, ib):
    ux2, uy2, uz2, len2 = (jnp.broadcast_to(feat[pl.ds(ib * 8 + q, 1), :], (8, 128)) for q in range(4))
    sums = None
    for g in range(16):
        rows = slice(8 * g, 8 * g + 8)
        w, c, f, ox, oy, oz, reach, compliance, curvature, ux1, uy1, uz1, len1 = (
            prod[rows, 128 * n : 128 * (n + 1)] for n in range(OUTS)
        )
        inverse = pl.reciprocal(jnp.maximum(1.0 - w * w, PARALLEL_FLOOR))
        s = jnp.minimum(jnp.maximum((w * f - c) * inverse, 0.0), len1)
        t = jnp.minimum(jnp.maximum(w * s + f, 0.0), len2)
        s = jnp.minimum(jnp.maximum(w * t - c, 0.0), len1)
        gx = ox + s * ux1 - t * ux2
        gy = oy + s * uy1 - t * uy2
        gz = oz + s * uz1 - t * uz2
        square = jnp.maximum(gx * gx + gy * gy + gz * gz, DIST_FLOOR)
        near = lax.rsqrt(square)
        depth = jnp.maximum(reach - square * near, TINY)
        root = lax.rsqrt(depth * curvature)
        scale = (depth * root) * (depth * near) * pl.reciprocal(compliance)
        force = [scale * gx, scale * gy, scale * gz]
        on_a = force + [s * x for x in force]
        on_b = force + [t * x for x in force]
        for q in range(6):
            part[rows, q : q + 1] = jnp.sum(on_a[q], axis=1, keepdims=True)
        sums = on_b if sums is None else [x + y for x, y in zip(sums, on_b)]
    return jnp.concatenate([jnp.sum(x, axis=0, keepdims=True) for x in sums] + [jnp.zeros((2, 128), F32)], axis=0)


def block_arrays(blocks):
    return [
        pltpu.VMEM((blocks * 8, 128), F32),
        pltpu.VMEM((blocks * 128, 128), BF16),
        pltpu.VMEM((blocks * RIGHT_ROWS, 128), BF16),
    ]


def tile_scratch():
    return [
        pltpu.VMEM((DEPTH, OUTS * 128), BF16),
        *[pltpu.VMEM((128, OUTS * 128), F32)] * (2 * BATCH),
        *[pltpu.VMEM((128, 128), F32)] * (2 * BATCH),
        *[pltpu.VMEM((8, 128), F32)] * (2 * BATCH),
    ]


def run_tiles(blocks, scratch, acc, code_at, count):
    feat, left, right = blocks
    fixed = scratch[0]
    prods, sums_a, sums_b = (scratch[1 + 2 * BATCH * k : 1 + 2 * BATCH * (k + 1)] for k in range(3))
    write_template(fixed)
    for ref in (*sums_a, *sums_b):
        ref[...] = jnp.zeros_like(ref)

    def ids(n):
        code = code_at(n)
        return lax.shift_right_logical(code, SHIFT), code & ((1 << SHIFT) - 1)

    def collect(first, side):
        for u in range(BATCH):
            ia, ib = ids(jnp.maximum(first + u, 0))
            slot = side * BATCH + u
            acc[pl.ds(pl.multiple_of(ia * 8, 8), 8), :] += jnp.transpose(sums_a[slot][...])[0:8, :]
            acc[pl.ds(pl.multiple_of(ib * 8, 8), 8), :] -= sums_b[slot][...]

    def prepare(first, side):
        for u in range(BATCH):
            products(left, right, fixed, prods[side * BATCH + u], ids(first + u))

    def batch(first, side):
        collect(first - BATCH, 1 - side)
        prepare(first + BATCH, 1 - side)
        for u in range(BATCH):
            slot = side * BATCH + u
            sums_b[slot][...] = pair_sums(feat, prods[slot], sums_a[slot], ids(first + u)[1])

    prepare(0, 0)

    def step(n, carry):
        first = 2 * BATCH * n
        batch(first, 0)

        @pl.when(first + BATCH < count)
        def _():
            batch(first + BATCH, 1)

        return carry

    lax.fori_loop(0, (count + 2 * BATCH - 1) // (2 * BATCH), step, 0)
    batches = (count + BATCH - 1) // BATCH

    @pl.when((batches & 1) == 1)
    def _():
        collect((batches - 1) * BATCH, 0)

    @pl.when((batches > 0) & ((batches & 1) == 0))
    def _():
        collect((batches - 1) * BATCH, 1)


def gather_kernel(ship_ref, seg_ref, out_ref):
    slots, bricks = ship_ref.shape[1:]
    for q in range(bricks):
        for k in range(slots):
            out_ref[q, 8 * k : 8 * k + 8, :] = seg_ref[pl.ds(pl.multiple_of(ship_ref[0, k, q] * 8, 8), 8), :]


def plan_kernel(leaves, ship_ref, kept_ref, count_ref, lent_ref, plan_ref, list_ref, near_ref):
    slots, bricks = ship_ref.shape[1:]
    peers = lent_ref.shape[1]
    brick = lax.axis_index("brick")
    region = lax.axis_index("region")
    mine = leaves + brick * slots

    def local_id(e):
        ghost = e - mine
        is_mine = (ghost >= 0) & (ghost < slots)
        return jnp.where(is_mine, ship_ref[0, jnp.where(is_mine, ghost, 0), brick], e)

    def file_tile(a, b, carry):
        near, far = carry
        a, b = local_id(a), local_id(b)
        code = lax.shift_left(a, SHIFT) | b
        is_near = (a < leaves) & (b < leaves)
        near_ref[near] = code
        list_ref[HEAD + far] = code
        step = is_near.astype(jnp.int32)
        return near + step, far + 1 - step

    carry = lax.fori_loop(
        0, count_ref[0], lambda k, c: file_tile(kept_ref[0, 0, k], kept_ref[0, 1, k], c), (0, 0)
    )
    for j in range(peers):
        carry = lax.fori_loop(
            0, plan_ref[0, region, j], lambda k, c: file_tile(lent_ref[0, j, 0, k], lent_ref[0, j, 1, k], c), carry
        )
    near, far = carry

    def append(k, carry):
        list_ref[HEAD + far + k] = near_ref[k]
        return carry

    lax.fori_loop(0, near, append, 0)
    list_ref[0] = near + far
    list_ref[1] = near


def tile_kernel(
    list_ref, other_in, seg_ref, ghost_ref, guest_ref, own_ref, back_ref, loan_ref, other_ref, sem, acc, feat, left, right, *scratch
):
    own_rows = seg_ref.shape[0]
    leaves = own_rows // 8
    ghosts = ghost_ref.shape[0] // 8
    ext = leaves + ghosts
    bricks = back_ref.shape[0]
    slots = ghosts // bricks
    last = list_ref.shape[0] - 1
    fetch = pltpu.make_async_copy(other_in, other_ref, sem)
    fetch.start()
    acc[...] = jnp.zeros_like(acc)
    write_blocks(seg_ref, feat, left, right, 0, leaves)
    write_blocks(ghost_ref, feat, left, right, leaves, ghosts)
    fetch.wait()
    excess = list_ref[0] - other_ref[0]
    give = jnp.minimum(lax.shift_right_arithmetic(jnp.maximum(excess, 0), 1), list_ref[1])
    take = jnp.minimum(lax.shift_right_arithmetic(jnp.maximum(-excess, 0), 1), other_ref[1])
    keep = list_ref[0] - give
    borrowed = HEAD + other_ref[0] - take - keep
    guest_code = (ext << SHIFT) | ext
    dummy_code = ((ext + leaves) << SHIFT) | (ext + leaves)

    def code_at(n):
        kept = list_ref[jnp.minimum(HEAD + n, last)]
        lent = other_ref[jnp.clip(borrowed + n, 0, last)] + guest_code
        return jnp.where(n < keep, kept, jnp.where(n < keep + take, lent, dummy_code))

    @pl.when(take > 0)
    def _():
        write_blocks(guest_ref, feat, left, right, ext, leaves)

    run_tiles((feat, left, right), scratch, acc, code_at, keep + take)
    own_ref[...] = acc[0:own_rows, :]
    loan_ref[...] = acc[8 * ext : 8 * ext + own_rows, :]
    for q in range(bricks):
        for k in range(slots):
            row = own_rows + 8 * (q * slots + k)
            back_ref[q, 6 * k : 6 * k + 6, :] = acc[row : row + 6, :]


def stride_rows(first, count, row, stride):
    return pl.ds(first * stride + row, count, stride=stride)


def finish_kernel(ship_ref, seg_ref, own_ref, loan_ref, back_ref, out_ref, acc):
    leaves = seg_ref.shape[0] // 8
    slots, bricks = ship_ref.shape[1:]
    acc[...] = own_ref[...] + loan_ref[...]
    for q in range(bricks):
        for k in range(slots):
            row = pl.multiple_of(ship_ref[0, k, q] * 8, 8)
            acc[pl.ds(row, 6), :] += back_ref[q, 6 * k : 6 * k + 6, :]
    for c in range(0, leaves, 8):
        d = [seg_ref[stride_rows(c, 8, 3 + q, 8), :] for q in range(3)]
        force = [acc[stride_rows(c, 8, q, 8), :] for q in range(3)]
        lever = [acc[stride_rows(c, 8, 3 + q, 8), :] for q in range(3)]
        squared = d[0] * d[0] + d[1] * d[1] + d[2] * d[2]
        inverse = lax.rsqrt(squared)
        half = 0.5 * squared * inverse
        unit = [x * inverse for x in d]
        m = [x - half * y for x, y in zip(lever, force)]
        for q in range(3):
            i, j = (q + 1) % 3, (q + 2) % 3
            out_ref[q, c : c + 8, :] = force[q]
            out_ref[3 + q, c : c + 8, :] = unit[i] * m[j] - unit[j] * m[i]


def body(segments, ship_list, kept_tiles, kept_count, lent_tiles, lent_count):
    leaves = segments.shape[0]
    bricks, slots = ship_list.shape[1:]
    keep = kept_tiles.shape[1]
    peers, lend = lent_tiles.shape[1:3]
    ghosts = bricks * slots
    ext = leaves + ghosts
    cap = -(-(HEAD + keep + peers * lend + 1) // 128) * 128
    ship = jnp.transpose(ship_list, (0, 2, 1))
    kept = jnp.transpose(kept_tiles, (0, 2, 1))
    lent = jnp.transpose(lent_tiles, (0, 1, 3, 2))
    flat = segments.reshape(leaves * 8, 128)
    smem = pl.BlockSpec(memory_space=pltpu.SMEM)
    vmem = pl.BlockSpec(memory_space=pltpu.VMEM)
    tile_list = jax.ShapeDtypeStruct((cap,), jnp.int32)
    own_sums = jax.ShapeDtypeStruct((leaves * 8, 128), F32)

    def on_chip(x):
        return pltpu.with_memory_space_constraint(x, pltpu.VMEM)

    outgoing = pl.pallas_call(
        gather_kernel,
        out_shape=jax.ShapeDtypeStruct((bricks, slots * 8, 128), F32),
        in_specs=[smem, vmem],
        out_specs=vmem,
        name="ship_gather",
    )(ship, flat)
    incoming = lax.all_to_all(outgoing, "brick", split_axis=0, concat_axis=0, tiled=True)
    partner = [(r, r ^ 1) for r in range(lax.axis_size("region"))]
    guests = lax.ppermute(flat, "region", partner)
    tiles = pl.pallas_call(
        functools.partial(plan_kernel, leaves),
        out_shape=tile_list,
        in_specs=[smem] * 5,
        out_specs=smem,
        scratch_shapes=[pltpu.SMEM((cap,), jnp.int32)],
        name="plan_tiles",
    )(ship, kept, kept_count, lent, lent_count)
    other_tiles = lax.ppermute(tiles, "region", partner)
    own, back, loan = pl.pallas_call(
        tile_kernel,
        out_shape=[
            pltpu.VMEM(own_sums.shape, F32),
            jax.ShapeDtypeStruct((bricks, slots * 6, 128), F32),
            pltpu.VMEM(own_sums.shape, F32),
        ],
        in_specs=[smem, vmem, vmem, vmem, vmem],
        out_specs=[vmem, vmem, vmem],
        scratch_shapes=[
            pltpu.SMEM((cap,), jnp.int32),
            pltpu.SemaphoreType.DMA(()),
            pltpu.VMEM(((ext + leaves + 1) * 8, 128), F32),
            *block_arrays(ext + leaves + 1),
            *tile_scratch(),
        ],
        name="all_tiles",
    )(tiles, on_chip(other_tiles), on_chip(flat), on_chip(incoming.reshape(ghosts * 8, 128)), on_chip(guests))
    repaid = lax.ppermute(loan, "region", partner)
    returned = lax.all_to_all(back, "brick", split_axis=0, concat_axis=0, tiled=True)
    loads = pl.pallas_call(
        finish_kernel,
        out_shape=jax.ShapeDtypeStruct((6, leaves, 128), F32),
        in_specs=[smem, vmem, vmem, vmem, vmem],
        out_specs=vmem,
        scratch_shapes=[pltpu.VMEM((leaves * 8, 128), F32)],
        name="finish",
    )(ship, on_chip(flat), on_chip(own), on_chip(repaid), on_chip(returned))
    return jnp.transpose(loads, (1, 0, 2))


def solution(mesh):
    placed = (
        P(("brick", "region"), None, None),
        P(("brick", "region"), None, None),
        P(("brick", "region"), None, None),
        P(("brick", "region")),
        P(("brick", "region"), None, None, None),
        P("brick", None, None),
    )
    return jax.shard_map(
        body,
        mesh=mesh,
        in_specs=placed,
        out_specs=P(("brick", "region"), None, None),
        check_vma=False,
    )
```

```python
import functools

import jax
import jax.numpy as jnp
from jax import lax
from jax.experimental import pallas as pl
from jax.experimental.pallas import tpu as pltpu
from jax.sharding import PartitionSpec as P

DIST_FLOOR = 0.0025
PARALLEL_FLOOR = 0.05
TINY = 1e-20
STAND_IN = 1e-30
SHIFT = 10
F32 = jnp.float32
BF16 = jnp.bfloat16

GROUPS = 12
DEPTH = 8 * GROUPS
RIGHT_ROWS = 8 * (3 * 6 + 7 * 4)
OUTS = 13
PLACES = [{0: 3 * n, 1: 3 * n + 1, 2: 3 * n + 2} for n in range(3)] + [{}, {}, {}, {}, {}, {}]
for _n in range(7):
    PLACES[2 + _n].update({4: 9 + 2 * _n, 5: 10 + 2 * _n})
PLACES += [{}] * 4
HEAD = 8
LOAN_COST = 3
BATCH = 4
PREP = 8


def parts(x):
    first = x.astype(BF16).astype(F32)
    rest = x - first
    second = rest.astype(BF16).astype(F32)
    return first, second, rest - second


def write_blocks(src, feat, left, right, first, blocks):
    row = lax.broadcasted_iota(jnp.int32, (8, 128), 0)
    is_dir = (row >= 3) & (row < 6)
    one = jnp.ones((8, 128), F32)
    zero = jnp.zeros((8, 128), F32)

    def pick(mask, x):
        return jnp.where(mask, x, 0.0)

    def total(x):
        return jnp.broadcast_to(jnp.sum(x, axis=0, keepdims=True), (8, 128))

    def spread(x, r):
        return jnp.broadcast_to(x[r : r + 1, :], (8, 128))

    def one_block(n):
        x = src[pl.ds(pl.multiple_of(n * 8, 8), 8), :]
        squared = total(pick(is_dir, x * x))
        inverse = lax.rsqrt(squared)
        pose = jnp.where(is_dir, x * inverse, pick(row < 3, x))
        along = total(pick(is_dir, pose * pltpu.roll(pose, 3, 0)))
        length = squared * inverse
        flipped = 1.0 / jnp.where(x == 0.0, STAND_IN, x)
        single = pick(row == 4, length)
        for r, value in ((3, spread(flipped, 6)), (2, 0.75 * spread(flipped, 7)), (1, spread(x, 6)), (0, along)):
            single = jnp.where(row == r, value, single)
        at = first + n
        feat[pl.ds(pl.multiple_of(at * 8, 8), 8), :] = jnp.where(row == 3, length, pltpu.roll(pose, 5, 0))
        p, q = parts(pose), parts(single)
        stack = jnp.concatenate([p[0], p[0], p[0], p[1], p[1], p[2], *q, one, one, one], axis=0)
        left[pl.ds(pl.multiple_of(at * 128, 128), 128), 0:DEPTH] = jnp.transpose(stack.astype(BF16))
        halves = []
        for three in (
            [pick(is_dir, y) for y in p],
            [pick(is_dir, -pltpu.roll(y, 3, 0)) for y in p],
            [pick(row < 3, pltpu.roll(y, 5, 0)) for y in p],
        ):
            halves += [three[m] for m in (0, 1, 2, 0, 1, 0)]
        for source, r in ((q, 0), (p, 0), (p, 1), (p, 2)):
            halves += [zero] + [pick(row == r, -y) for y in source]
        for r in (1, 2, 3):
            halves += [jnp.where(row == r, 1.0, 0.0)] + [pick(row == r, y) for y in q]
        right[pl.ds(pl.multiple_of(at * RIGHT_ROWS, 16), RIGHT_ROWS), :] = jnp.concatenate(halves, axis=0).astype(BF16)

    def step(n, carry):
        for u in range(PREP):
            one_block(n * PREP + u)
        return carry

    lax.fori_loop(0, blocks // PREP, step, 0)


def write_template(fixed):
    row = lax.broadcasted_iota(jnp.int32, (DEPTH, 128), 0)
    picks = [[], [48, 56, 64], []]
    picks += [[k, 24 + k, 40 + k] for k in range(3)]
    picks += [[48 + n, 56 + n, 64 + n] for n in (1, 2, 3)]
    picks += [[3 + k, 27 + k, 43 + k] for k in range(3)]
    picks += [[52, 60, 68]]
    for n, chosen in enumerate(picks):
        hit = jnp.zeros((DEPTH, 128), jnp.bool_)
        for r in chosen:
            hit = hit | (row == r)
        fixed[:, 128 * n : 128 * (n + 1)] = jnp.where(hit, 1.0, 0.0).astype(BF16)


def products(left, right, fixed, prod, pair):
    ia, ib = pair
    a = left[pl.ds(pl.multiple_of(ia * 128, 128), 128), 0:DEPTH]
    mine = right[pl.ds(pl.multiple_of(ib * RIGHT_ROWS, 16), RIGHT_ROWS), :]

    def column(n):
        places = PLACES[n]
        rows = []
        for k in range(GROUPS // 2):
            if k in places:
                rows.append(mine[16 * places[k] : 16 * places[k] + 16, :])
            else:
                rows.append(fixed[16 * k : 16 * k + 16, 128 * n : 128 * (n + 1)])
        return jnp.concatenate(rows, axis=0)

    for low in range(0, OUTS, 2):
        high = min(low + 2, OUTS)
        b = jnp.concatenate([column(n) for n in range(low, high)], axis=1)
        prod[:, 128 * low : 128 * high] = lax.dot_general(
            a, b, (((1,), (0,)), ((), ())), preferred_element_type=F32
        )


def pair_sums(feat, prod, part, ib):
    ux2, uy2, uz2, len2 = (jnp.broadcast_to(feat[pl.ds(ib * 8 + q, 1), :], (8, 128)) for q in range(4))
    sums = None
    for g in range(16):
        rows = slice(8 * g, 8 * g + 8)
        w, c, f, ox, oy, oz, reach, compliance, curvature, ux1, uy1, uz1, len1 = (
            prod[rows, 128 * n : 128 * (n + 1)] for n in range(OUTS)
        )
        inverse = pl.reciprocal(jnp.maximum(1.0 - w * w, PARALLEL_FLOOR))
        s = jnp.minimum(jnp.maximum((w * f - c) * inverse, 0.0), len1)
        t = jnp.minimum(jnp.maximum(w * s + f, 0.0), len2)
        s = jnp.minimum(jnp.maximum(w * t - c, 0.0), len1)
        gx = ox + s * ux1 - t * ux2
        gy = oy + s * uy1 - t * uy2
        gz = oz + s * uz1 - t * uz2
        square = jnp.maximum(gx * gx + gy * gy + gz * gz, DIST_FLOOR)
        near = lax.rsqrt(square)
        depth = jnp.maximum(reach - square * near, TINY)
        root = lax.rsqrt(depth * curvature)
        scale = (depth * root) * (depth * near) * pl.reciprocal(compliance)
        force = [scale * gx, scale * gy, scale * gz]
        on_a = force + [s * x for x in force]
        on_b = force + [t * x for x in force]
        for q in range(6):
            part[rows, q : q + 1] = jnp.sum(on_a[q], axis=1, keepdims=True)
        sums = on_b if sums is None else [x + y for x, y in zip(sums, on_b)]
    return jnp.concatenate([jnp.sum(x, axis=0, keepdims=True) for x in sums] + [jnp.zeros((2, 128), F32)], axis=0)


def block_arrays(blocks):
    return [
        pltpu.VMEM((blocks * 8, 128), F32),
        pltpu.VMEM((blocks * 128, 128), BF16),
        pltpu.VMEM((blocks * RIGHT_ROWS, 128), BF16),
    ]


def tile_scratch():
    return [
        pltpu.VMEM((DEPTH, OUTS * 128), BF16),
        *[pltpu.VMEM((128, OUTS * 128), F32)] * (2 * BATCH),
        *[pltpu.VMEM((128, 128), F32)] * (2 * BATCH),
        *[pltpu.VMEM((8, 128), F32)] * (2 * BATCH),
    ]


def run_tiles(blocks, scratch, acc, code_at, count):
    feat, left, right = blocks
    fixed = scratch[0]
    prods, sums_a, sums_b = (scratch[1 + 2 * BATCH * k : 1 + 2 * BATCH * (k + 1)] for k in range(3))
    write_template(fixed)
    for ref in (*sums_a, *sums_b):
        ref[...] = jnp.zeros_like(ref)

    def ids(n):
        code = code_at(n)
        return lax.shift_right_logical(code, SHIFT), code & ((1 << SHIFT) - 1)

    def collect(first, side):
        for u in range(BATCH):
            ia, ib = ids(jnp.maximum(first + u, 0))
            slot = side * BATCH + u
            acc[pl.ds(pl.multiple_of(ia * 8, 8), 8), :] += jnp.transpose(sums_a[slot][...])[0:8, :]
            acc[pl.ds(pl.multiple_of(ib * 8, 8), 8), :] -= sums_b[slot][...]

    def prepare(first, side):
        for u in range(BATCH):
            products(left, right, fixed, prods[side * BATCH + u], ids(first + u))

    def batch(first, side):
        collect(first - BATCH, 1 - side)
        prepare(first + BATCH, 1 - side)
        for u in range(BATCH):
            slot = side * BATCH + u
            sums_b[slot][...] = pair_sums(feat, prods[slot], sums_a[slot], ids(first + u)[1])

    prepare(0, 0)

    def step(n, carry):
        first = 2 * BATCH * n
        batch(first, 0)

        @pl.when(first + BATCH < count)
        def _():
            batch(first + BATCH, 1)

        return carry

    lax.fori_loop(0, (count + 2 * BATCH - 1) // (2 * BATCH), step, 0)
    batches = (count + BATCH - 1) // BATCH

    @pl.when((batches & 1) == 1)
    def _():
        collect((batches - 1) * BATCH, 0)

    @pl.when((batches > 0) & ((batches & 1) == 0))
    def _():
        collect((batches - 1) * BATCH, 1)


def gather_kernel(ship_ref, seg_ref, out_ref):
    slots, bricks = ship_ref.shape[1:]
    for q in range(bricks):
        for k in range(slots):
            out_ref[q, 8 * k : 8 * k + 8, :] = seg_ref[pl.ds(pl.multiple_of(ship_ref[0, k, q] * 8, 8), 8), :]


def plan_kernel(leaves, ship_ref, kept_ref, count_ref, lent_ref, plan_ref, list_ref, near_ref):
    slots, bricks = ship_ref.shape[1:]
    peers = lent_ref.shape[1]
    brick = lax.axis_index("brick")
    region = lax.axis_index("region")
    mine = leaves + brick * slots

    def local_id(e):
        ghost = e - mine
        is_mine = (ghost >= 0) & (ghost < slots)
        return jnp.where(is_mine, ship_ref[0, jnp.where(is_mine, ghost, 0), brick], e)

    def file_tile(a, b, carry):
        near, far = carry
        a, b = local_id(a), local_id(b)
        code = lax.shift_left(a, SHIFT) | b
        is_near = (a < leaves) & (b < leaves)
        near_ref[near] = code
        list_ref[HEAD + far] = code
        step = is_near.astype(jnp.int32)
        return near + step, far + 1 - step

    carry = lax.fori_loop(
        0, count_ref[0], lambda k, c: file_tile(kept_ref[0, 0, k], kept_ref[0, 1, k], c), (0, 0)
    )
    for j in range(peers):
        carry = lax.fori_loop(
            0, plan_ref[0, region, j], lambda k, c: file_tile(lent_ref[0, j, 0, k], lent_ref[0, j, 1, k], c), carry
        )
    near, far = carry

    def append(k, carry):
        list_ref[HEAD + far + k] = near_ref[k]
        return carry

    lax.fori_loop(0, near, append, 0)
    list_ref[0] = near + far
    list_ref[1] = near


def tile_kernel(
    list_ref, other_in, seg_ref, ghost_ref, guest_ref, own_ref, back_ref, loan_ref, other_ref, sem, acc, feat, left, right, *scratch
):
    own_rows = seg_ref.shape[0]
    leaves = own_rows // 8
    ghosts = ghost_ref.shape[0] // 8
    ext = leaves + ghosts
    bricks = back_ref.shape[0]
    slots = ghosts // bricks
    last = list_ref.shape[0] - 1
    fetch = pltpu.make_async_copy(other_in, other_ref, sem)
    fetch.start()
    acc[...] = jnp.zeros_like(acc)
    write_blocks(seg_ref, feat, left, right, 0, leaves)
    write_blocks(ghost_ref, feat, left, right, leaves, ghosts)
    fetch.wait()
    excess = list_ref[0] - other_ref[0]
    give = jnp.minimum(lax.shift_right_arithmetic(jnp.maximum(excess - LOAN_COST, 0), 1), list_ref[1])
    take = jnp.minimum(lax.shift_right_arithmetic(jnp.maximum(-excess - LOAN_COST, 0), 1), other_ref[1])
    keep = list_ref[0] - give
    borrowed = HEAD + other_ref[0] - take - keep
    guest_code = (ext << SHIFT) | ext
    dummy_code = ((ext + leaves) << SHIFT) | (ext + leaves)

    def code_at(n):
        kept = list_ref[jnp.minimum(HEAD + n, last)]
        lent = other_ref[jnp.clip(borrowed + n, 0, last)] + guest_code
        return jnp.where(n < keep, kept, jnp.where(n < keep + take, lent, dummy_code))

    @pl.when(take > 0)
    def _():
        write_blocks(guest_ref, feat, left, right, ext, leaves)

    run_tiles((feat, left, right), scratch, acc, code_at, keep + take)
    own_ref[...] = acc[0:own_rows, :]
    loan_ref[...] = acc[8 * ext : 8 * ext + own_rows, :]
    for q in range(bricks):
        for k in range(slots):
            row = own_rows + 8 * (q * slots + k)
            back_ref[q, 6 * k : 6 * k + 6, :] = acc[row : row + 6, :]


def stride_rows(first, count, row, stride):
    return pl.ds(first * stride + row, count, stride=stride)


def finish_kernel(ship_ref, seg_ref, own_ref, loan_ref, back_ref, out_ref, *accs):
    leaves = seg_ref.shape[0] // 8
    slots, bricks = ship_ref.shape[1:]
    for k, acc in enumerate(accs):
        acc[...] = own_ref[...] if k == 0 else loan_ref[...] if k == 1 else jnp.zeros_like(acc)
    for q in range(bricks):
        for k in range(slots):
            row = pl.multiple_of(ship_ref[0, k, q] * 8, 8)
            accs[k % len(accs)][pl.ds(row, 6), :] += back_ref[q, 6 * k : 6 * k + 6, :]

    def summed(c, q):
        rows = stride_rows(c, 8, q, 8)
        first, second, third, fourth = (acc[rows, :] for acc in accs)
        return (first + second) + (third + fourth)

    for c in range(0, leaves, 8):
        d = [seg_ref[stride_rows(c, 8, 3 + q, 8), :] for q in range(3)]
        force = [summed(c, q) for q in range(3)]
        lever = [summed(c, 3 + q) for q in range(3)]
        squared = d[0] * d[0] + d[1] * d[1] + d[2] * d[2]
        inverse = lax.rsqrt(squared)
        half = 0.5 * squared * inverse
        unit = [x * inverse for x in d]
        m = [x - half * y for x, y in zip(lever, force)]
        for q in range(3):
            i, j = (q + 1) % 3, (q + 2) % 3
            out_ref[q, c : c + 8, :] = force[q]
            out_ref[3 + q, c : c + 8, :] = unit[i] * m[j] - unit[j] * m[i]


def body(segments, ship_list, kept_tiles, kept_count, lent_tiles, lent_count):
    leaves = segments.shape[0]
    bricks, slots = ship_list.shape[1:]
    keep = kept_tiles.shape[1]
    peers, lend = lent_tiles.shape[1:3]
    ghosts = bricks * slots
    ext = leaves + ghosts
    cap = -(-(HEAD + keep + peers * lend + 1) // 128) * 128
    ship = jnp.transpose(ship_list, (0, 2, 1))
    kept = jnp.transpose(kept_tiles, (0, 2, 1))
    lent = jnp.transpose(lent_tiles, (0, 1, 3, 2))
    flat = segments.reshape(leaves * 8, 128)
    smem = pl.BlockSpec(memory_space=pltpu.SMEM)
    vmem = pl.BlockSpec(memory_space=pltpu.VMEM)
    tile_list = jax.ShapeDtypeStruct((cap,), jnp.int32)
    own_sums = jax.ShapeDtypeStruct((leaves * 8, 128), F32)

    def on_chip(x):
        return pltpu.with_memory_space_constraint(x, pltpu.VMEM)

    outgoing = pl.pallas_call(
        gather_kernel,
        out_shape=jax.ShapeDtypeStruct((bricks, slots * 8, 128), F32),
        in_specs=[smem, vmem],
        out_specs=vmem,
        name="ship_gather",
    )(ship, flat)
    incoming = lax.all_to_all(outgoing, "brick", split_axis=0, concat_axis=0, tiled=True)
    partner = [(r, r ^ 1) for r in range(lax.axis_size("region"))]
    guests = lax.ppermute(flat, "region", partner)
    tiles = pl.pallas_call(
        functools.partial(plan_kernel, leaves),
        out_shape=tile_list,
        in_specs=[smem] * 5,
        out_specs=smem,
        scratch_shapes=[pltpu.SMEM((cap,), jnp.int32)],
        name="plan_tiles",
    )(ship, kept, kept_count, lent, lent_count)
    other_tiles = lax.ppermute(tiles, "region", partner)
    own, back, loan = pl.pallas_call(
        tile_kernel,
        out_shape=[
            pltpu.VMEM(own_sums.shape, F32),
            jax.ShapeDtypeStruct((bricks, slots * 6, 128), F32),
            pltpu.VMEM(own_sums.shape, F32),
        ],
        in_specs=[smem, vmem, vmem, vmem, vmem],
        out_specs=[vmem, vmem, vmem],
        scratch_shapes=[
            pltpu.SMEM((cap,), jnp.int32),
            pltpu.SemaphoreType.DMA(()),
            pltpu.VMEM(((ext + leaves + 1) * 8, 128), F32),
            *block_arrays(ext + leaves + 1),
            *tile_scratch(),
        ],
        name="all_tiles",
    )(tiles, on_chip(other_tiles), on_chip(flat), on_chip(incoming.reshape(ghosts * 8, 128)), on_chip(guests))
    repaid = lax.ppermute(loan, "region", partner)
    returned = lax.all_to_all(back, "brick", split_axis=0, concat_axis=0, tiled=True)
    loads = pl.pallas_call(
        finish_kernel,
        out_shape=jax.ShapeDtypeStruct((6, leaves, 128), F32),
        in_specs=[smem, vmem, vmem, vmem, vmem],
        out_specs=vmem,
        scratch_shapes=[pltpu.VMEM((leaves * 8, 128), F32)] * 4,
        name="finish",
    )(ship, on_chip(flat), on_chip(own), on_chip(repaid), on_chip(returned))
    return jnp.transpose(loads, (1, 0, 2))


def solution(mesh):
    placed = (
        P(("brick", "region"), None, None),
        P(("brick", "region"), None, None),
        P(("brick", "region"), None, None),
        P(("brick", "region")),
        P(("brick", "region"), None, None, None),
        P("brick", None, None),
    )
    return jax.shard_map(
        body,
        mesh=mesh,
        in_specs=placed,
        out_specs=P(("brick", "region"), None, None),
        check_vma=False,
    )
```

```python
import functools

import jax
import jax.numpy as jnp
from jax import lax
from jax.experimental import pallas as pl
from jax.experimental.pallas import tpu as pltpu
from jax.sharding import PartitionSpec as P

DIST_FLOOR = 0.0025
PARALLEL_FLOOR = 0.05
TINY = 1e-20
STAND_IN = 1e-30
SHIFT = 10
F32 = jnp.float32
BF16 = jnp.bfloat16

GROUPS = 12
DEPTH = 8 * GROUPS
RIGHT_ROWS = 8 * (3 * 6 + 7 * 4)
OUTS = 13
PLACES = [{0: 3 * n, 1: 3 * n + 1, 2: 3 * n + 2} for n in range(3)] + [{}, {}, {}, {}, {}, {}]
for _n in range(7):
    PLACES[2 + _n].update({4: 9 + 2 * _n, 5: 10 + 2 * _n})
PLACES += [{}] * 4
HEAD = 8
FILED = 4
LOAN_COST = 3
BATCH = 4
PREP = 8


def parts(x):
    first = x.astype(BF16).astype(F32)
    rest = x - first
    second = rest.astype(BF16).astype(F32)
    return first, second, rest - second


def write_blocks(src, feat, left, right, first, blocks):
    row = lax.broadcasted_iota(jnp.int32, (8, 128), 0)
    is_dir = (row >= 3) & (row < 6)
    one = jnp.ones((8, 128), F32)
    zero = jnp.zeros((8, 128), F32)

    def pick(mask, x):
        return jnp.where(mask, x, 0.0)

    def total(x):
        return jnp.broadcast_to(jnp.sum(x, axis=0, keepdims=True), (8, 128))

    def spread(x, r):
        return jnp.broadcast_to(x[r : r + 1, :], (8, 128))

    def one_block(n):
        x = src[pl.ds(pl.multiple_of(n * 8, 8), 8), :]
        squared = total(pick(is_dir, x * x))
        inverse = lax.rsqrt(squared)
        pose = jnp.where(is_dir, x * inverse, pick(row < 3, x))
        along = total(pick(is_dir, pose * pltpu.roll(pose, 3, 0)))
        length = squared * inverse
        flipped = 1.0 / jnp.where(x == 0.0, STAND_IN, x)
        single = pick(row == 4, length)
        for r, value in ((3, spread(flipped, 6)), (2, 0.75 * spread(flipped, 7)), (1, spread(x, 6)), (0, along)):
            single = jnp.where(row == r, value, single)
        at = first + n
        feat[pl.ds(pl.multiple_of(at * 8, 8), 8), :] = jnp.where(row == 3, length, pltpu.roll(pose, 5, 0))
        p, q = parts(pose), parts(single)
        stack = jnp.concatenate([p[0], p[0], p[0], p[1], p[1], p[2], *q, one, one, one], axis=0)
        left[pl.ds(pl.multiple_of(at * 128, 128), 128), 0:DEPTH] = jnp.transpose(stack.astype(BF16))
        halves = []
        for three in (
            [pick(is_dir, y) for y in p],
            [pick(is_dir, -pltpu.roll(y, 3, 0)) for y in p],
            [pick(row < 3, pltpu.roll(y, 5, 0)) for y in p],
        ):
            halves += [three[m] for m in (0, 1, 2, 0, 1, 0)]
        for source, r in ((q, 0), (p, 0), (p, 1), (p, 2)):
            halves += [zero] + [pick(row == r, -y) for y in source]
        for r in (1, 2, 3):
            halves += [jnp.where(row == r, 1.0, 0.0)] + [pick(row == r, y) for y in q]
        right[pl.ds(pl.multiple_of(at * RIGHT_ROWS, 16), RIGHT_ROWS), :] = jnp.concatenate(halves, axis=0).astype(BF16)

    def step(n, carry):
        for u in range(PREP):
            one_block(n * PREP + u)
        return carry

    lax.fori_loop(0, blocks // PREP, step, 0)


def write_template(fixed):
    row = lax.broadcasted_iota(jnp.int32, (DEPTH, 128), 0)
    picks = [[], [48, 56, 64], []]
    picks += [[k, 24 + k, 40 + k] for k in range(3)]
    picks += [[48 + n, 56 + n, 64 + n] for n in (1, 2, 3)]
    picks += [[3 + k, 27 + k, 43 + k] for k in range(3)]
    picks += [[52, 60, 68]]
    for n, chosen in enumerate(picks):
        hit = jnp.zeros((DEPTH, 128), jnp.bool_)
        for r in chosen:
            hit = hit | (row == r)
        fixed[:, 128 * n : 128 * (n + 1)] = jnp.where(hit, 1.0, 0.0).astype(BF16)


def products(left, right, fixed, prod, pair):
    ia, ib = pair
    a = left[pl.ds(pl.multiple_of(ia * 128, 128), 128), 0:DEPTH]
    mine = right[pl.ds(pl.multiple_of(ib * RIGHT_ROWS, 16), RIGHT_ROWS), :]

    def column(n):
        places = PLACES[n]
        rows = []
        for k in range(GROUPS // 2):
            if k in places:
                rows.append(mine[16 * places[k] : 16 * places[k] + 16, :])
            else:
                rows.append(fixed[16 * k : 16 * k + 16, 128 * n : 128 * (n + 1)])
        return jnp.concatenate(rows, axis=0)

    for low in range(0, OUTS, 2):
        high = min(low + 2, OUTS)
        b = jnp.concatenate([column(n) for n in range(low, high)], axis=1)
        prod[:, 128 * low : 128 * high] = lax.dot_general(
            a, b, (((1,), (0,)), ((), ())), preferred_element_type=F32
        )


def pair_sums(feat, prod, part, ib):
    ux2, uy2, uz2, len2 = (jnp.broadcast_to(feat[pl.ds(ib * 8 + q, 1), :], (8, 128)) for q in range(4))
    sums = None
    for g in range(16):
        rows = slice(8 * g, 8 * g + 8)
        w, c, f, ox, oy, oz, reach, compliance, curvature, ux1, uy1, uz1, len1 = (
            prod[rows, 128 * n : 128 * (n + 1)] for n in range(OUTS)
        )
        inverse = pl.reciprocal(jnp.maximum(1.0 - w * w, PARALLEL_FLOOR))
        s = jnp.minimum(jnp.maximum((w * f - c) * inverse, 0.0), len1)
        t = jnp.minimum(jnp.maximum(w * s + f, 0.0), len2)
        s = jnp.minimum(jnp.maximum(w * t - c, 0.0), len1)
        gx = ox + s * ux1 - t * ux2
        gy = oy + s * uy1 - t * uy2
        gz = oz + s * uz1 - t * uz2
        square = jnp.maximum(gx * gx + gy * gy + gz * gz, DIST_FLOOR)
        near = lax.rsqrt(square)
        depth = jnp.maximum(reach - square * near, TINY)
        root = lax.rsqrt(depth * curvature)
        scale = (depth * root) * (depth * near) * pl.reciprocal(compliance)
        force = [scale * gx, scale * gy, scale * gz]
        on_a = force + [s * x for x in force]
        on_b = force + [t * x for x in force]
        for q in range(6):
            part[rows, q : q + 1] = jnp.sum(on_a[q], axis=1, keepdims=True)
        sums = on_b if sums is None else [x + y for x, y in zip(sums, on_b)]
    return jnp.concatenate([jnp.sum(x, axis=0, keepdims=True) for x in sums] + [jnp.zeros((2, 128), F32)], axis=0)


def block_arrays(blocks):
    return [
        pltpu.VMEM((blocks * 8, 128), F32),
        pltpu.VMEM((blocks * 128, 128), BF16),
        pltpu.VMEM((blocks * RIGHT_ROWS, 128), BF16),
    ]


def tile_scratch():
    return [
        pltpu.VMEM((DEPTH, OUTS * 128), BF16),
        *[pltpu.VMEM((128, OUTS * 128), F32)] * (2 * BATCH),
        *[pltpu.VMEM((128, 128), F32)] * (2 * BATCH),
        *[pltpu.VMEM((8, 128), F32)] * (2 * BATCH),
    ]


def run_tiles(blocks, scratch, acc, code_at, count):
    feat, left, right = blocks
    fixed = scratch[0]
    prods, sums_a, sums_b = (scratch[1 + 2 * BATCH * k : 1 + 2 * BATCH * (k + 1)] for k in range(3))
    write_template(fixed)
    for ref in (*sums_a, *sums_b):
        ref[...] = jnp.zeros_like(ref)

    def ids(n):
        code = code_at(n)
        return lax.shift_right_logical(code, SHIFT), code & ((1 << SHIFT) - 1)

    def collect(first, side):
        for u in range(BATCH):
            ia, ib = ids(jnp.maximum(first + u, 0))
            slot = side * BATCH + u
            acc[pl.ds(pl.multiple_of(ia * 8, 8), 8), :] += jnp.transpose(sums_a[slot][...])[0:8, :]
            acc[pl.ds(pl.multiple_of(ib * 8, 8), 8), :] -= sums_b[slot][...]

    def prepare(first, side):
        for u in range(BATCH):
            products(left, right, fixed, prods[side * BATCH + u], ids(first + u))

    def batch(first, side):
        collect(first - BATCH, 1 - side)
        prepare(first + BATCH, 1 - side)
        for u in range(BATCH):
            slot = side * BATCH + u
            sums_b[slot][...] = pair_sums(feat, prods[slot], sums_a[slot], ids(first + u)[1])

    prepare(0, 0)

    def step(n, carry):
        first = 2 * BATCH * n
        batch(first, 0)

        @pl.when(first + BATCH < count)
        def _():
            batch(first + BATCH, 1)

        return carry

    lax.fori_loop(0, (count + 2 * BATCH - 1) // (2 * BATCH), step, 0)
    batches = (count + BATCH - 1) // BATCH

    @pl.when((batches & 1) == 1)
    def _():
        collect((batches - 1) * BATCH, 0)

    @pl.when((batches > 0) & ((batches & 1) == 0))
    def _():
        collect((batches - 1) * BATCH, 1)


def gather_kernel(ship_ref, seg_ref, out_ref):
    slots, bricks = ship_ref.shape[1:]
    for q in range(bricks):
        for k in range(slots):
            out_ref[q, 8 * k : 8 * k + 8, :] = seg_ref[pl.ds(pl.multiple_of(ship_ref[0, k, q] * 8, 8), 8), :]


def plan_kernel(leaves, ship_ref, kept_ref, count_ref, lent_ref, plan_ref, list_ref, near_ref):
    slots, bricks = ship_ref.shape[1:]
    peers = lent_ref.shape[1]
    brick = lax.axis_index("brick")
    region = lax.axis_index("region")
    mine = leaves + brick * slots

    def local_id(e):
        ghost = e - mine
        is_mine = (ghost >= 0) & (ghost < slots)
        return jnp.where(is_mine, ship_ref[0, jnp.where(is_mine, ghost, 0), brick], e)

    def file_tiles(pair_at, count, carry):
        def step(n, carry):
            near, far = carry
            for u in range(FILED):
                k = n * FILED + u
                a, b = pair_at(k)
                a, b = local_id(a), local_id(b)
                code = lax.shift_left(a, SHIFT) | b
                live = (k < count).astype(jnp.int32)
                is_near = ((a < leaves) & (b < leaves)).astype(jnp.int32) * live
                near_ref[near] = code
                list_ref[HEAD + far] = code
                near, far = near + is_near, far + live - is_near
            return near, far

        return lax.fori_loop(0, (count + FILED - 1) // FILED, step, carry)

    carry = file_tiles(lambda k: (kept_ref[0, 0, k], kept_ref[0, 1, k]), count_ref[0], (0, 0))
    for j in range(peers):
        carry = file_tiles(lambda k: (lent_ref[0, j, 0, k], lent_ref[0, j, 1, k]), plan_ref[0, region, j], carry)
    near, far = carry

    def append(k, carry):
        list_ref[HEAD + far + k] = near_ref[k]
        return carry

    lax.fori_loop(0, near, append, 0)
    list_ref[0] = near + far
    list_ref[1] = near


def tile_kernel(
    list_ref, other_in, seg_ref, ghost_ref, guest_ref, own_ref, back_ref, loan_ref, other_ref, sem, acc, feat, left, right, *scratch
):
    own_rows = seg_ref.shape[0]
    leaves = own_rows // 8
    ghosts = ghost_ref.shape[0] // 8
    ext = leaves + ghosts
    bricks = back_ref.shape[0]
    slots = ghosts // bricks
    last = list_ref.shape[0] - 1
    fetch = pltpu.make_async_copy(other_in, other_ref, sem)
    fetch.start()
    acc[...] = jnp.zeros_like(acc)
    write_blocks(seg_ref, feat, left, right, 0, leaves)
    write_blocks(ghost_ref, feat, left, right, leaves, ghosts)
    fetch.wait()
    excess = list_ref[0] - other_ref[0]
    give = jnp.minimum(lax.shift_right_arithmetic(jnp.maximum(excess - LOAN_COST, 0), 1), list_ref[1])
    take = jnp.minimum(lax.shift_right_arithmetic(jnp.maximum(-excess - LOAN_COST, 0), 1), other_ref[1])
    keep = list_ref[0] - give
    borrowed = HEAD + other_ref[0] - take - keep
    guest_code = (ext << SHIFT) | ext
    dummy_code = ((ext + leaves) << SHIFT) | (ext + leaves)

    def code_at(n):
        kept = list_ref[jnp.minimum(HEAD + n, last)]
        lent = other_ref[jnp.clip(borrowed + n, 0, last)] + guest_code
        return jnp.where(n < keep, kept, jnp.where(n < keep + take, lent, dummy_code))

    @pl.when(take > 0)
    def _():
        write_blocks(guest_ref, feat, left, right, ext, leaves)

    run_tiles((feat, left, right), scratch, acc, code_at, keep + take)
    own_ref[...] = acc[0:own_rows, :]
    loan_ref[...] = acc[8 * ext : 8 * ext + own_rows, :]
    for q in range(bricks):
        for k in range(slots):
            row = own_rows + 8 * (q * slots + k)
            back_ref[q, 6 * k : 6 * k + 6, :] = acc[row : row + 6, :]


def stride_rows(first, count, row, stride):
    return pl.ds(first * stride + row, count, stride=stride)


def finish_kernel(ship_ref, seg_ref, own_ref, loan_ref, back_ref, out_ref, *accs):
    leaves = seg_ref.shape[0] // 8
    slots, bricks = ship_ref.shape[1:]
    for k, acc in enumerate(accs):
        acc[...] = own_ref[...] if k == 0 else loan_ref[...] if k == 1 else jnp.zeros_like(acc)
    for q in range(bricks):
        for k in range(slots):
            row = pl.multiple_of(ship_ref[0, k, q] * 8, 8)
            accs[k % len(accs)][pl.ds(row, 6), :] += back_ref[q, 6 * k : 6 * k + 6, :]

    def summed(c, q):
        rows = stride_rows(c, 8, q, 8)
        first, second, third, fourth = (acc[rows, :] for acc in accs)
        return (first + second) + (third + fourth)

    for c in range(0, leaves, 8):
        d = [seg_ref[stride_rows(c, 8, 3 + q, 8), :] for q in range(3)]
        force = [summed(c, q) for q in range(3)]
        lever = [summed(c, 3 + q) for q in range(3)]
        squared = d[0] * d[0] + d[1] * d[1] + d[2] * d[2]
        inverse = lax.rsqrt(squared)
        half = 0.5 * squared * inverse
        unit = [x * inverse for x in d]
        m = [x - half * y for x, y in zip(lever, force)]
        for q in range(3):
            i, j = (q + 1) % 3, (q + 2) % 3
            out_ref[q, c : c + 8, :] = force[q]
            out_ref[3 + q, c : c + 8, :] = unit[i] * m[j] - unit[j] * m[i]


def body(segments, ship_list, kept_tiles, kept_count, lent_tiles, lent_count):
    leaves = segments.shape[0]
    bricks, slots = ship_list.shape[1:]
    keep = kept_tiles.shape[1]
    peers, lend = lent_tiles.shape[1:3]
    ghosts = bricks * slots
    ext = leaves + ghosts
    cap = -(-(HEAD + keep + peers * lend + 1) // 128) * 128
    ship = jnp.transpose(ship_list, (0, 2, 1))
    kept = jnp.transpose(kept_tiles, (0, 2, 1))
    lent = jnp.transpose(lent_tiles, (0, 1, 3, 2))
    flat = segments.reshape(leaves * 8, 128)
    smem = pl.BlockSpec(memory_space=pltpu.SMEM)
    vmem = pl.BlockSpec(memory_space=pltpu.VMEM)
    tile_list = jax.ShapeDtypeStruct((cap,), jnp.int32)
    own_sums = jax.ShapeDtypeStruct((leaves * 8, 128), F32)

    def on_chip(x):
        return pltpu.with_memory_space_constraint(x, pltpu.VMEM)

    outgoing = pl.pallas_call(
        gather_kernel,
        out_shape=jax.ShapeDtypeStruct((bricks, slots * 8, 128), F32),
        in_specs=[smem, vmem],
        out_specs=vmem,
        name="ship_gather",
    )(ship, flat)
    incoming = lax.all_to_all(outgoing, "brick", split_axis=0, concat_axis=0, tiled=True)
    partner = [(r, r ^ 1) for r in range(lax.axis_size("region"))]
    guests = lax.ppermute(flat, "region", partner)
    tiles = pl.pallas_call(
        functools.partial(plan_kernel, leaves),
        out_shape=tile_list,
        in_specs=[smem] * 5,
        out_specs=smem,
        scratch_shapes=[pltpu.SMEM((cap,), jnp.int32)],
        name="plan_tiles",
    )(ship, kept, kept_count, lent, lent_count)
    other_tiles = lax.ppermute(tiles, "region", partner)
    own, back, loan = pl.pallas_call(
        tile_kernel,
        out_shape=[
            pltpu.VMEM(own_sums.shape, F32),
            jax.ShapeDtypeStruct((bricks, slots * 6, 128), F32),
            pltpu.VMEM(own_sums.shape, F32),
        ],
        in_specs=[smem, vmem, vmem, vmem, vmem],
        out_specs=[vmem, vmem, vmem],
        scratch_shapes=[
            pltpu.SMEM((cap,), jnp.int32),
            pltpu.SemaphoreType.DMA(()),
            pltpu.VMEM(((ext + leaves + 1) * 8, 128), F32),
            *block_arrays(ext + leaves + 1),
            *tile_scratch(),
        ],
        name="all_tiles",
    )(tiles, on_chip(other_tiles), on_chip(flat), on_chip(incoming.reshape(ghosts * 8, 128)), on_chip(guests))
    repaid = lax.ppermute(loan, "region", partner)
    returned = lax.all_to_all(back, "brick", split_axis=0, concat_axis=0, tiled=True)
    loads = pl.pallas_call(
        finish_kernel,
        out_shape=jax.ShapeDtypeStruct((6, leaves, 128), F32),
        in_specs=[smem, vmem, vmem, vmem, vmem],
        out_specs=vmem,
        scratch_shapes=[pltpu.VMEM((leaves * 8, 128), F32)] * 4,
        name="finish",
    )(ship, on_chip(flat), on_chip(own), on_chip(repaid), on_chip(returned))
    return jnp.transpose(loads, (1, 0, 2))


def solution(mesh):
    placed = (
        P(("brick", "region"), None, None),
        P(("brick", "region"), None, None),
        P(("brick", "region"), None, None),
        P(("brick", "region")),
        P(("brick", "region"), None, None, None),
        P("brick", None, None),
    )
    return jax.shard_map(
        body,
        mesh=mesh,
        in_specs=placed,
        out_specs=P(("brick", "region"), None, None),
        check_vma=False,
    )
```

```python
import functools

import jax
import jax.numpy as jnp
from jax import lax
from jax.experimental import pallas as pl
from jax.experimental.pallas import tpu as pltpu
from jax.sharding import PartitionSpec as P

DIST_FLOOR = 0.0025
PARALLEL_FLOOR = 0.05
TINY = 1e-20
STAND_IN = 1e-30
SHIFT = 10
F32 = jnp.float32
BF16 = jnp.bfloat16

GROUPS = 12
DEPTH = 8 * GROUPS
RIGHT_ROWS = 8 * (3 * 6 + 7 * 4)
OUTS = 13
PLACES = [{0: 3 * n, 1: 3 * n + 1, 2: 3 * n + 2} for n in range(3)] + [{}, {}, {}, {}, {}, {}]
for _n in range(7):
    PLACES[2 + _n].update({4: 9 + 2 * _n, 5: 10 + 2 * _n})
PLACES += [{}] * 4
HEAD = 8
BATCH = 4
PREP = 16


def parts(x):
    first = x.astype(BF16).astype(F32)
    rest = x - first
    second = rest.astype(BF16).astype(F32)
    return first, second, rest - second


def write_blocks(src, feat, left, right, first, blocks):
    row = lax.broadcasted_iota(jnp.int32, (8, 128), 0)
    is_dir = (row >= 3) & (row < 6)
    one = jnp.ones((8, 128), F32)
    zero = jnp.zeros((8, 128), F32)

    def pick(mask, x):
        return jnp.where(mask, x, 0.0)

    def total(x):
        return jnp.broadcast_to(jnp.sum(x, axis=0, keepdims=True), (8, 128))

    def spread(x, r):
        return jnp.broadcast_to(x[r : r + 1, :], (8, 128))

    def one_block(n):
        x = src[pl.ds(pl.multiple_of(n * 8, 8), 8), :]
        squared = total(pick(is_dir, x * x))
        inverse = lax.rsqrt(squared)
        pose = jnp.where(is_dir, x * inverse, pick(row < 3, x))
        along = total(pick(is_dir, pose * pltpu.roll(pose, 3, 0)))
        length = squared * inverse
        flipped = 1.0 / jnp.where(x == 0.0, STAND_IN, x)
        single = pick(row == 4, length)
        for r, value in ((3, spread(flipped, 6)), (2, 0.75 * spread(flipped, 7)), (1, spread(x, 6)), (0, along)):
            single = jnp.where(row == r, value, single)
        at = first + n
        feat[pl.ds(pl.multiple_of(at * 8, 8), 8), :] = jnp.where(row == 3, length, pltpu.roll(pose, 5, 0))
        p, q = parts(pose), parts(single)
        stack = jnp.concatenate([p[0], p[0], p[0], p[1], p[1], p[2], *q, one, one, one], axis=0)
        left[pl.ds(pl.multiple_of(at * 128, 128), 128), 0:DEPTH] = jnp.transpose(stack.astype(BF16))
        halves = []
        for three in (
            [pick(is_dir, y) for y in p],
            [pick(is_dir, -pltpu.roll(y, 3, 0)) for y in p],
            [pick(row < 3, pltpu.roll(y, 5, 0)) for y in p],
        ):
            halves += [three[m] for m in (0, 1, 2, 0, 1, 0)]
        for source, r in ((q, 0), (p, 0), (p, 1), (p, 2)):
            halves += [zero] + [pick(row == r, -y) for y in source]
        for r in (1, 2, 3):
            halves += [jnp.where(row == r, 1.0, 0.0)] + [pick(row == r, y) for y in q]
        right[pl.ds(pl.multiple_of(at * RIGHT_ROWS, 16), RIGHT_ROWS), :] = jnp.concatenate(halves, axis=0).astype(BF16)

    def step(n, carry):
        for u in range(PREP):
            one_block(n * PREP + u)
        return carry

    lax.fori_loop(0, blocks // PREP, step, 0)


def write_template(fixed):
    row = lax.broadcasted_iota(jnp.int32, (DEPTH, 128), 0)
    picks = [[], [48, 56, 64], []]
    picks += [[k, 24 + k, 40 + k] for k in range(3)]
    picks += [[48 + n, 56 + n, 64 + n] for n in (1, 2, 3)]
    picks += [[3 + k, 27 + k, 43 + k] for k in range(3)]
    picks += [[52, 60, 68]]
    for n, chosen in enumerate(picks):
        hit = jnp.zeros((DEPTH, 128), jnp.bool_)
        for r in chosen:
            hit = hit | (row == r)
        fixed[:, 128 * n : 128 * (n + 1)] = jnp.where(hit, 1.0, 0.0).astype(BF16)


def products(left, right, fixed, prod, pair):
    ia, ib = pair
    a = left[pl.ds(pl.multiple_of(ia * 128, 128), 128), 0:DEPTH]
    mine = right[pl.ds(pl.multiple_of(ib * RIGHT_ROWS, 16), RIGHT_ROWS), :]

    def column(n):
        places = PLACES[n]
        rows = []
        for k in range(GROUPS // 2):
            if k in places:
                rows.append(mine[16 * places[k] : 16 * places[k] + 16, :])
            else:
                rows.append(fixed[16 * k : 16 * k + 16, 128 * n : 128 * (n + 1)])
        return jnp.concatenate(rows, axis=0)

    for low in range(0, OUTS, 2):
        high = min(low + 2, OUTS)
        b = jnp.concatenate([column(n) for n in range(low, high)], axis=1)
        prod[:, 128 * low : 128 * high] = lax.dot_general(
            a, b, (((1,), (0,)), ((), ())), preferred_element_type=F32
        )


def pair_sums(feat, prod, part, ib):
    ux2, uy2, uz2, len2 = (jnp.broadcast_to(feat[pl.ds(ib * 8 + q, 1), :], (8, 128)) for q in range(4))
    sums = None
    for g in range(16):
        rows = slice(8 * g, 8 * g + 8)
        w, c, f, ox, oy, oz, reach, compliance, curvature, ux1, uy1, uz1, len1 = (
            prod[rows, 128 * n : 128 * (n + 1)] for n in range(OUTS)
        )
        inverse = pl.reciprocal(jnp.maximum(1.0 - w * w, PARALLEL_FLOOR))
        s = jnp.minimum(jnp.maximum((w * f - c) * inverse, 0.0), len1)
        t = jnp.minimum(jnp.maximum(w * s + f, 0.0), len2)
        s = jnp.minimum(jnp.maximum(w * t - c, 0.0), len1)
        gx = ox + s * ux1 - t * ux2
        gy = oy + s * uy1 - t * uy2
        gz = oz + s * uz1 - t * uz2
        square = jnp.maximum(gx * gx + gy * gy + gz * gz, DIST_FLOOR)
        near = lax.rsqrt(square)
        depth = jnp.maximum(reach - square * near, TINY)
        root = lax.rsqrt(depth * curvature)
        scale = (depth * root) * (depth * near) * pl.reciprocal(compliance)
        force = [scale * gx, scale * gy, scale * gz]
        on_a = force + [s * x for x in force]
        on_b = force + [t * x for x in force]
        for q in range(6):
            part[rows, q : q + 1] = jnp.sum(on_a[q], axis=1, keepdims=True)
        sums = on_b if sums is None else [x + y for x, y in zip(sums, on_b)]
    return jnp.concatenate([jnp.sum(x, axis=0, keepdims=True) for x in sums] + [jnp.zeros((2, 128), F32)], axis=0)


def block_arrays(blocks):
    return [
        pltpu.VMEM((blocks * 8, 128), F32),
        pltpu.VMEM((blocks * 128, 128), BF16),
        pltpu.VMEM((blocks * RIGHT_ROWS, 128), BF16),
    ]


def tile_scratch():
    return [
        pltpu.VMEM((DEPTH, OUTS * 128), BF16),
        *[pltpu.VMEM((128, OUTS * 128), F32)] * (2 * BATCH),
        *[pltpu.VMEM((128, 128), F32)] * (2 * BATCH),
        *[pltpu.VMEM((8, 128), F32)] * (2 * BATCH),
    ]


def run_tiles(blocks, scratch, acc, code_at, count):
    feat, left, right = blocks
    fixed = scratch[0]
    prods, sums_a, sums_b = (scratch[1 + 2 * BATCH * k : 1 + 2 * BATCH * (k + 1)] for k in range(3))
    write_template(fixed)
    for ref in (*sums_a, *sums_b):
        ref[...] = jnp.zeros_like(ref)

    def ids(n):
        code = code_at(n)
        return lax.shift_right_logical(code, SHIFT), code & ((1 << SHIFT) - 1)

    def collect(first, side):
        for u in range(BATCH):
            ia, ib = ids(jnp.maximum(first + u, 0))
            slot = side * BATCH + u
            acc[pl.ds(pl.multiple_of(ia * 8, 8), 8), :] += jnp.transpose(sums_a[slot][...])[0:8, :]
            acc[pl.ds(pl.multiple_of(ib * 8, 8), 8), :] -= sums_b[slot][...]

    def prepare(first, side):
        for u in range(BATCH):
            products(left, right, fixed, prods[side * BATCH + u], ids(first + u))

    def batch(first, side):
        collect(first - BATCH, 1 - side)
        prepare(first + BATCH, 1 - side)
        for u in range(BATCH):
            slot = side * BATCH + u
            sums_b[slot][...] = pair_sums(feat, prods[slot], sums_a[slot], ids(first + u)[1])

    prepare(0, 0)

    def step(n, carry):
        first = 2 * BATCH * n
        batch(first, 0)

        @pl.when(first + BATCH < count)
        def _():
            batch(first + BATCH, 1)

        return carry

    lax.fori_loop(0, (count + 2 * BATCH - 1) // (2 * BATCH), step, 0)
    batches = (count + BATCH - 1) // BATCH

    @pl.when((batches & 1) == 1)
    def _():
        collect((batches - 1) * BATCH, 0)

    @pl.when((batches > 0) & ((batches & 1) == 0))
    def _():
        collect((batches - 1) * BATCH, 1)


def gather_kernel(ship_ref, seg_ref, out_ref):
    slots, bricks = ship_ref.shape[1:]
    for q in range(bricks):
        for k in range(slots):
            out_ref[q, 8 * k : 8 * k + 8, :] = seg_ref[pl.ds(pl.multiple_of(ship_ref[0, k, q] * 8, 8), 8), :]


def plan_kernel(leaves, ship_ref, kept_ref, count_ref, lent_ref, plan_ref, list_ref, near_ref):
    slots, bricks = ship_ref.shape[1:]
    peers = lent_ref.shape[1]
    brick = lax.axis_index("brick")
    region = lax.axis_index("region")
    mine = leaves + brick * slots

    def local_id(e):
        ghost = e - mine
        is_mine = (ghost >= 0) & (ghost < slots)
        return jnp.where(is_mine, ship_ref[0, jnp.where(is_mine, ghost, 0), brick], e)

    def file_tile(a, b, carry):
        near, far = carry
        a, b = local_id(a), local_id(b)
        code = lax.shift_left(a, SHIFT) | b
        is_near = (a < leaves) & (b < leaves)
        near_ref[near] = code
        list_ref[HEAD + far] = code
        step = is_near.astype(jnp.int32)
        return near + step, far + 1 - step

    carry = lax.fori_loop(
        0, count_ref[0], lambda k, c: file_tile(kept_ref[0, 0, k], kept_ref[0, 1, k], c), (0, 0)
    )
    for j in range(peers):
        carry = lax.fori_loop(
            0, plan_ref[0, region, j], lambda k, c: file_tile(lent_ref[0, j, 0, k], lent_ref[0, j, 1, k], c), carry
        )
    near, far = carry

    def append(k, carry):
        list_ref[HEAD + far + k] = near_ref[k]
        return carry

    lax.fori_loop(0, near, append, 0)
    list_ref[0] = near + far
    list_ref[1] = near


def tile_kernel(
    list_ref, other_in, seg_ref, ghost_ref, guest_ref, own_ref, back_ref, loan_ref, other_ref, sem, acc, feat, left, right, *scratch
):
    own_rows = seg_ref.shape[0]
    leaves = own_rows // 8
    ghosts = ghost_ref.shape[0] // 8
    ext = leaves + ghosts
    bricks = back_ref.shape[0]
    slots = ghosts // bricks
    last = list_ref.shape[0] - 1
    fetch = pltpu.make_async_copy(other_in, other_ref, sem)
    fetch.start()
    acc[...] = jnp.zeros_like(acc)
    write_blocks(seg_ref, feat, left, right, 0, leaves)
    write_blocks(ghost_ref, feat, left, right, leaves, ghosts)
    fetch.wait()
    excess = list_ref[0] - other_ref[0]
    give = jnp.minimum(lax.shift_right_arithmetic(jnp.maximum(excess, 0), 1), list_ref[1])
    take = jnp.minimum(lax.shift_right_arithmetic(jnp.maximum(-excess, 0), 1), other_ref[1])
    keep = list_ref[0] - give
    borrowed = HEAD + other_ref[0] - take - keep
    guest_code = (ext << SHIFT) | ext
    dummy_code = ((ext + leaves) << SHIFT) | (ext + leaves)

    def code_at(n):
        kept = list_ref[jnp.minimum(HEAD + n, last)]
        lent = other_ref[jnp.clip(borrowed + n, 0, last)] + guest_code
        return jnp.where(n < keep, kept, jnp.where(n < keep + take, lent, dummy_code))

    @pl.when(take > 0)
    def _():
        write_blocks(guest_ref, feat, left, right, ext, leaves)

    run_tiles((feat, left, right), scratch, acc, code_at, keep + take)
    own_ref[...] = acc[0:own_rows, :]
    loan_ref[...] = acc[8 * ext : 8 * ext + own_rows, :]
    for q in range(bricks):
        for k in range(slots):
            row = own_rows + 8 * (q * slots + k)
            back_ref[q, 6 * k : 6 * k + 6, :] = acc[row : row + 6, :]


def stride_rows(first, count, row, stride):
    return pl.ds(first * stride + row, count, stride=stride)


def finish_kernel(ship_ref, seg_ref, own_ref, loan_ref, back_ref, out_ref, acc):
    leaves = seg_ref.shape[0] // 8
    slots, bricks = ship_ref.shape[1:]
    acc[...] = own_ref[...] + loan_ref[...]
    for q in range(bricks):
        for k in range(slots):
            row = pl.multiple_of(ship_ref[0, k, q] * 8, 8)
            acc[pl.ds(row, 6), :] += back_ref[q, 6 * k : 6 * k + 6, :]
    for c in range(0, leaves, 8):
        d = [seg_ref[stride_rows(c, 8, 3 + q, 8), :] for q in range(3)]
        force = [acc[stride_rows(c, 8, q, 8), :] for q in range(3)]
        lever = [acc[stride_rows(c, 8, 3 + q, 8), :] for q in range(3)]
        squared = d[0] * d[0] + d[1] * d[1] + d[2] * d[2]
        inverse = lax.rsqrt(squared)
        half = 0.5 * squared * inverse
        unit = [x * inverse for x in d]
        m = [x - half * y for x, y in zip(lever, force)]
        for q in range(3):
            i, j = (q + 1) % 3, (q + 2) % 3
            out_ref[q, c : c + 8, :] = force[q]
            out_ref[3 + q, c : c + 8, :] = unit[i] * m[j] - unit[j] * m[i]


def body(segments, ship_list, kept_tiles, kept_count, lent_tiles, lent_count):
    leaves = segments.shape[0]
    bricks, slots = ship_list.shape[1:]
    keep = kept_tiles.shape[1]
    peers, lend = lent_tiles.shape[1:3]
    ghosts = bricks * slots
    ext = leaves + ghosts
    cap = -(-(HEAD + keep + peers * lend + 1) // 128) * 128
    ship = jnp.transpose(ship_list, (0, 2, 1))
    kept = jnp.transpose(kept_tiles, (0, 2, 1))
    lent = jnp.transpose(lent_tiles, (0, 1, 3, 2))
    flat = segments.reshape(leaves * 8, 128)
    smem = pl.BlockSpec(memory_space=pltpu.SMEM)
    vmem = pl.BlockSpec(memory_space=pltpu.VMEM)
    tile_list = jax.ShapeDtypeStruct((cap,), jnp.int32)
    own_sums = jax.ShapeDtypeStruct((leaves * 8, 128), F32)

    def on_chip(x):
        return pltpu.with_memory_space_constraint(x, pltpu.VMEM)

    outgoing = pl.pallas_call(
        gather_kernel,
        out_shape=jax.ShapeDtypeStruct((bricks, slots * 8, 128), F32),
        in_specs=[smem, vmem],
        out_specs=vmem,
        name="ship_gather",
    )(ship, flat)
    incoming = lax.all_to_all(outgoing, "brick", split_axis=0, concat_axis=0, tiled=True)
    partner = [(r, r ^ 1) for r in range(lax.axis_size("region"))]
    guests = lax.ppermute(flat, "region", partner)
    tiles = pl.pallas_call(
        functools.partial(plan_kernel, leaves),
        out_shape=tile_list,
        in_specs=[smem] * 5,
        out_specs=smem,
        scratch_shapes=[pltpu.SMEM((cap,), jnp.int32)],
        name="plan_tiles",
    )(ship, kept, kept_count, lent, lent_count)
    other_tiles = lax.ppermute(tiles, "region", partner)
    own, back, loan = pl.pallas_call(
        tile_kernel,
        out_shape=[
            pltpu.VMEM(own_sums.shape, F32),
            jax.ShapeDtypeStruct((bricks, slots * 6, 128), F32),
            pltpu.VMEM(own_sums.shape, F32),
        ],
        in_specs=[smem, vmem, vmem, vmem, vmem],
        out_specs=[vmem, vmem, vmem],
        scratch_shapes=[
            pltpu.SMEM((cap,), jnp.int32),
            pltpu.SemaphoreType.DMA(()),
            pltpu.VMEM(((ext + leaves + 1) * 8, 128), F32),
            *block_arrays(ext + leaves + 1),
            *tile_scratch(),
        ],
        name="all_tiles",
    )(tiles, on_chip(other_tiles), on_chip(flat), on_chip(incoming.reshape(ghosts * 8, 128)), on_chip(guests))
    repaid = lax.ppermute(loan, "region", partner)
    returned = lax.all_to_all(back, "brick", split_axis=0, concat_axis=0, tiled=True)
    loads = pl.pallas_call(
        finish_kernel,
        out_shape=jax.ShapeDtypeStruct((6, leaves, 128), F32),
        in_specs=[smem, vmem, vmem, vmem, vmem],
        out_specs=vmem,
        scratch_shapes=[pltpu.VMEM((leaves * 8, 128), F32)],
        name="finish",
    )(ship, on_chip(flat), on_chip(own), on_chip(repaid), on_chip(returned))
    return jnp.transpose(loads, (1, 0, 2))


def solution(mesh):
    placed = (
        P(("brick", "region"), None, None),
        P(("brick", "region"), None, None),
        P(("brick", "region"), None, None),
        P(("brick", "region")),
        P(("brick", "region"), None, None, None),
        P("brick", None, None),
    )
    return jax.shard_map(
        body,
        mesh=mesh,
        in_specs=placed,
        out_specs=P(("brick", "region"), None, None),
        check_vma=False,
    )
```
